32 devices in a mesh: fsdp: 8 (over y, x, core), seq: 4 (over z).
Axes of the slice: x: 2, y: 2, z: 4, core: 2. Of those that a mesh axis runs over, the one named last changes fastest.
Arguments:
- tokens: bfloat16 [8, 2, 2048, 768], P('fsdp', None, 'seq'), may hold values from -6 to 6
- doc_lengths: int32 [8, 2, 8], P('fsdp'), may hold values from 1 to 1024, 2048 in all within a row
- qkv_weight: bfloat16 [768, 2304], P('fsdp'), may hold values from -0.21875 to 0.21875
- q_bias: bfloat16 [768], P('fsdp'), may hold values from -1.5 to 1.5
- v_bias: bfloat16 [768], P('fsdp'), may hold values from -0.25 to 0.25
- out_weight: bfloat16 [768, 768], P('fsdp'), may hold values from -1.25 to 1.25
- out_bias: bfloat16 [768], P('fsdp'), may hold values from -1.5 to 1.5
- norm1_gain: bfloat16 [768], P('fsdp'), may hold values from 0.25 to 1.75
- norm1_bias: bfloat16 [768], P('fsdp'), may hold values from -1.5 to 1.5
- ff_in_weight: bfloat16 [768, 3072], P('fsdp'), may hold values from -0.21875 to 0.21875
- ff_in_bias: bfloat16 [3072], P('fsdp'), may hold values from -2.5 to 2.5
- ff_out_weight: bfloat16 [3072, 768], P('fsdp'), may hold values from -0.109375 to 0.109375
- ff_out_bias: bfloat16 [768], P('fsdp'), may hold values from -1.5 to 1.5
- norm2_gain: bfloat16 [768], P('fsdp'), may hold values from 0.25 to 1.75
- norm2_bias: bfloat16 [768], P('fsdp'), may hold values from -1.5 to 1.5
- out_cotangent: bfloat16 [8, 2, 2048, 768], P('fsdp', None, 'seq'), may hold values from -6 to 6
Outputs:
- output: bfloat16 [8, 2, 2048, 768], P('fsdp', None, 'seq')
- input_grad: float32 [8, 2, 2048, 768], P('fsdp', None, 'seq')
- qkv_weight_grad: float32 [768, 2304], P('fsdp')
- q_bias_grad: float32 [768], P('fsdp')
- v_bias_grad: float32 [768], P('fsdp')
- out_weight_grad: float32 [768, 768], P('fsdp')
- out_bias_grad: float32 [768], P('fsdp')
- norm1_gain_grad: float32 [768], P('fsdp')
- norm1_bias_grad: float32 [768], P('fsdp')
- ff_in_weight_grad: float32 [768, 3072], P('fsdp')
- ff_in_bias_grad: float32 [3072], P('fsdp')
- ff_out_weight_grad: float32 [3072, 768], P('fsdp')
- ff_out_bias_grad: float32 [768], P('fsdp')
- norm2_gain_grad: float32 [768], P('fsdp')
- norm2_bias_grad: float32 [768], P('fsdp')
The draws below stay inside these ranges and needn't reach their ends.
Inputs may be any that keep to these rules, and one draw needn't show every extreme that they name: `doc_lengths`: the 8 lengths of a stretch sum to 2048; in every stretch the longest is exactly 1024 tokens.
All inputs are finite; a program needn't handle non-finite values.
Results may differ from the reference program's by a relative error of at most 0.017.
Values may be sent and summed in bfloat16 or wider, within the bound.
A program may use at most 192 MiB of HBM per device.

```python
import math
import jax
import jax.numpy as jnp
import numpy as np
from jax import lax

D = 768
HEADS = 12
FF = 3072
HEAD_DIM = 64
STRETCH = 2048
MICRO = 2
NDOC = 8
BLOCK = 512
GROUPS = 8


def block_levels(own_key, extent, shards, least, top_value):
    level = 1.0
    for axis_at, shards_of in shards:
        draws = jax.random.uniform(jax.random.fold_in(jax.random.fold_in(own_key, 6), axis_at), (shards_of,), jnp.float32, least / len(shards), top_value / len(shards))
        level = level * jnp.repeat(jnp.exp(draws), extent[axis_at] // shards_of).reshape((-1,) + (1,) * (len(extent) - 1 - axis_at))
    return level


def profile(count, total, bound, slope):
    portions = [(1 << 20) // math.isqrt(rank ** slope) + 1 for rank in range(2, count + 1)]
    surplus, holding = total - bound - (count - 1), [1] * (count - 1)
    while surplus > 0:
        candidates = [i for i in range(count - 1) if holding[i] < bound]
        mass, budget = sum([portions[i] for i in candidates]), surplus
        for i in candidates:
            addition = min(bound - holding[i], max(1, budget * portions[i] // mass), surplus)
            holding[i] = holding[i] + addition
            surplus = surplus - addition
    return np.array([bound] + holding)


def ragged_sizes(own_key, amount, total, limit, lean):
    if amount == 2:
        one = jax.random.randint(own_key, (), max(1, total - limit), min(limit, total - 1) + 1)
        return jnp.stack([one, total - one])
    tallies = jnp.asarray(profile(amount, total, limit, lean), jnp.int32)
    twos = (amount - 1) // 2
    source_of, sink = tallies[1:1 + 2 * twos:2], tallies[2:2 + 2 * twos:2]
    margin = jnp.minimum(source_of - 1, limit - sink)
    passed = jax.random.randint(jax.random.fold_in(own_key, 1), (twos,), 0, 1 << 20) % (margin + 1)
    tallies = tallies.at[1:1 + 2 * twos:2].set(source_of - passed).at[2:2 + 2 * twos:2].set(sink + passed)
    return tallies[jax.random.permutation(jax.random.fold_in(own_key, 2), amount)]


def bell_draw(stream_key, dims, deviation, most, cuts=(), kind=jnp.bfloat16):
    array = deviation * jax.random.normal(stream_key, dims, jnp.float32)
    if cuts:
        array = array * block_levels(stream_key, dims, cuts, -0.22, 0.18)
    return jnp.clip(array, -most, most).astype(kind)


def setup_inputs(seed: int = 0) -> dict:
    streams_of = jax.random.split(jax.random.key(seed), 17)
    tokens = bell_draw(streams_of[0], (GROUPS, MICRO, STRETCH, D), 1.0, 6.0, ((0, 8), (2, 4)))
    doc_lengths = jax.vmap(lambda own: ragged_sizes(own, NDOC, STRETCH, STRETCH // 2, 2))(jax.random.split(streams_of[1], GROUPS * MICRO)).reshape((GROUPS, MICRO, NDOC)).astype(jnp.int32)
    qkv_weight = bell_draw(streams_of[2], (D, 3 * D), D ** -0.5, 0.21875, ((0, 8),))
    q_bias = bell_draw(streams_of[3], (D,), 0.3, 1.5, ((0, 8),))
    v_bias = bell_draw(streams_of[4], (D,), 0.05, 0.25, ((0, 8),))
    out_weight = bell_draw(streams_of[5], (D, D), (D // 32) ** -0.5, 1.25, ((0, 8),))
    out_bias = bell_draw(streams_of[6], (D,), 0.3, 1.5, ((0, 8),))
    norm1_gain = jnp.clip(1.0 + 0.15 * jax.random.normal(streams_of[7], (D,), jnp.float32), 0.25, 1.75).astype(jnp.bfloat16)
    norm1_bias = bell_draw(streams_of[8], (D,), 0.3, 1.5, ((0, 8),))
    ff_in_weight = bell_draw(streams_of[9], (D, FF), D ** -0.5, 0.21875, ((0, 8),))
    ff_in_bias = bell_draw(streams_of[10], (FF,), 0.5, 2.5, ((0, 8),))
    ff_out_weight = bell_draw(streams_of[11], (FF, D), FF ** -0.5, 0.109375, ((0, 8),))
    ff_out_bias = bell_draw(streams_of[12], (D,), 0.3, 1.5, ((0, 8),))
    norm2_gain = jnp.clip(1.0 + 0.15 * jax.random.normal(streams_of[13], (D,), jnp.float32), 0.25, 1.75).astype(jnp.bfloat16)
    norm2_bias = bell_draw(streams_of[14], (D,), 0.3, 1.5, ((0, 8),))
    out_cotangent = bell_draw(streams_of[15], (GROUPS, MICRO, STRETCH, D), 1.0, 6.0, ((0, 8), (2, 4)))
    return dict(tokens=tokens, doc_lengths=doc_lengths, qkv_weight=qkv_weight, q_bias=q_bias, v_bias=v_bias, out_weight=out_weight, out_bias=out_bias, norm1_gain=norm1_gain, norm1_bias=norm1_bias, ff_in_weight=ff_in_weight, ff_in_bias=ff_in_bias, ff_out_weight=ff_out_weight, ff_out_bias=ff_out_bias, norm2_gain=norm2_gain, norm2_bias=norm2_bias, out_cotangent=out_cotangent)


@jax.custom_vjp
def low(v):
    return lax.optimization_barrier(v.astype(jnp.bfloat16)).astype(jnp.float32)

@jax.custom_vjp
def low_back(v):
    return v

def low_keep(v):
    return (low(v), None)

def low_pass(kept, grad):
    return (grad,)

def back_keep(v):
    return (v, None)

def back_low(kept, grad):
    return (low(grad),)
low.defvjp(low_keep, low_pass)
low_back.defvjp(back_keep, back_low)
EPS = 1e-05
NEG = -1e+30
HIGH = lax.Precision.HIGHEST

def norm_forward(resid, gain, shift):
    mean = lax.optimization_barrier(jnp.mean(resid, axis=-1, keepdims=True))
    centered = resid - mean
    inv = lax.rsqrt(lax.optimization_barrier(jnp.mean(centered * centered, axis=-1, keepdims=True)) + EPS)
    return centered * inv * gain + shift

def doc_ids(lengths):
    ends = jnp.cumsum(lengths).astype(jnp.int32)
    places = jnp.arange(STRETCH, dtype=jnp.int32)
    return lax.optimization_barrier(jnp.sum((places[:, None] >= ends[None, :]).astype(jnp.int32), axis=1)).astype(jnp.int32)

def attend_block(qblock, sblock, keys, values, seg):
    raw = jnp.einsum('qhd,khd->hqk', qblock, keys, precision=HIGH) * HEAD_DIM ** (-0.5)
    raw = low_back(raw)
    same = sblock[:, None] == seg[None, :]
    masked = jnp.where(same[None], raw, NEG)
    probs = low(jax.nn.softmax(masked, axis=-1))
    return jnp.einsum('hqk,khd->qhd', probs, values, precision=HIGH)
attend_saved = jax.checkpoint(attend_block)

def layer(x, seg, params):
    w_qkv, bias_q, bias_v, w_out, bias_out, gain_one, shift_one, w_in, bias_in, w_down, bias_down, gain_two, shift_two = params
    proj_bias = jnp.concatenate([bias_q, jnp.zeros((D,), jnp.float32), bias_v])
    proj = jnp.dot(x, w_qkv, precision=HIGH) + proj_bias
    queries = low_back(low(proj[:, :D])).reshape(STRETCH, HEADS, HEAD_DIM)
    keys = low_back(low(proj[:, D:2 * D])).reshape(STRETCH, HEADS, HEAD_DIM)
    values = low_back(low(proj[:, 2 * D:])).reshape(STRETCH, HEADS, HEAD_DIM)
    blocks = STRETCH // BLOCK
    context = lax.map(lambda item: attend_saved(item[0], item[1], keys, values, seg), (queries.reshape(blocks, BLOCK, HEADS, HEAD_DIM), seg.reshape(blocks, BLOCK)))
    context = low_back(low(context.reshape(STRETCH, D)))
    attn = low_back(jnp.dot(context, w_out, precision=HIGH) + bias_out)
    hidden = norm_forward(x + attn, gain_one, shift_one)
    pre = low_back(jnp.dot(low(hidden), w_in, precision=HIGH) + bias_in)
    act = low(jax.nn.gelu(pre, approximate=False))
    branch = low_back(jnp.dot(act, w_down, precision=HIGH) + bias_down)
    return norm_forward(hidden + branch, gain_two, shift_two)

def reference(tokens, doc_lengths, qkv_weight, q_bias, v_bias, out_weight, out_bias, norm1_gain, norm1_bias, ff_in_weight, ff_in_bias, ff_out_weight, ff_out_bias, norm2_gain, norm2_bias, out_cotangent):
    params = tuple((p.astype(jnp.float32) for p in (qkv_weight, q_bias, v_bias, out_weight, out_bias, norm1_gain, norm1_bias, ff_in_weight, ff_in_bias, ff_out_weight, ff_out_bias, norm2_gain, norm2_bias)))
    stretches = GROUPS * MICRO
    inputs = tokens.reshape(stretches, STRETCH, D)
    lengths = doc_lengths.reshape(stretches, NDOC)
    cotangents = out_cotangent.reshape(stretches, STRETCH, D)

    def one(totals, item):
        x, lens, cot = item
        seg = doc_ids(lens)
        result, pullback = jax.vjp(lambda xx, pp: layer(xx, seg, pp), x.astype(jnp.float32), params)
        grad_x, grad_params = pullback(cot.astype(jnp.float32))
        totals = jax.tree.map(lambda a, b: a + b, totals, grad_params)
        return (totals, (result.astype(jnp.bfloat16), grad_x))
    start = tuple((jnp.zeros(p.shape, jnp.float32) for p in params))
    totals, (results, grads_x) = lax.scan(one, start, (inputs, lengths, cotangents))
    output = results.reshape(GROUPS, MICRO, STRETCH, D)
    input_grad = grads_x.reshape(GROUPS, MICRO, STRETCH, D)
    return (output, input_grad, totals[0], totals[1], totals[2], totals[3], totals[4], totals[5], totals[6], totals[7], totals[8], totals[9], totals[10], totals[11], totals[12])
```

```python
import functools
import math

import jax
import jax.numpy as jnp
from jax import lax
from jax.experimental import pallas as pl
from jax.experimental.pallas import tpu as pltpu
from jax.sharding import Mesh
from jax.sharding import PartitionSpec as P

HEAD_DIM = 64
LANES = 128
NEG = -1e30
TILE = 256
NT = (((1,), (1,)), ((), ()))
NN = (((1,), (0,)), ((), ()))
TN = (((0,), (0,)), ((), ()))


def mm(left, right, dims):
    return lax.dot_general(left, right, dims, preferred_element_type=jnp.float32)


def key_tiles(ends_ref, first, last, tile, total):
    low = jnp.int32(0)
    high = jnp.int32(total)
    for doc in reversed(range(ends_ref.shape[0])):
        end = ends_ref[doc]
        low = jnp.maximum(low, jnp.where(end <= first, end, 0))
        high = jnp.minimum(high, jnp.where(end > last, end, total))
    return low // tile, (high + tile - 1) // tile


def lane_halves(x, fill):
    lane = lax.broadcasted_iota(jnp.int32, x.shape, 1)
    fill = jnp.full_like(x, fill)
    return jnp.where(lane < HEAD_DIM, x, fill), jnp.where(lane < HEAD_DIM, fill, x)


def piece_copies(halves, columns, place, scratch, slot, sems, run, mask, inbound):
    copies = []
    pieces = halves[0].shape[0] // run
    for half, ref in enumerate(halves):
        for part in range(pieces):
            index = half * pieces + part
            natural = pl.multiple_of(jnp.bitwise_xor(mask, index) * run, run)
            outer = ref.at[pl.ds(part * run, run), pl.ds(columns, LANES)]
            inner = scratch.at[place, pl.ds(natural, run), :]
            ends = (outer, inner) if inbound else (inner, outer)
            copies.append(pltpu.make_async_copy(ends[0], ends[1], sems.at[slot, index]))
    return copies


def forward_kernel(run, mask_ref, ends_ref, own, sib, seg_col, seg_row, ctx_own, ctx_sib, lse_ref, qkv, out, acc, top, sems, out_sems):
    total = qkv.shape[1]
    pairs = out.shape[0]
    width = pairs * LANES
    mask = mask_ref[0]

    def loads(pair):
        copies = []
        for kind in range(3):
            copies += piece_copies(
                (own, sib), kind * width + pair * LANES, kind * pairs + pair, qkv, kind * pairs + pair, sems, run, mask, True
            )
        return copies

    for pair in range(pairs):
        for copy in loads(pair):
            copy.start()

    for pair in range(pairs):
        for copy in loads(pair):
            copy.wait()

        @pl.loop(0, total // TILE)
        def _(block):
            rows = pl.multiple_of(block * TILE, TILE)
            q_heads = lane_halves(qkv[pair, pl.ds(rows, TILE), :], 0.0)
            segq = seg_col[pl.ds(rows, TILE), :]
            segq = jnp.concatenate([segq] * (TILE // LANES), axis=1)
            first, after = key_tiles(ends_ref, rows, rows + TILE - 1, TILE, total)
            acc[...] = jnp.zeros_like(acc)
            top[...] = jnp.full_like(top, NEG)

            @pl.loop(first, after)
            def _(step):
                at = pl.multiple_of(step * TILE, TILE)
                keys = qkv[pairs + pair, pl.ds(at, TILE), :]
                v_heads = lane_halves(qkv[2 * pairs + pair, pl.ds(at, TILE), :], 1.0)
                same = segq == seg_row[:, pl.ds(at, TILE)]
                for head in range(2):
                    scores = jnp.where(same, mm(q_heads[head], keys, NT), NEG)
                    old = top[head]
                    new = jnp.maximum(old, jnp.max(scores, axis=1, keepdims=True))
                    top[head] = new
                    probs = jnp.exp(scores - jnp.concatenate([new] * (TILE // LANES), axis=1)).astype(jnp.bfloat16)
                    acc[head] = acc[head] * jnp.exp(old - new) + mm(probs, v_heads[head], NN)

            lane = lax.broadcasted_iota(jnp.int32, (TILE, LANES), 1)
            sum_a = acc[0][:, HEAD_DIM : HEAD_DIM + 1]
            sum_b = acc[1][:, 0:1]
            out[pair, pl.ds(rows, TILE), :] = jnp.where(lane < HEAD_DIM, acc[0] / sum_a, acc[1] / sum_b).astype(jnp.bfloat16)
            lse_a = (top[0] + jnp.log(sum_a)).T
            lse_b = (top[1] + jnp.log(sum_b)).T
            lse_ref[2 * pair, :, pl.ds(rows, TILE)] = lse_a[0:8]
            lse_ref[2 * pair + 1, :, pl.ds(rows, TILE)] = lse_b[0:8]

        for copy in piece_copies((ctx_own, ctx_sib), pair * LANES, pair, out, pair, out_sems, run, mask, False):
            copy.start()
    for pair in range(pairs):
        for copy in piece_copies((ctx_own, ctx_sib), pair * LANES, pair, out, pair, out_sems, run, mask, False):
            copy.wait()


def attend_forward(mask, ends, own, sib, seg_col, seg_row, run):
    half, columns = own.shape
    total = 2 * half
    pairs = columns // (3 * LANES)
    pieces = total // run
    any_spec = pl.BlockSpec(memory_space=pl.ANY)
    vmem = pl.BlockSpec(memory_space=pltpu.VMEM)
    smem = pl.BlockSpec(memory_space=pltpu.SMEM)
    return pl.pallas_call(
        functools.partial(forward_kernel, run),
        out_shape=(
            jax.ShapeDtypeStruct((half, pairs * LANES), jnp.bfloat16),
            jax.ShapeDtypeStruct((half, pairs * LANES), jnp.bfloat16),
            jax.ShapeDtypeStruct((2 * pairs, 8, total), jnp.float32),
        ),
        in_specs=[smem, smem, any_spec, any_spec, vmem, vmem],
        out_specs=(any_spec, any_spec, vmem),
        scratch_shapes=[
            pltpu.VMEM((3 * pairs, total, LANES), jnp.bfloat16),
            pltpu.VMEM((pairs, total, LANES), jnp.bfloat16),
            pltpu.VMEM((2, TILE, LANES), jnp.float32),
            pltpu.VMEM((2, TILE, LANES), jnp.float32),
            pltpu.SemaphoreType.DMA((3 * pairs, pieces)),
            pltpu.SemaphoreType.DMA((pairs, pieces)),
        ],
        compiler_params=pltpu.CompilerParams(vmem_limit_bytes=40 << 20),
        name="attend_forward",
    )(mask, ends, own, sib, seg_col, seg_row)


def backward_kernel(
    run, mask_ref, ends_ref, own, sib, ctx_own, ctx_sib, dctx_own, dctx_sib, seg_col, seg_row, lse_ref,
    d_own, d_sib, qkv, ctx, dctx, out, delta, dq, dkv, sems, out_sems
):
    total = qkv.shape[1]
    pairs = ctx.shape[0]
    width = pairs * LANES
    mask = mask_ref[0]

    def loads(pair):
        copies = []
        for kind in range(3):
            copies += piece_copies(
                (own, sib), kind * width + pair * LANES, kind * pairs + pair, qkv, kind * pairs + pair, sems, run, mask, True
            )
        copies += piece_copies((ctx_own, ctx_sib), pair * LANES, pair, ctx, 3 * pairs + pair, sems, run, mask, True)
        copies += piece_copies((dctx_own, dctx_sib), pair * LANES, pair, dctx, 4 * pairs + pair, sems, run, mask, True)
        return copies

    def stores(pair):
        copies = []
        for kind in range(3):
            copies += piece_copies(
                (d_own, d_sib), kind * width + pair * LANES, kind * pairs + pair, out, kind * pairs + pair, out_sems, run, mask, False
            )
        return copies

    for pair in range(pairs):
        for copy in loads(pair):
            copy.start()

    for pair in range(pairs):
        for copy in loads(pair):
            copy.wait()

        @pl.loop(0, total // TILE)
        def _(block):
            rows = pl.multiple_of(block * TILE, TILE)
            product = ctx[pair, pl.ds(rows, TILE), :].astype(jnp.float32) * dctx[pair, pl.ds(rows, TILE), :].astype(jnp.float32)
            product = product.T
            for head in range(2):
                part = jnp.sum(product[head * HEAD_DIM : (head + 1) * HEAD_DIM], axis=0, keepdims=True)
                delta[head, :, pl.ds(rows, TILE)] = jnp.broadcast_to(part, (8, TILE))
            dq[pl.ds(rows, TILE), :] = jnp.zeros((TILE, LANES), jnp.float32)

        @pl.loop(0, total // TILE)
        def _(block):
            rows = pl.multiple_of(block * TILE, TILE)
            k_heads = lane_halves(qkv[pairs + pair, pl.ds(rows, TILE), :], 0.0)
            v_heads = lane_halves(qkv[2 * pairs + pair, pl.ds(rows, TILE), :], 0.0)
            segk = seg_col[pl.ds(rows, TILE), :]
            segk = jnp.concatenate([segk] * (TILE // LANES), axis=1)
            first, after = key_tiles(ends_ref, rows, rows + TILE - 1, TILE, total)
            dkv[...] = jnp.zeros_like(dkv)

            @pl.loop(first, after)
            def _(step):
                at = pl.multiple_of(step * TILE, TILE)
                queries = qkv[pair, pl.ds(at, TILE), :]
                grads = dctx[pair, pl.ds(at, TILE), :]
                q_heads = lane_halves(queries, 0.0)
                g_heads = lane_halves(grads, 0.0)
                same = segk == seg_row[:, pl.ds(at, TILE)]
                for head in range(2):
                    scores = mm(k_heads[head], queries, NT)
                    lse = lse_ref[2 * pair + head, 0:1, pl.ds(at, TILE)]
                    probs = jnp.exp(jnp.where(same, scores - lse, NEG))
                    dprobs = mm(v_heads[head], grads, NT)
                    dscores = (probs * (dprobs - delta[head, 0:1, pl.ds(at, TILE)])).astype(jnp.bfloat16)
                    dkv[1] += mm(probs.astype(jnp.bfloat16), g_heads[head], NN)
                    dkv[0] += mm(dscores, q_heads[head], NN)
                    dq[pl.ds(at, TILE), :] += mm(dscores, k_heads[head], TN)

            out[pairs + pair, pl.ds(rows, TILE), :] = dkv[0].astype(jnp.bfloat16)
            out[2 * pairs + pair, pl.ds(rows, TILE), :] = dkv[1].astype(jnp.bfloat16)

        out[pair] = (dq[...] * HEAD_DIM**-0.5).astype(jnp.bfloat16)
        for copy in stores(pair):
            copy.start()
    for pair in range(pairs):
        for copy in stores(pair):
            copy.wait()


def attend_backward(mask, ends, own, sib, ctx_own, ctx_sib, dctx_own, dctx_sib, seg_col, seg_row, lse, run):
    half, columns = own.shape
    total = 2 * half
    pairs = columns // (3 * LANES)
    pieces = total // run
    any_spec = pl.BlockSpec(memory_space=pl.ANY)
    vmem = pl.BlockSpec(memory_space=pltpu.VMEM)
    smem = pl.BlockSpec(memory_space=pltpu.SMEM)
    return pl.pallas_call(
        functools.partial(backward_kernel, run),
        out_shape=(
            jax.ShapeDtypeStruct((half, columns), jnp.bfloat16),
            jax.ShapeDtypeStruct((half, columns), jnp.bfloat16),
        ),
        in_specs=[smem, smem] + [any_spec] * 6 + [vmem] * 3,
        out_specs=(any_spec, any_spec),
        scratch_shapes=[
            pltpu.VMEM((3 * pairs, total, LANES), jnp.bfloat16),
            pltpu.VMEM((pairs, total, LANES), jnp.bfloat16),
            pltpu.VMEM((pairs, total, LANES), jnp.bfloat16),
            pltpu.VMEM((3 * pairs, total, LANES), jnp.bfloat16),
            pltpu.VMEM((2, 8, total), jnp.float32),
            pltpu.VMEM((total, LANES), jnp.float32),
            pltpu.VMEM((2, TILE, LANES), jnp.float32),
            pltpu.SemaphoreType.DMA((5 * pairs, pieces)),
            pltpu.SemaphoreType.DMA((3 * pairs, pieces)),
        ],
        compiler_params=pltpu.CompilerParams(vmem_limit_bytes=48 << 20),
        name="attend_backward",
    )(mask, ends, own, sib, ctx_own, ctx_sib, dctx_own, dctx_sib, seg_col, seg_row, lse)


EPS = 1e-05


def norm_forward(resid, gain, shift):
    mean = jnp.mean(resid, axis=-1, keepdims=True)
    centered = resid - mean
    inv = lax.rsqrt(jnp.mean(centered * centered, axis=-1, keepdims=True) + EPS)
    normed = centered * inv
    return (normed * gain + shift, normed, inv)


def norm_backward(grad, normed, inv, gain):
    scaled = grad * gain
    return inv * (
        scaled
        - jnp.mean(scaled, axis=-1, keepdims=True)
        - normed * jnp.mean(scaled * normed, axis=-1, keepdims=True)
    )


def gelu_slope(pre):
    cdf = 0.5 * (1.0 + lax.erf(pre * (1.0 / math.sqrt(2.0))))
    density = jnp.exp(-0.5 * pre * pre) * (1.0 / math.sqrt(2.0 * math.pi))
    return cdf + pre * density


def doc_ids(ends, count):
    places = jnp.arange(count, dtype=jnp.int32)
    return jnp.sum((places[:, None] >= ends[None, :]).astype(jnp.int32), axis=1)


CORES = 2


def routes(nseq):
    first, second = [], []
    for core in range(CORES):
        for z in range(nseq):
            source = core * nseq + z
            first.append((source, (z // 2) * nseq + 2 * core + z % 2))
            second.append((source, (z // 2) * nseq + 2 * core + 1 - z % 2))
    return first, second


def swap(x):
    return lax.ppermute(x, "core", [(0, 1), (1, 0)])


def either(core, own, other, axis):
    return jnp.where(core == 0, jnp.concatenate([own, other], axis), jnp.concatenate([other, own], axis))


def per_device(
    tokens, doc_lengths, qkv_weight, q_bias, v_bias, out_weight, out_bias, norm1_gain, norm1_bias,
    ff_in_weight, ff_in_bias, ff_out_weight, ff_out_bias, norm2_gain, norm2_bias, out_cotangent,
):
    bf16, f32 = jnp.bfloat16, jnp.float32
    fsdp = ("xy", "core")
    nseq = lax.axis_size("seq")
    planes = lax.axis_size("xy")
    shards = planes * CORES
    core = lax.axis_index("core")
    odd = lax.axis_index("seq") % 2
    micro, run, width = tokens.shape[1:]
    assert micro == 2 and nseq == 4
    stretch = run * nseq
    mine = width // CORES
    rows = width // shards
    first, second = routes(nseq)
    back = [[(b, a) for a, b in route] for route in (first, second)]

    def spread(x):
        halves = [lax.dynamic_index_in_dim(x[0], which, 0, keepdims=False) for which in (odd, 1 - odd)]
        return [lax.ppermute(h, ("core", "seq"), r) for h, r in zip(halves, (first, second))]

    def collect(x):
        got = [lax.ppermute(x[i * run : (i + 1) * run], ("core", "seq"), back[i]) for i in range(2)]
        return jnp.where(odd == 0, jnp.stack(got), jnp.stack(got[::-1]))[None]

    pieces = spread(tokens)
    lengths = jnp.stack([doc_lengths[0], swap(doc_lengths[0])])
    z = lax.axis_index("seq")
    theirs = jnp.where(z // 2 == core, lengths[0], lengths[1])
    ends = jnp.cumsum(lax.dynamic_index_in_dim(theirs, odd, 0, keepdims=False)).astype(jnp.int32)
    seg = doc_ids(ends, stretch)
    seg_col = jnp.broadcast_to(seg[:, None], (stretch, LANES))
    seg_row = seg[None]
    mask = (odd + 2 * core).astype(jnp.int32)[None]

    small = [q_bias, v_bias, out_bias, norm1_gain, norm1_bias, ff_out_bias, norm2_gain, norm2_bias, ff_in_bias]
    vector = jnp.concatenate(small)
    packed = jnp.zeros((16, 3 * width), bf16).at[0, : vector.shape[0]].set(vector)
    packed = jnp.concatenate([qkv_weight, packed], axis=0)
    packed = lax.all_gather(packed, fsdp, axis=0, tiled=False)
    w_qkv = packed[:, :rows].reshape(width, 3, CORES, mine)
    w_mine = lax.dynamic_index_in_dim(w_qkv, core, 2, keepdims=False).reshape(width, 3 * mine)
    vectors = packed[:, rows, : vector.shape[0]].astype(f32)
    bias_q, bias_v, bias_out, gain_one, shift_one, bias_down, gain_two, shift_two = [
        vectors[:, i * rows : (i + 1) * rows].reshape(width) for i in range(8)
    ]
    bias_in = vectors[:, 8 * rows :].reshape(-1)
    w_out = lax.all_gather(out_weight, fsdp, axis=0, tiled=True)
    w_in = lax.all_gather(ff_in_weight, fsdp, axis=0, tiled=True)
    w_down = lax.all_gather(ff_out_weight, fsdp, axis=0, tiled=True)

    own_slice = lambda v: lax.dynamic_slice_in_dim(v, core * mine, mine, 0)
    bias_mine = jnp.concatenate([own_slice(bias_q), jnp.zeros((mine,), f32), own_slice(bias_v)])
    scale = jnp.concatenate([jnp.full((mine,), HEAD_DIM**-0.5, f32), jnp.ones((2 * mine,), f32)])
    x_own = jnp.concatenate(pieces)
    x_sib = jnp.concatenate([swap(p) for p in pieces])
    projected = [((mm(x, w_mine, NN) + bias_mine) * scale).astype(bf16) for x in (x_own, x_sib)]
    ctx_own, ctx_sib, lse = attend_forward(mask, ends, *projected, seg_col, seg_row, run)
    ctx_far = swap(ctx_sib)

    wo_own = lax.dynamic_slice_in_dim(w_out, core * mine, mine, 0)
    wo_far = lax.dynamic_slice_in_dim(w_out, (1 - core) * mine, mine, 0)
    attn = mm(ctx_own, wo_own, NN) + mm(ctx_far, wo_far, NN) + bias_out
    hidden, normed_one, inv_one = norm_forward(x_own.astype(f32) + attn, gain_one, shift_one)
    hidden_low = hidden.astype(bf16)
    pre = mm(hidden_low, w_in, NN) + bias_in
    act_low = jax.nn.gelu(pre, approximate=False).astype(bf16)
    resid_two = hidden + mm(act_low, w_down, NN) + bias_down
    result, normed_two, inv_two = norm_forward(resid_two, gain_two, shift_two)
    output = collect(result.astype(bf16))

    grad_out = jnp.concatenate(spread(out_cotangent)).astype(f32)
    gain_two_grad = jnp.sum(grad_out * normed_two, axis=0)
    shift_two_grad = jnp.sum(grad_out, axis=0)
    grad_two = norm_backward(grad_out, normed_two, inv_two, gain_two)
    grad_down = grad_two.astype(bf16)
    down_grad = mm(act_low, grad_down, TN).astype(bf16)
    down_grad = lax.psum_scatter(down_grad, fsdp, scatter_dimension=0, tiled=True)
    down_grad = lax.psum(down_grad, "seq").astype(f32)
    down_bias_grad = jnp.sum(grad_down.astype(f32), axis=0)
    grad_pre = (mm(grad_down, w_down, NT) * gelu_slope(pre)).astype(bf16)
    in_grad = mm(hidden_low, grad_pre, TN).astype(bf16)
    in_grad = lax.psum_scatter(in_grad, fsdp, scatter_dimension=0, tiled=True)
    in_grad = lax.psum(in_grad, "seq").astype(f32)
    in_bias_grad = jnp.sum(grad_pre.astype(f32), axis=0)
    grad_hidden = grad_two + mm(grad_pre, w_in, NT)
    gain_one_grad = jnp.sum(grad_hidden * normed_one, axis=0)
    shift_one_grad = jnp.sum(grad_hidden, axis=0)
    grad_one = norm_backward(grad_hidden, normed_one, inv_one, gain_one)
    grad_attn = grad_one.astype(bf16)
    dctx_far = swap(mm(grad_attn, wo_far, NT).astype(bf16))
    dctx_own = mm(grad_attn, wo_own, NT).astype(bf16)
    out_bias_grad = jnp.sum(grad_attn.astype(f32), axis=0)
    out_grad = [mm(c, grad_attn, TN).astype(bf16) for c in (ctx_own, ctx_far)]
    out_grad = lax.psum_scatter(either(core, *out_grad, 0), fsdp, scatter_dimension=0, tiled=True)
    out_grad = lax.psum(out_grad, "seq").astype(f32)

    d_own, d_sib = attend_backward(
        mask, ends, *projected, ctx_own, ctx_sib, dctx_own, dctx_far, seg_col, seg_row, lse, run
    )
    grad_far = swap(mm(d_sib, w_mine, NT).astype(bf16))
    input_grad = grad_one + mm(d_own, w_mine, NT) + grad_far.astype(f32)
    input_grad = collect(input_grad.astype(bf16)).astype(f32)

    qkv_grad = (mm(x_own, d_own, TN) + mm(x_sib, d_sib, TN)).astype(bf16)
    columns = jnp.sum(d_own.astype(f32), axis=0) + jnp.sum(d_sib.astype(f32), axis=0)
    none = jnp.zeros((mine,), f32)
    q_bias_grad = either(core, columns[:mine], none, 0)
    v_bias_grad = either(core, columns[2 * mine :], none, 0)
    small = [q_bias_grad, v_bias_grad, out_bias_grad, gain_one_grad, shift_one_grad, down_bias_grad,
             gain_two_grad, shift_two_grad, in_bias_grad]
    vector = jnp.concatenate([v.reshape(shards, -1) for v in small], axis=1).astype(bf16)
    vector = vector.reshape(planes, CORES, -1)
    vector = jnp.pad(vector, ((0, 0), (0, 16 - CORES), (0, 3 * mine - vector.shape[2])))
    packed = jnp.concatenate([qkv_grad.reshape(planes, CORES * rows, 3 * mine), vector], axis=1)
    packed = lax.psum_scatter(packed.reshape(-1, 3 * mine), "xy", scatter_dimension=0, tiled=True)
    packed = lax.psum(packed, "seq")
    block = packed[: CORES * rows].reshape(CORES, rows, 3 * mine)
    tail = packed[CORES * rows : CORES * rows + CORES]
    pick = lambda v, which: lax.dynamic_index_in_dim(v, which, 0, keepdims=False)
    block_far, tail_far = swap(pick(block, 1 - core)), swap(pick(tail, 1 - core))
    own_block = pick(block, core).reshape(rows, 3, 1, mine)
    qkv_final = either(core, own_block, block_far.reshape(rows, 3, 1, mine), 2).reshape(rows, 3 * width).astype(f32)
    tail = pick(tail, core).astype(f32) + tail_far.astype(f32)
    g = [tail[i * rows : (i + 1) * rows] for i in range(8)]
    return (
        output, input_grad, qkv_final, g[0], g[1], out_grad, g[2], g[3], g[4], in_grad,
        tail[8 * rows : 8 * rows + ff_in_bias.shape[0]], down_grad, g[5], g[6], g[7],
    )


def solution(mesh):
    fsdp, nseq = mesh.shape["fsdp"], mesh.shape["seq"]
    fine = Mesh(mesh.devices.reshape(fsdp // CORES, CORES, nseq), ("xy", "core", "seq"))
    shard = ("xy", "core")
    stream, matrix, vector = P(shard, None, "seq", None), P(shard, None), P(shard)
    return jax.shard_map(
        per_device,
        mesh=fine,
        in_specs=(
            stream, P(shard, None, None), matrix, vector, vector, matrix, vector, vector, vector,
            matrix, vector, matrix, vector, vector, vector, stream,
        ),
        out_specs=(
            stream, stream, matrix, vector, vector, matrix, vector, vector, vector,
            matrix, vector, matrix, vector, vector, vector,
        ),
        check_vma=False,
    )
```

```python
import functools
import math

import jax
import jax.numpy as jnp
from jax import lax
from jax.experimental import pallas as pl
from jax.experimental.pallas import tpu as pltpu
from jax.sharding import Mesh
from jax.sharding import PartitionSpec as P

HEAD_DIM = 64
LANES = 128
NEG = -1e30
TILE = 256
NT = (((1,), (1,)), ((), ()))
NN = (((1,), (0,)), ((), ()))
TN = (((0,), (0,)), ((), ()))


def mm(left, right, dims):
    return lax.dot_general(left, right, dims, preferred_element_type=jnp.float32)


def key_tiles(ends_ref, first, last, tile, total):
    low = jnp.int32(0)
    high = jnp.int32(total)
    for doc in reversed(range(ends_ref.shape[0])):
        end = ends_ref[doc]
        low = jnp.maximum(low, jnp.where(end <= first, end, 0))
        high = jnp.minimum(high, jnp.where(end > last, end, total))
    return low // tile, (high + tile - 1) // tile


def lane_halves(x, fill):
    lane = lax.broadcasted_iota(jnp.int32, x.shape, 1)
    fill = jnp.full_like(x, fill)
    return jnp.where(lane < HEAD_DIM, x, fill), jnp.where(lane < HEAD_DIM, fill, x)


def piece_copies(halves, columns, place, scratch, slot, sems, run, mask, inbound):
    copies = []
    pieces = halves[0].shape[0] // run
    for half, ref in enumerate(halves):
        for part in range(pieces):
            index = half * pieces + part
            natural = pl.multiple_of(jnp.bitwise_xor(mask, index) * run, run)
            outer = ref.at[pl.ds(part * run, run), pl.ds(columns, LANES)]
            inner = scratch.at[place, pl.ds(natural, run), :]
            ends = (outer, inner) if inbound else (inner, outer)
            copies.append(pltpu.make_async_copy(ends[0], ends[1], sems.at[slot, index]))
    return copies


def forward_kernel(run, mask_ref, ends_ref, own, sib, seg_col, seg_row, ctx_own, ctx_sib, lse_ref, qkv, out, acc, top, sems, out_sems):
    total = qkv.shape[1]
    pairs = out.shape[0]
    mask = mask_ref[0]

    def loads(pair):
        copies = []
        for kind in range(3):
            copies += piece_copies(
                (own, sib), (3 * pair + kind) * LANES, kind * pairs + pair, qkv, kind * pairs + pair, sems, run, mask, True
            )
        return copies

    for pair in range(pairs):
        for copy in loads(pair):
            copy.start()

    for pair in range(pairs):
        for copy in loads(pair):
            copy.wait()

        @pl.loop(0, total // TILE)
        def _(block):
            rows = pl.multiple_of(block * TILE, TILE)
            q_heads = lane_halves(qkv[pair, pl.ds(rows, TILE), :], 0.0)
            segq = seg_col[pl.ds(rows, TILE), :]
            segq = jnp.concatenate([segq] * (TILE // LANES), axis=1)
            first, after = key_tiles(ends_ref, rows, rows + TILE - 1, TILE, total)
            acc[...] = jnp.zeros_like(acc)
            top[...] = jnp.full_like(top, NEG)

            @pl.loop(first, after)
            def _(step):
                at = pl.multiple_of(step * TILE, TILE)
                keys = qkv[pairs + pair, pl.ds(at, TILE), :]
                v_heads = lane_halves(qkv[2 * pairs + pair, pl.ds(at, TILE), :], 1.0)
                same = segq == seg_row[:, pl.ds(at, TILE)]
                for head in range(2):
                    scores = jnp.where(same, mm(q_heads[head], keys, NT), NEG)
                    old = top[head]
                    new = jnp.maximum(old, jnp.max(scores, axis=1, keepdims=True))
                    top[head] = new
                    probs = jnp.exp(scores - jnp.concatenate([new] * (TILE // LANES), axis=1)).astype(jnp.bfloat16)
                    acc[head] = acc[head] * jnp.exp(old - new) + mm(probs, v_heads[head], NN)

            lane = lax.broadcasted_iota(jnp.int32, (TILE, LANES), 1)
            sum_a = acc[0][:, HEAD_DIM : HEAD_DIM + 1]
            sum_b = acc[1][:, 0:1]
            out[pair, pl.ds(rows, TILE), :] = jnp.where(lane < HEAD_DIM, acc[0] / sum_a, acc[1] / sum_b).astype(jnp.bfloat16)
            lse_a = (top[0] + jnp.log(sum_a)).T
            lse_b = (top[1] + jnp.log(sum_b)).T
            lse_ref[2 * pair, :, pl.ds(rows, TILE)] = lse_a[0:8]
            lse_ref[2 * pair + 1, :, pl.ds(rows, TILE)] = lse_b[0:8]

        for copy in piece_copies((ctx_own, ctx_sib), pair * LANES, pair, out, pair, out_sems, run, mask, False):
            copy.start()
    for pair in range(pairs):
        for copy in piece_copies((ctx_own, ctx_sib), pair * LANES, pair, out, pair, out_sems, run, mask, False):
            copy.wait()


def attend_forward(mask, ends, own, sib, seg_col, seg_row, run):
    half, columns = own.shape
    total = 2 * half
    pairs = columns // (3 * LANES)
    pieces = total // run
    any_spec = pl.BlockSpec(memory_space=pl.ANY)
    vmem = pl.BlockSpec(memory_space=pltpu.VMEM)
    smem = pl.BlockSpec(memory_space=pltpu.SMEM)
    return pl.pallas_call(
        functools.partial(forward_kernel, run),
        out_shape=(
            jax.ShapeDtypeStruct((half, pairs * LANES), jnp.bfloat16),
            jax.ShapeDtypeStruct((half, pairs * LANES), jnp.bfloat16),
            jax.ShapeDtypeStruct((2 * pairs, 8, total), jnp.float32),
        ),
        in_specs=[smem, smem, any_spec, any_spec, vmem, vmem],
        out_specs=(any_spec, any_spec, vmem),
        scratch_shapes=[
            pltpu.VMEM((3 * pairs, total, LANES), jnp.bfloat16),
            pltpu.VMEM((pairs, total, LANES), jnp.bfloat16),
            pltpu.VMEM((2, TILE, LANES), jnp.float32),
            pltpu.VMEM((2, TILE, LANES), jnp.float32),
            pltpu.SemaphoreType.DMA((3 * pairs, pieces)),
            pltpu.SemaphoreType.DMA((pairs, pieces)),
        ],
        compiler_params=pltpu.CompilerParams(vmem_limit_bytes=40 << 20),
        cost_estimate=pl.CostEstimate(flops=50_000_000_000, bytes_accessed=8_000_000, transcendentals=0),
        name="attend_forward",
    )(mask, ends, own, sib, seg_col, seg_row)


def backward_kernel(
    run, pair, mask_ref, ends_ref, own, sib, ctx_own, ctx_sib, dctx_own, dctx_sib, seg_col, seg_row, lse_ref,
    d_own, d_sib, qkv, ctx, out, delta, dq, dkv, sems, out_sems
):
    total = qkv.shape[1]
    mask = mask_ref[0]
    loads, stores = [], []
    for kind in range(3):
        loads += piece_copies((own, sib), (3 * pair + kind) * LANES, kind, qkv, kind, sems, run, mask, True)
        stores += piece_copies((d_own, d_sib), kind * LANES, kind, out, kind, out_sems, run, mask, False)
    loads += piece_copies((ctx_own, ctx_sib), pair * LANES, 0, ctx, 3, sems, run, mask, True)
    loads += piece_copies((dctx_own, dctx_sib), pair * LANES, 1, ctx, 4, sems, run, mask, True)
    for copy in loads:
        copy.start()
    for copy in loads:
        copy.wait()

    @pl.loop(0, total // TILE)
    def _(block):
        rows = pl.multiple_of(block * TILE, TILE)
        product = ctx[0, pl.ds(rows, TILE), :].astype(jnp.float32) * ctx[1, pl.ds(rows, TILE), :].astype(jnp.float32)
        product = product.T
        for head in range(2):
            part = jnp.sum(product[head * HEAD_DIM : (head + 1) * HEAD_DIM], axis=0, keepdims=True)
            delta[head, :, pl.ds(rows, TILE)] = jnp.broadcast_to(part, (8, TILE))
        dq[pl.ds(rows, TILE), :] = jnp.zeros((TILE, LANES), jnp.float32)

    @pl.loop(0, total // TILE)
    def _(block):
        rows = pl.multiple_of(block * TILE, TILE)
        k_heads = lane_halves(qkv[1, pl.ds(rows, TILE), :], 0.0)
        v_heads = lane_halves(qkv[2, pl.ds(rows, TILE), :], 0.0)
        segk = seg_col[pl.ds(rows, TILE), :]
        segk = jnp.concatenate([segk] * (TILE // LANES), axis=1)
        first, after = key_tiles(ends_ref, rows, rows + TILE - 1, TILE, total)
        dkv[...] = jnp.zeros_like(dkv)

        @pl.loop(first, after)
        def _(step):
            at = pl.multiple_of(step * TILE, TILE)
            queries = qkv[0, pl.ds(at, TILE), :]
            grads = ctx[1, pl.ds(at, TILE), :]
            q_heads = lane_halves(queries, 0.0)
            g_heads = lane_halves(grads, 0.0)
            same = segk == seg_row[:, pl.ds(at, TILE)]
            for head in range(2):
                scores = mm(k_heads[head], queries, NT)
                lse = lse_ref[2 * pair + head, 0:1, pl.ds(at, TILE)]
                probs = jnp.exp(jnp.where(same, scores - lse, NEG))
                dprobs = mm(v_heads[head], grads, NT)
                dscores = (probs * (dprobs - delta[head, 0:1, pl.ds(at, TILE)])).astype(jnp.bfloat16)
                dkv[1] += mm(probs.astype(jnp.bfloat16), g_heads[head], NN)
                dkv[0] += mm(dscores, q_heads[head], NN)
                dq[pl.ds(at, TILE), :] += mm(dscores, k_heads[head], TN)

        out[1, pl.ds(rows, TILE), :] = dkv[0].astype(jnp.bfloat16)
        out[2, pl.ds(rows, TILE), :] = dkv[1].astype(jnp.bfloat16)

    out[0] = (dq[...] * HEAD_DIM**-0.5).astype(jnp.bfloat16)
    for copy in stores:
        copy.start()
    for copy in stores:
        copy.wait()


def attend_backward(pair, mask, ends, own, sib, ctx_own, ctx_sib, dctx_own, dctx_sib, seg_col, seg_row, lse, run):
    half = own.shape[0]
    total = 2 * half
    pieces = total // run
    any_spec = pl.BlockSpec(memory_space=pl.ANY)
    vmem = pl.BlockSpec(memory_space=pltpu.VMEM)
    smem = pl.BlockSpec(memory_space=pltpu.SMEM)
    return pl.pallas_call(
        functools.partial(backward_kernel, run, pair),
        out_shape=(
            jax.ShapeDtypeStruct((half, 3 * LANES), jnp.bfloat16),
            jax.ShapeDtypeStruct((half, 3 * LANES), jnp.bfloat16),
        ),
        in_specs=[smem, smem] + [any_spec] * 6 + [vmem] * 3,
        out_specs=(any_spec, any_spec),
        scratch_shapes=[
            pltpu.VMEM((3, total, LANES), jnp.bfloat16),
            pltpu.VMEM((2, total, LANES), jnp.bfloat16),
            pltpu.VMEM((3, total, LANES), jnp.bfloat16),
            pltpu.VMEM((2, 8, total), jnp.float32),
            pltpu.VMEM((total, LANES), jnp.float32),
            pltpu.VMEM((2, TILE, LANES), jnp.float32),
            pltpu.SemaphoreType.DMA((5, pieces)),
            pltpu.SemaphoreType.DMA((3, pieces)),
        ],
        compiler_params=pltpu.CompilerParams(vmem_limit_bytes=24 << 20),
        cost_estimate=pl.CostEstimate(flops=20_000_000_000, bytes_accessed=8_000_000, transcendentals=0),
        name=f"attend_backward_{pair}",
    )(mask, ends, own, sib, ctx_own, ctx_sib, dctx_own, dctx_sib, seg_col, seg_row, lse)


EPS = 1e-05


def norm_forward(resid, gain, shift):
    mean = jnp.mean(resid, axis=-1, keepdims=True)
    centered = resid - mean
    inv = lax.rsqrt(jnp.mean(centered * centered, axis=-1, keepdims=True) + EPS)
    normed = centered * inv
    return (normed * gain + shift, normed, inv)


def norm_backward(grad, normed, inv, gain):
    scaled = grad * gain
    return inv * (
        scaled
        - jnp.mean(scaled, axis=-1, keepdims=True)
        - normed * jnp.mean(scaled * normed, axis=-1, keepdims=True)
    )


def gelu_slope(pre):
    cdf = 0.5 * (1.0 + lax.erf(pre * (1.0 / math.sqrt(2.0))))
    density = jnp.exp(-0.5 * pre * pre) * (1.0 / math.sqrt(2.0 * math.pi))
    return cdf + pre * density


def doc_ids(ends, count):
    places = jnp.arange(count, dtype=jnp.int32)
    return jnp.sum((places[:, None] >= ends[None, :]).astype(jnp.int32), axis=1)


CORES = 2


def routes(nseq):
    first, second = [], []
    for core in range(CORES):
        for z in range(nseq):
            source = core * nseq + z
            first.append((source, (z // 2) * nseq + 2 * core + z % 2))
            second.append((source, (z // 2) * nseq + 2 * core + 1 - z % 2))
    return first, second


def swap(x):
    return lax.ppermute(x, "core", [(0, 1), (1, 0)])


def after(value, *done):
    return lax.optimization_barrier((value, done))[0]


def pick(value, which, axis=0):
    return lax.dynamic_index_in_dim(value, which, axis, keepdims=False)


def total(keep, received):
    return (keep.astype(jnp.float32) + received.astype(jnp.float32)).astype(jnp.bfloat16)


class Halving:
    def __init__(self, blocks, planes):
        bits = planes.bit_length() - 1
        rows = blocks.shape[1]
        self.planes = planes
        self.orders = (list(range(bits)), list(range(bits))[::-1])
        self.left = [list(range(bits))[::-1] for _ in range(2)]
        parts = (blocks[:, : rows // 2], blocks[:, rows // 2 :])
        self.parts = [p.reshape((2,) * bits + p.shape[1:]) for p in parts]
        self.steps = bits

    def send(self, step):
        place = lax.axis_index("xy")
        self.keep, self.received, self.sent = [], [], []
        for half in range(2):
            bit = self.orders[half][step]
            axis = self.left[half].index(bit)
            mine = (place >> bit) % 2
            self.left[half].remove(bit)
            out = pick(self.parts[half], 1 - mine, axis)
            self.keep.append(pick(self.parts[half], mine, axis))
            self.sent.append(out)
            self.received.append(lax.ppermute(out, "xy", [(i, i ^ (1 << bit)) for i in range(self.planes)]))

    def add(self, *done):
        self.parts = [total(k, after(r, *done)) for k, r in zip(self.keep, self.received)]

    def result(self):
        return jnp.concatenate(self.parts)


class Spread:
    def __init__(self, value, nseq):
        self.nseq, self.rows = nseq, value.shape[0] // nseq
        self.me = lax.axis_index("seq")
        quarter = lambda which: lax.dynamic_slice_in_dim(value, (which % nseq) * self.rows, self.rows, 0)
        self.keep = quarter(self.me)
        self.received = [self.shift(quarter(self.me + d), d) for d in range(1, nseq)]

    def shift(self, value, distance):
        return lax.ppermute(value, "seq", [(i, (i + distance) % self.nseq) for i in range(self.nseq)])

    def add(self, *done):
        parts = [self.keep] + [after(r, *done) for r in self.received]
        self.keep = sum(p.astype(jnp.float32) for p in parts).astype(jnp.bfloat16)
        self.received = [self.shift(self.keep, d) for d in range(1, self.nseq)]

    def result(self):
        whole = jnp.zeros((self.nseq * self.rows,) + self.keep.shape[1:], jnp.bfloat16)
        for d, part in enumerate([self.keep] + self.received):
            start = ((self.me - d) % self.nseq) * self.rows
            whole = lax.dynamic_update_slice_in_dim(whole, part, start, 0)
        return whole


def either(core, own, other, axis):
    return jnp.where(core == 0, jnp.concatenate([own, other], axis), jnp.concatenate([other, own], axis))


def per_device(
    tokens, doc_lengths, qkv_weight, q_bias, v_bias, out_weight, out_bias, norm1_gain, norm1_bias,
    ff_in_weight, ff_in_bias, ff_out_weight, ff_out_bias, norm2_gain, norm2_bias, out_cotangent,
):
    bf16, f32 = jnp.bfloat16, jnp.float32
    fsdp = ("xy", "core")
    nseq = lax.axis_size("seq")
    planes = lax.axis_size("xy")
    shards = planes * CORES
    core = lax.axis_index("core")
    odd = lax.axis_index("seq") % 2
    micro, run, width = tokens.shape[1:]
    assert micro == 2 and nseq == 4
    stretch = run * nseq
    mine = width // CORES
    rows = width // shards
    first, second = routes(nseq)
    back = [[(b, a) for a, b in route] for route in (first, second)]

    def spread(x):
        halves = [lax.dynamic_index_in_dim(x[0], which, 0, keepdims=False) for which in (odd, 1 - odd)]
        return [lax.ppermute(h, ("core", "seq"), r) for h, r in zip(halves, (first, second))]

    def collect(x):
        got = [lax.ppermute(x[i * run : (i + 1) * run], ("core", "seq"), back[i]) for i in range(2)]
        return jnp.where(odd == 0, jnp.stack(got), jnp.stack(got[::-1]))[None]

    pieces = spread(tokens)
    lengths = jnp.stack([doc_lengths[0], swap(doc_lengths[0])])
    z = lax.axis_index("seq")
    theirs = jnp.where(z // 2 == core, lengths[0], lengths[1])
    ends = jnp.cumsum(lax.dynamic_index_in_dim(theirs, odd, 0, keepdims=False)).astype(jnp.int32)
    seg = doc_ids(ends, stretch)
    seg_col = jnp.broadcast_to(seg[:, None], (stretch, LANES))
    seg_row = seg[None]
    mask = (odd + 2 * core).astype(jnp.int32)[None]

    pairs = mine // LANES
    own_columns = qkv_weight.reshape(rows, 3, CORES, pairs, LANES)
    own_columns = jnp.moveaxis(own_columns, (2, 3), (0, 2)).reshape(CORES, rows, 3 * mine)
    kept = pick(own_columns, core)
    w_mine = either(core, kept, swap(pick(own_columns, 1 - core)), 0)
    w_mine = lax.all_gather(w_mine, "xy", axis=0, tiled=True)
    small = [q_bias, v_bias, out_bias, norm1_gain, norm1_bias, ff_out_bias, norm2_gain, norm2_bias, ff_in_bias]
    vectors = lax.all_gather(jnp.concatenate(small)[None, None], fsdp, axis=0, tiled=True)[:, 0].astype(f32)
    bias_q, bias_v, bias_out, gain_one, shift_one, bias_down, gain_two, shift_two = [
        vectors[:, i * rows : (i + 1) * rows].reshape(width) for i in range(8)
    ]
    bias_in = vectors[:, 8 * rows :].reshape(-1)
    w_out = lax.all_gather(out_weight, fsdp, axis=0, tiled=True)
    w_in = lax.all_gather(ff_in_weight, fsdp, axis=0, tiled=True)
    w_down = lax.all_gather(ff_out_weight, fsdp, axis=0, tiled=True)

    own_slice = lambda v: lax.dynamic_slice_in_dim(v, core * mine, mine, 0).reshape(pairs, LANES)
    one = jnp.ones((pairs, LANES), f32)
    bias_mine = jnp.stack([own_slice(bias_q), 0.0 * one, own_slice(bias_v)], axis=1).reshape(-1)
    scale = jnp.stack([HEAD_DIM**-0.5 * one, one, one], axis=1).reshape(-1)
    x_own = jnp.concatenate(pieces)
    x_sib = jnp.concatenate([swap(p) for p in pieces])
    projected = [((mm(x, w_mine, NN) + bias_mine) * scale).astype(bf16) for x in (x_own, x_sib)]
    ctx_own, ctx_sib, lse = attend_forward(mask, ends, *projected, seg_col, seg_row, run)
    ctx_far = swap(ctx_sib)

    wo_own = lax.dynamic_slice_in_dim(w_out, core * mine, mine, 0)
    wo_far = lax.dynamic_slice_in_dim(w_out, (1 - core) * mine, mine, 0)
    attn = mm(ctx_own, wo_own, NN) + mm(ctx_far, wo_far, NN) + bias_out
    hidden, normed_one, inv_one = norm_forward(x_own.astype(f32) + attn, gain_one, shift_one)
    hidden_low = hidden.astype(bf16)
    pre = mm(hidden_low, w_in, NN) + bias_in
    act_low = jax.nn.gelu(pre, approximate=False).astype(bf16)
    resid_two = hidden + mm(act_low, w_down, NN) + bias_down
    result, normed_two, inv_two = norm_forward(resid_two, gain_two, shift_two)
    output = collect(result.astype(bf16))

    grad_out = jnp.concatenate(spread(out_cotangent)).astype(f32)
    gain_two_grad = jnp.sum(grad_out * normed_two, axis=0)
    shift_two_grad = jnp.sum(grad_out, axis=0)
    grad_two = norm_backward(grad_out, normed_two, inv_two, gain_two)
    grad_down = grad_two.astype(bf16)

    def cores(blocks):
        return pick(blocks, core, 1), swap(pick(blocks, 1 - core, 1))

    down_grad = cores(mm(act_low, grad_down, TN).astype(bf16).reshape(planes, CORES, -1, width))
    down_bias_grad = jnp.sum(grad_down.astype(f32), axis=0)
    grad_pre = (mm(grad_down, w_down, NT) * gelu_slope(pre)).astype(bf16)
    in_grad = cores(mm(hidden_low, grad_pre, TN).astype(bf16).reshape(planes, CORES, rows, -1))
    in_bias_grad = jnp.sum(grad_pre.astype(f32), axis=0)
    grad_hidden = grad_two + mm(grad_pre, w_in, NT)
    gain_one_grad = jnp.sum(grad_hidden * normed_one, axis=0)
    shift_one_grad = jnp.sum(grad_hidden, axis=0)
    grad_one = norm_backward(grad_hidden, normed_one, inv_one, gain_one)
    grad_attn = grad_one.astype(bf16)
    dctx_far = swap(mm(grad_attn, wo_far, NT).astype(bf16))
    dctx_own = mm(grad_attn, wo_own, NT).astype(bf16)
    out_bias_grad = jnp.sum(grad_attn.astype(f32), axis=0)
    out_grad = [mm(c, grad_attn, TN).astype(bf16) for c in (ctx_own, ctx_far)]
    out_grad = cores(either(core, *out_grad, 0).reshape(planes, CORES, rows, width))
    small = [out_bias_grad, gain_one_grad, shift_one_grad, down_bias_grad, gain_two_grad, shift_two_grad, in_bias_grad]
    vector = jnp.concatenate([v.reshape(shards, -1) for v in small], axis=1).astype(bf16)
    lines = -(-vector.shape[1] // width)
    vector = jnp.pad(vector, ((0, 0), (0, lines * width - vector.shape[1])))
    vector = jnp.pad(vector.reshape(shards, lines, width), ((0, 0), (0, 32 - lines), (0, 0)))
    vector = cores(vector.reshape(planes, CORES, 32, width))
    inner = in_grad[0].shape[2] // width
    joined = []
    for which in range(2):
        wide = in_grad[which]
        wide = [wide[:, :, i * width : (i + 1) * width] for i in range(inner)]
        joined.append(jnp.concatenate([down_grad[which]] + wide + [out_grad[which], vector[which]], axis=1))
    early = Halving(total(*joined), planes)
    early.send(0)

    def attend(pair, *ready):
        held = after(mask, *ready)
        return attend_backward(
            pair, held, ends, *projected, ctx_own, ctx_sib, dctx_own, dctx_far, seg_col, seg_row, lse, run
        )

    def weight_sums(grads):
        near = jnp.concatenate([g[0] for g in grads], axis=1)
        far = jnp.concatenate([g[1] for g in grads], axis=1)
        matrix = (mm(x_own, near, TN) + mm(x_sib, far, TN)).astype(bf16)
        column = (jnp.sum(near.astype(f32), axis=0) + jnp.sum(far.astype(f32), axis=0)).astype(bf16)
        column = jnp.pad(column[None], ((0, 63), (0, 0)))
        column = jnp.broadcast_to(column, (planes,) + column.shape)
        return jnp.concatenate([matrix.reshape(planes, CORES * rows, -1), column], axis=1)

    grads = [attend(0, *early.sent)]
    sent = []
    for pair in range(1, pairs):
        if len(early.left[0]):
            early.add(grads[-1][0])
            early.send(early.steps - len(early.left[0]))
            sent = early.sent
        if pair == pairs - 1:
            first_sums = Halving(weight_sums(grads), planes)
            first_sums.send(0)
            sent = sent + first_sums.sent
        grads.append(attend(pair, *sent))
    while len(early.left[0]):
        early.add(grads[-1][0])
        early.send(early.steps - len(early.left[0]))
    early.add(grads[-1][0])
    early_sum = Spread(early.result(), nseq)

    near = jnp.concatenate([g[0] for g in grads], axis=1)
    far = jnp.concatenate([g[1] for g in grads], axis=1)
    grad_far = swap(mm(far, w_mine, NT).astype(bf16))
    last_sums = Halving(weight_sums(grads[-1:]), planes)
    last_sums.send(0)
    input_grad = grad_one + mm(near, w_mine, NT) + grad_far.astype(f32)
    input_grad = collect(input_grad.astype(bf16)).astype(f32)
    for step in range(last_sums.steps):
        for sums in (first_sums, last_sums):
            sums.add()
            if step + 1 < sums.steps:
                sums.send(step + 1)
    qkv_sum = Spread(jnp.concatenate([first_sums.result(), last_sums.result()], axis=1), nseq)
    early_sum.add()
    qkv_sum.add()
    early_total = early_sum.result()
    qkv_total = qkv_sum.result()

    down_rows = down_grad[0].shape[1]
    down_final = early_total[:down_rows].astype(f32)
    wide = [early_total[down_rows + i * rows : down_rows + (i + 1) * rows] for i in range(inner)]
    in_final = jnp.concatenate(wide, axis=1).astype(f32)
    at = down_rows + inner * rows
    out_final = early_total[at : at + rows].astype(f32)
    at = at + rows
    line = early_total[at : at + lines].reshape(-1).astype(f32)
    out_bias_final, g1, b1, down_bias_final, g2, b2 = [line[i * rows : (i + 1) * rows] for i in range(6)]
    in_bias_final = line[6 * rows : 6 * rows + ff_in_bias.shape[0]]

    part = qkv_total
    column = part[CORES * rows]
    other = swap(jnp.concatenate([lax.dynamic_slice_in_dim(part, (1 - core) * rows, rows, 0), part[CORES * rows : CORES * rows + 16]]))
    own_block = lax.dynamic_slice_in_dim(part, core * rows, rows, 0)
    spread_out = lambda v: jnp.moveaxis(v.reshape(-1, pairs, 3, LANES), 2, 1).reshape(-1, 3, 1, mine)
    qkv_final = either(core, spread_out(own_block), spread_out(other[:rows]), 2).reshape(rows, 3 * width).astype(f32)
    sums = either(core, spread_out(column), spread_out(other[rows]), 2).reshape(3, width)
    shard = lax.axis_index("xy") * CORES + core
    q_final = lax.dynamic_slice_in_dim(sums[0], shard * rows, rows, 0).astype(f32)
    v_final = lax.dynamic_slice_in_dim(sums[2], shard * rows, rows, 0).astype(f32)
    return (
        output, input_grad, qkv_final, q_final, v_final, out_final, out_bias_final, g1, b1, in_final,
        in_bias_final, down_final, down_bias_final, g2, b2,
    )


def solution(mesh):
    fsdp, nseq = mesh.shape["fsdp"], mesh.shape["seq"]
    fine = Mesh(mesh.devices.reshape(fsdp // CORES, CORES, nseq), ("xy", "core", "seq"))
    shard = ("xy", "core")
    stream, matrix, vector = P(shard, None, "seq", None), P(shard, None), P(shard)
    return jax.shard_map(
        per_device,
        mesh=fine,
        in_specs=(
            stream, P(shard, None, None), matrix, vector, vector, matrix, vector, vector, vector,
            matrix, vector, matrix, vector, vector, vector, stream,
        ),
        out_specs=(
            stream, stream, matrix, vector, vector, matrix, vector, vector, vector,
            matrix, vector, matrix, vector, vector, vector,
        ),
        check_vma=False,
    )
```

```python
import functools
import math

import jax
import jax.numpy as jnp
from jax import lax
from jax.experimental import pallas as pl
from jax.experimental.pallas import tpu as pltpu
from jax.sharding import Mesh
from jax.sharding import PartitionSpec as P

HEAD_DIM = 64
LANES = 128
NEG = -1e30
TILE = 256
VALUE_ROWS = HEAD_DIM + 16
KEY_TILES = 2
QUERY_TILES = 2
NT = (((1,), (1,)), ((), ()))
NN = (((1,), (0,)), ((), ()))
TN = (((0,), (0,)), ((), ()))


def mm(left, right, dims):
    return lax.dot_general(left, right, dims, preferred_element_type=jnp.float32)


def key_tiles(ends_ref, first, last, tile, total):
    low = jnp.int32(0)
    high = jnp.int32(total)
    for doc in reversed(range(ends_ref.shape[0])):
        end = ends_ref[doc]
        low = jnp.maximum(low, jnp.where(end <= first, end, 0))
        high = jnp.minimum(high, jnp.where(end > last, end, total))
    return low // tile, (high + tile - 1) // tile


def spans(first, after, count, tiles):
    steps = (after - first + count - 1) // count
    return jnp.minimum(first, tiles - steps * count), steps


def lane_halves(x, fill):
    lane = lax.broadcasted_iota(jnp.int32, x.shape, 1)
    fill = jnp.full_like(x, fill)
    return jnp.where(lane < HEAD_DIM, x, fill), jnp.where(lane < HEAD_DIM, fill, x)


def piece_copies(halves, columns, place, scratch, slot, sems, run, mask, inbound):
    copies = []
    pieces = halves[0].shape[0] // run
    for half, ref in enumerate(halves):
        for part in range(pieces):
            index = half * pieces + part
            natural = pl.multiple_of(jnp.bitwise_xor(mask, index) * run, run)
            outer = ref.at[pl.ds(part * run, run), pl.ds(columns, LANES)]
            inner = scratch.at[place, pl.ds(natural, run), :]
            ends = (outer, inner) if inbound else (inner, outer)
            copies.append(pltpu.make_async_copy(ends[0], ends[1], sems.at[slot, index]))
    return copies


def forward_kernel(run, mask_ref, ends_ref, own, sib, seg_col, seg_row, ctx_own, ctx_sib, lse_ref, qkv, out, turned, acc, top, sems, out_sems):
    total = qkv.shape[1]
    pairs = out.shape[0]
    mask = mask_ref[0]

    def loads(pair):
        copies = []
        for kind in range(3):
            copies += piece_copies(
                (own, sib), (3 * pair + kind) * LANES, kind * pairs + pair, qkv, kind * pairs + pair, sems, run, mask, True
            )
        return copies

    for pair in range(pairs):
        for copy in loads(pair):
            copy.start()

    for head in range(2 * pairs):
        turned[head, HEAD_DIM:, :] = jnp.ones((VALUE_ROWS - HEAD_DIM, total), jnp.bfloat16)
    for pair in range(pairs):
        for copy in loads(pair):
            copy.wait()
    heads = [(pair, head) for pair in range(pairs) for head in range(2)]
    if True:

        @pl.loop(0, total // TILE)
        def _(block):
            rows = pl.multiple_of(block * TILE, TILE)
            for pair in range(pairs):
                values = qkv[2 * pairs + pair, pl.ds(rows, TILE), :].astype(jnp.float32).T.astype(jnp.bfloat16)
                for head in range(2):
                    turned[2 * pair + head, :HEAD_DIM, pl.ds(rows, TILE)] = values[head * HEAD_DIM : (head + 1) * HEAD_DIM]

        @pl.loop(0, total // TILE)
        def _(block):
            rows = pl.multiple_of(block * TILE, TILE)
            q_heads = sum([list(lane_halves(qkv[pair, pl.ds(rows, TILE), :], 0.0)) for pair in range(pairs)], [])
            segq = seg_row[:, pl.ds(rows, TILE)]
            first, after = key_tiles(ends_ref, rows, rows + TILE - 1, TILE, total)
            acc[...] = jnp.zeros_like(acc)
            top[...] = jnp.full_like(top, NEG)

            first, steps = spans(first, after, KEY_TILES, total // TILE)

            @pl.loop(0, steps)
            def _(step):
                at = pl.multiple_of((first + step * KEY_TILES) * TILE, TILE)
                keys = [qkv[pairs + pair, pl.ds(at, KEY_TILES * TILE), :] for pair in range(pairs)]
                segk = seg_col[pl.ds(at, KEY_TILES * TILE), :]
                same = jnp.concatenate([segk] * (TILE // LANES), axis=1) == segq
                for head in range(2 * pairs):
                    scores = jnp.where(same, mm(keys[head // 2], q_heads[head], NT), NEG)
                    old = top[head, 0:1]
                    new = jnp.maximum(old, jnp.max(scores, axis=0, keepdims=True))
                    probs = jnp.exp(scores - new).astype(jnp.bfloat16)
                    acc[head] = acc[head] * jnp.exp(old - new) + mm(turned[head, :, pl.ds(at, KEY_TILES * TILE)], probs, NN)
                    top[head] = jnp.broadcast_to(new, (8, TILE))

            for pair in range(pairs):
                parts = []
                for head in (2 * pair, 2 * pair + 1):
                    weight = acc[head, HEAD_DIM : HEAD_DIM + 1]
                    parts.append(acc[head, :HEAD_DIM] / weight)
                    lse_ref[head, :, pl.ds(rows, TILE)] = top[head] + jnp.log(acc[head, HEAD_DIM : HEAD_DIM + 8])
                out[pair, pl.ds(rows, TILE), :] = jnp.concatenate(parts, axis=0).T.astype(jnp.bfloat16)

    for pair in range(pairs):
        for copy in piece_copies((ctx_own, ctx_sib), pair * LANES, pair, out, pair, out_sems, run, mask, False):
            copy.start()
    for pair in range(pairs):
        for copy in piece_copies((ctx_own, ctx_sib), pair * LANES, pair, out, pair, out_sems, run, mask, False):
            copy.wait()


def attend_forward(mask, ends, own, sib, seg_col, seg_row, run):
    half, columns = own.shape
    total = 2 * half
    pairs = columns // (3 * LANES)
    pieces = total // run
    any_spec = pl.BlockSpec(memory_space=pl.ANY)
    vmem = pl.BlockSpec(memory_space=pltpu.VMEM)
    smem = pl.BlockSpec(memory_space=pltpu.SMEM)
    return pl.pallas_call(
        functools.partial(forward_kernel, run),
        out_shape=(
            jax.ShapeDtypeStruct((half, pairs * LANES), jnp.bfloat16),
            jax.ShapeDtypeStruct((half, pairs * LANES), jnp.bfloat16),
            jax.ShapeDtypeStruct((2 * pairs, 8, total), jnp.float32),
        ),
        in_specs=[smem, smem, any_spec, any_spec, vmem, vmem],
        out_specs=(any_spec, any_spec, vmem),
        scratch_shapes=[
            pltpu.VMEM((3 * pairs, total, LANES), jnp.bfloat16),
            pltpu.VMEM((pairs, total, LANES), jnp.bfloat16),
            pltpu.VMEM((2 * pairs, VALUE_ROWS, total), jnp.bfloat16),
            pltpu.VMEM((2 * pairs, VALUE_ROWS, TILE), jnp.float32),
            pltpu.VMEM((2 * pairs, 8, TILE), jnp.float32),
            pltpu.SemaphoreType.DMA((3 * pairs, pieces)),
            pltpu.SemaphoreType.DMA((pairs, pieces)),
        ],
        compiler_params=pltpu.CompilerParams(vmem_limit_bytes=40 << 20),
        cost_estimate=pl.CostEstimate(flops=50_000_000_000, bytes_accessed=8_000_000, transcendentals=0),
        name="attend_forward",
    )(mask, ends, own, sib, seg_col, seg_row)


def backward_kernel(
    run, pair, mask_ref, ends_ref, own, sib, ctx_own, ctx_sib, dctx_own, dctx_sib, seg_col, seg_row, lse_ref,
    d_own, d_sib, qkv, ctx, out, turned, delta, dq, dkv, sems, out_sems
):
    total = qkv.shape[1]
    mask = mask_ref[0]
    loads, stores = [], []
    for kind in range(3):
        loads += piece_copies((own, sib), (3 * pair + kind) * LANES, kind, qkv, kind, sems, run, mask, True)
        stores += piece_copies((d_own, d_sib), kind * LANES, kind, out, kind, out_sems, run, mask, False)
    loads += piece_copies((ctx_own, ctx_sib), pair * LANES, 0, ctx, 3, sems, run, mask, True)
    loads += piece_copies((dctx_own, dctx_sib), pair * LANES, 1, ctx, 4, sems, run, mask, True)
    for copy in loads:
        copy.start()
    for copy in loads:
        copy.wait()

    @pl.loop(0, total // TILE)
    def _(block):
        rows = pl.multiple_of(block * TILE, TILE)
        product = ctx[0, pl.ds(rows, TILE), :].astype(jnp.float32) * ctx[1, pl.ds(rows, TILE), :].astype(jnp.float32)
        product = product.T
        for head in range(2):
            part = jnp.sum(product[head * HEAD_DIM : (head + 1) * HEAD_DIM], axis=0, keepdims=True)
            delta[head, :, pl.ds(rows, TILE)] = jnp.broadcast_to(part, (8, TILE))
        turned[:, pl.ds(rows, TILE)] = qkv[1, pl.ds(rows, TILE), :].astype(jnp.float32).T.astype(jnp.bfloat16)
        dq[:, pl.ds(rows, TILE)] = jnp.zeros((LANES, TILE), jnp.float32)

    @pl.loop(0, total // TILE)
    def _(block):
        rows = pl.multiple_of(block * TILE, TILE)
        k_heads = lane_halves(qkv[1, pl.ds(rows, TILE), :], 0.0)
        v_heads = lane_halves(qkv[2, pl.ds(rows, TILE), :], 0.0)
        segk = seg_col[pl.ds(rows, TILE), :]
        segk = jnp.concatenate([segk] * (TILE // LANES), axis=1)
        first, after = key_tiles(ends_ref, rows, rows + TILE - 1, TILE, total)
        dkv[...] = jnp.zeros_like(dkv)

        first, steps = spans(first, after, QUERY_TILES, total // TILE)

        @pl.loop(0, steps)
        def _(step):
            at = pl.multiple_of((first + step * QUERY_TILES) * TILE, TILE)
            span = pl.ds(at, QUERY_TILES * TILE)
            queries = qkv[0, span, :]
            grads = ctx[1, span, :]
            q_heads = lane_halves(queries, 0.0)
            g_heads = lane_halves(grads, 0.0)
            same = jnp.concatenate([segk] * QUERY_TILES, axis=1) == seg_row[:, span]
            for head in range(2):
                scores = mm(k_heads[head], queries, NT)
                probs = jnp.exp(jnp.where(same, scores - lse_ref[2 * pair + head, 0:1, span], NEG))
                dprobs = mm(v_heads[head], grads, NT)
                dscores = (probs * (dprobs - delta[head, 0:1, span])).astype(jnp.bfloat16)
                dkv[1] += mm(probs.astype(jnp.bfloat16), g_heads[head], NN)
                dkv[0] += mm(dscores, q_heads[head], NN)
                lanes = slice(head * HEAD_DIM, (head + 1) * HEAD_DIM)
                dq[lanes, span] += mm(turned[lanes, pl.ds(rows, TILE)], dscores, NN)

        out[1, pl.ds(rows, TILE), :] = dkv[0].astype(jnp.bfloat16)
        out[2, pl.ds(rows, TILE), :] = dkv[1].astype(jnp.bfloat16)

    @pl.loop(0, total // TILE)
    def _(block):
        rows = pl.multiple_of(block * TILE, TILE)
        out[0, pl.ds(rows, TILE), :] = (dq[:, pl.ds(rows, TILE)].T * HEAD_DIM**-0.5).astype(jnp.bfloat16)

    for copy in stores:
        copy.start()
    for copy in stores:
        copy.wait()


def attend_backward(pair, mask, ends, own, sib, ctx_own, ctx_sib, dctx_own, dctx_sib, seg_col, seg_row, lse, run):
    half = own.shape[0]
    total = 2 * half
    pieces = total // run
    any_spec = pl.BlockSpec(memory_space=pl.ANY)
    vmem = pl.BlockSpec(memory_space=pltpu.VMEM)
    smem = pl.BlockSpec(memory_space=pltpu.SMEM)
    return pl.pallas_call(
        functools.partial(backward_kernel, run, pair),
        out_shape=(
            jax.ShapeDtypeStruct((half, 3 * LANES), jnp.bfloat16),
            jax.ShapeDtypeStruct((half, 3 * LANES), jnp.bfloat16),
        ),
        in_specs=[smem, smem] + [any_spec] * 6 + [vmem] * 3,
        out_specs=(any_spec, any_spec),
        scratch_shapes=[
            pltpu.VMEM((3, total, LANES), jnp.bfloat16),
            pltpu.VMEM((2, total, LANES), jnp.bfloat16),
            pltpu.VMEM((3, total, LANES), jnp.bfloat16),
            pltpu.VMEM((LANES, total), jnp.bfloat16),
            pltpu.VMEM((2, 8, total), jnp.float32),
            pltpu.VMEM((LANES, total), jnp.float32),
            pltpu.VMEM((2, TILE, LANES), jnp.float32),
            pltpu.SemaphoreType.DMA((5, pieces)),
            pltpu.SemaphoreType.DMA((3, pieces)),
        ],
        compiler_params=pltpu.CompilerParams(vmem_limit_bytes=24 << 20),
        cost_estimate=pl.CostEstimate(flops=20_000_000_000, bytes_accessed=8_000_000, transcendentals=0),
        name=f"attend_backward_{pair}",
    )(mask, ends, own, sib, ctx_own, ctx_sib, dctx_own, dctx_sib, seg_col, seg_row, lse)


EPS = 1e-05


def norm_forward(resid, gain, shift):
    mean = jnp.mean(resid, axis=-1, keepdims=True)
    centered = resid - mean
    inv = lax.rsqrt(jnp.mean(centered * centered, axis=-1, keepdims=True) + EPS)
    normed = centered * inv
    return (normed * gain + shift, normed, inv)


def norm_backward(grad, normed, inv, gain):
    scaled = grad * gain
    return inv * (
        scaled
        - jnp.mean(scaled, axis=-1, keepdims=True)
        - normed * jnp.mean(scaled * normed, axis=-1, keepdims=True)
    )


def gelu_slope(pre):
    cdf = 0.5 * (1.0 + lax.erf(pre * (1.0 / math.sqrt(2.0))))
    density = jnp.exp(-0.5 * pre * pre) * (1.0 / math.sqrt(2.0 * math.pi))
    return cdf + pre * density


def doc_ids(ends, count):
    places = jnp.arange(count, dtype=jnp.int32)
    return jnp.sum((places[:, None] >= ends[None, :]).astype(jnp.int32), axis=1)


CORES = 2


def routes(nseq):
    first, second = [], []
    for core in range(CORES):
        for z in range(nseq):
            source = core * nseq + z
            first.append((source, (z // 2) * nseq + 2 * core + z % 2))
            second.append((source, (z // 2) * nseq + 2 * core + 1 - z % 2))
    return first, second


def swap(x):
    return lax.ppermute(x, "core", [(0, 1), (1, 0)])


def after(value, *done):
    return lax.optimization_barrier((value, done))[0]


def pick(value, which, axis=0):
    return lax.dynamic_index_in_dim(value, which, axis, keepdims=False)


def total(keep, received):
    return (keep.astype(jnp.float32) + received.astype(jnp.float32)).astype(jnp.bfloat16)


class Halving:
    def __init__(self, blocks, planes):
        bits = planes.bit_length() - 1
        rows = blocks.shape[1]
        self.planes = planes
        self.orders = (list(range(bits)), list(range(bits))[::-1])
        self.left = [list(range(bits))[::-1] for _ in range(2)]
        parts = (blocks[:, : rows // 2], blocks[:, rows // 2 :])
        self.parts = [p.reshape((2,) * bits + p.shape[1:]) for p in parts]
        self.steps = bits

    def send(self, step):
        place = lax.axis_index("xy")
        self.keep, self.received, self.sent = [], [], []
        for half in range(2):
            bit = self.orders[half][step]
            axis = self.left[half].index(bit)
            mine = (place >> bit) % 2
            self.left[half].remove(bit)
            out = pick(self.parts[half], 1 - mine, axis)
            self.keep.append(pick(self.parts[half], mine, axis))
            self.sent.append(out)
            self.received.append(lax.ppermute(out, "xy", [(i, i ^ (1 << bit)) for i in range(self.planes)]))

    def add(self, *done):
        self.parts = [total(k, after(r, *done)) for k, r in zip(self.keep, self.received)]

    def result(self):
        return jnp.concatenate(self.parts)


class Spread:
    def __init__(self, value, nseq):
        self.nseq, self.rows = nseq, value.shape[0] // nseq
        self.me = lax.axis_index("seq")
        quarter = lambda which: lax.dynamic_slice_in_dim(value, (which % nseq) * self.rows, self.rows, 0)
        self.keep = quarter(self.me)
        self.sent = [quarter(self.me + d) for d in range(1, nseq)]
        self.received = [self.shift(q, d) for d, q in enumerate(self.sent, 1)]

    def shift(self, value, distance):
        return lax.ppermute(value, "seq", [(i, (i + distance) % self.nseq) for i in range(self.nseq)])

    def add(self, *done):
        parts = [self.keep] + [after(r, *done) for r in self.received]
        self.keep = sum(p.astype(jnp.float32) for p in parts).astype(jnp.bfloat16)
        self.received = [self.shift(self.keep, d) for d in range(1, self.nseq)]

    def result(self):
        whole = jnp.zeros((self.nseq * self.rows,) + self.keep.shape[1:], jnp.bfloat16)
        for d, part in enumerate([self.keep] + self.received):
            start = ((self.me - d) % self.nseq) * self.rows
            whole = lax.dynamic_update_slice_in_dim(whole, part, start, 0)
        return whole


def either(core, own, other, axis):
    return jnp.where(core == 0, jnp.concatenate([own, other], axis), jnp.concatenate([other, own], axis))


def per_device(
    tokens, doc_lengths, qkv_weight, q_bias, v_bias, out_weight, out_bias, norm1_gain, norm1_bias,
    ff_in_weight, ff_in_bias, ff_out_weight, ff_out_bias, norm2_gain, norm2_bias, out_cotangent,
):
    bf16, f32 = jnp.bfloat16, jnp.float32
    fsdp = ("xy", "core")
    nseq = lax.axis_size("seq")
    planes = lax.axis_size("xy")
    shards = planes * CORES
    core = lax.axis_index("core")
    odd = lax.axis_index("seq") % 2
    micro, run, width = tokens.shape[1:]
    assert micro == 2 and nseq == 4
    stretch = run * nseq
    mine = width // CORES
    rows = width // shards
    first, second = routes(nseq)
    back = [[(b, a) for a, b in route] for route in (first, second)]

    def spread(x):
        halves = [lax.dynamic_index_in_dim(x[0], which, 0, keepdims=False) for which in (odd, 1 - odd)]
        return [lax.ppermute(h, ("core", "seq"), r) for h, r in zip(halves, (first, second))]

    def collect(x):
        got = [lax.ppermute(x[i * run : (i + 1) * run], ("core", "seq"), back[i]) for i in range(2)]
        return jnp.where(odd == 0, jnp.stack(got), jnp.stack(got[::-1]))[None]

    pieces = spread(tokens)
    lengths = jnp.stack([doc_lengths[0], swap(doc_lengths[0])])
    z = lax.axis_index("seq")
    theirs = jnp.where(z // 2 == core, lengths[0], lengths[1])
    ends = jnp.cumsum(lax.dynamic_index_in_dim(theirs, odd, 0, keepdims=False)).astype(jnp.int32)
    seg = doc_ids(ends, stretch)
    seg_col = jnp.broadcast_to(seg[:, None], (stretch, LANES))
    seg_row = seg[None]
    mask = (odd + 2 * core).astype(jnp.int32)[None]

    pairs = mine // LANES
    own_columns = qkv_weight.reshape(rows, 3, CORES, pairs, LANES)
    own_columns = jnp.moveaxis(own_columns, (2, 3), (0, 2)).reshape(CORES, rows, 3 * mine)
    kept = pick(own_columns, core)
    w_mine = either(core, kept, swap(pick(own_columns, 1 - core)), 0)
    w_mine = lax.all_gather(w_mine, "xy", axis=0, tiled=True)
    small = [q_bias, v_bias, out_bias, norm1_gain, norm1_bias, ff_out_bias, norm2_gain, norm2_bias, ff_in_bias]
    vectors = lax.all_gather(jnp.concatenate(small)[None, None], fsdp, axis=0, tiled=True)[:, 0].astype(f32)
    bias_q, bias_v, bias_out, gain_one, shift_one, bias_down, gain_two, shift_two = [
        vectors[:, i * rows : (i + 1) * rows].reshape(width) for i in range(8)
    ]
    bias_in = vectors[:, 8 * rows :].reshape(-1)
    w_out = lax.all_gather(out_weight, fsdp, axis=0, tiled=True)
    w_in = lax.all_gather(ff_in_weight, fsdp, axis=0, tiled=True)
    w_down = lax.all_gather(ff_out_weight, fsdp, axis=0, tiled=True)

    own_slice = lambda v: lax.dynamic_slice_in_dim(v, core * mine, mine, 0).reshape(pairs, LANES)
    one = jnp.ones((pairs, LANES), f32)
    bias_mine = jnp.stack([own_slice(bias_q), 0.0 * one, own_slice(bias_v)], axis=1).reshape(-1)
    scale = jnp.stack([HEAD_DIM**-0.5 * one, one, one], axis=1).reshape(-1)
    x_own = jnp.concatenate(pieces)
    x_sib = jnp.concatenate([swap(p) for p in pieces])
    projected = [((mm(x, w_mine, NN) + bias_mine) * scale).astype(bf16) for x in (x_own, x_sib)]
    ctx_own, ctx_sib, lse = attend_forward(mask, ends, *projected, seg_col, seg_row, run)
    ctx_far = swap(ctx_sib)

    wo_own = lax.dynamic_slice_in_dim(w_out, core * mine, mine, 0)
    wo_far = lax.dynamic_slice_in_dim(w_out, (1 - core) * mine, mine, 0)
    attn = mm(ctx_own, wo_own, NN) + mm(ctx_far, wo_far, NN) + bias_out
    hidden, normed_one, inv_one = norm_forward(x_own.astype(f32) + attn, gain_one, shift_one)
    hidden_low = hidden.astype(bf16)
    pre = mm(hidden_low, w_in, NN) + bias_in
    act_low = jax.nn.gelu(pre, approximate=False).astype(bf16)
    resid_two = hidden + mm(act_low, w_down, NN) + bias_down
    result, normed_two, inv_two = norm_forward(resid_two, gain_two, shift_two)
    output = collect(result.astype(bf16))

    grad_out = jnp.concatenate(spread(out_cotangent)).astype(f32)
    gain_two_grad = jnp.sum(grad_out * normed_two, axis=0)
    shift_two_grad = jnp.sum(grad_out, axis=0)
    grad_two = norm_backward(grad_out, normed_two, inv_two, gain_two)
    grad_down = grad_two.astype(bf16)

    def cores(blocks):
        return pick(blocks, core, 1), swap(pick(blocks, 1 - core, 1))

    down_grad = cores(mm(act_low, grad_down, TN).astype(bf16).reshape(planes, CORES, -1, width))
    down_bias_grad = jnp.sum(grad_down.astype(f32), axis=0)
    grad_pre = (mm(grad_down, w_down, NT) * gelu_slope(pre)).astype(bf16)
    in_grad = cores(mm(hidden_low, grad_pre, TN).astype(bf16).reshape(planes, CORES, rows, -1))
    in_bias_grad = jnp.sum(grad_pre.astype(f32), axis=0)
    grad_hidden = grad_two + mm(grad_pre, w_in, NT)
    gain_one_grad = jnp.sum(grad_hidden * normed_one, axis=0)
    shift_one_grad = jnp.sum(grad_hidden, axis=0)
    grad_one = norm_backward(grad_hidden, normed_one, inv_one, gain_one)
    grad_attn = grad_one.astype(bf16)
    dctx_far = swap(mm(grad_attn, wo_far, NT).astype(bf16))
    dctx_own = mm(grad_attn, wo_own, NT).astype(bf16)
    out_bias_grad = jnp.sum(grad_attn.astype(f32), axis=0)
    out_grad = [mm(c, grad_attn, TN).astype(bf16) for c in (ctx_own, ctx_far)]
    out_grad = cores(either(core, *out_grad, 0).reshape(planes, CORES, rows, width))
    small = [out_bias_grad, gain_one_grad, shift_one_grad, down_bias_grad, gain_two_grad, shift_two_grad, in_bias_grad]
    vector = jnp.concatenate([v.reshape(shards, -1) for v in small], axis=1).astype(bf16)
    lines = -(-vector.shape[1] // width)
    vector = jnp.pad(vector, ((0, 0), (0, lines * width - vector.shape[1])))
    vector = jnp.pad(vector.reshape(shards, lines, width), ((0, 0), (0, 32 - lines), (0, 0)))
    vector = cores(vector.reshape(planes, CORES, 32, width))
    inner = in_grad[0].shape[2] // width
    joined = []
    for which in range(2):
        wide = in_grad[which]
        wide = [wide[:, :, i * width : (i + 1) * width] for i in range(inner)]
        joined.append(jnp.concatenate([down_grad[which]] + wide + [out_grad[which], vector[which]], axis=1))
    early = Halving(total(*joined), planes)
    early.send(0)
    progress = [early]

    def advance(*done):
        if len(progress) > 1:
            return []
        early.add(*done)
        step = early.steps - len(early.left[0])
        if step < early.steps:
            early.send(step)
            return early.sent
        progress.append(Spread(early.result(), nseq))
        return progress[1].sent

    def attend(pair, *ready):
        held = after(mask, *ready)
        return attend_backward(
            pair, held, ends, *projected, ctx_own, ctx_sib, dctx_own, dctx_far, seg_col, seg_row, lse, run
        )

    def weight_sums(grads):
        near = jnp.concatenate([g[0] for g in grads], axis=1)
        far = jnp.concatenate([g[1] for g in grads], axis=1)
        matrix = (mm(x_own, near, TN) + mm(x_sib, far, TN)).astype(bf16)
        column = (jnp.sum(near.astype(f32), axis=0) + jnp.sum(far.astype(f32), axis=0)).astype(bf16)
        column = jnp.pad(column[None], ((0, 63), (0, 0)))
        column = jnp.broadcast_to(column, (planes,) + column.shape)
        return jnp.concatenate([matrix.reshape(planes, CORES * rows, -1), column], axis=1)

    grads = [attend(0, *early.sent)]
    for pair in range(1, pairs):
        sent = advance(grads[-1][0])
        if pair == pairs - 1:
            first_sums = Halving(weight_sums(grads), planes)
            first_sums.send(0)
            sent = sent + first_sums.sent
        grads.append(attend(pair, *sent))
    while len(progress) == 1:
        advance(grads[-1][0])
    early_sum = progress[1]

    near = jnp.concatenate([g[0] for g in grads], axis=1)
    far = jnp.concatenate([g[1] for g in grads], axis=1)
    grad_far = swap(mm(far, w_mine, NT).astype(bf16))
    early_sum.add(grads[-1][0])
    input_grad = (grad_one + mm(near, w_mine, NT) + grad_far.astype(f32)).astype(bf16)
    returned = [lax.ppermute(input_grad[i * run : (i + 1) * run], ("core", "seq"), back[i]) for i in range(2)]
    last_sums = Halving(after(weight_sums(grads[-1:]), input_grad), planes)
    last_sums.send(0)
    for step in range(last_sums.steps):
        for sums in (first_sums, last_sums):
            sums.add()
            if step + 1 < sums.steps:
                sums.send(step + 1)
    qkv_sum = Spread(jnp.concatenate([first_sums.result(), last_sums.result()], axis=1), nseq)
    qkv_sum.add(*returned)
    input_grad = jnp.where(odd == 0, jnp.stack(returned), jnp.stack(returned[::-1]))[None].astype(f32)
    early_total = early_sum.result()
    qkv_total = qkv_sum.result()

    down_rows = down_grad[0].shape[1]
    down_final = early_total[:down_rows].astype(f32)
    wide = [early_total[down_rows + i * rows : down_rows + (i + 1) * rows] for i in range(inner)]
    in_final = jnp.concatenate(wide, axis=1).astype(f32)
    at = down_rows + inner * rows
    out_final = early_total[at : at + rows].astype(f32)
    at = at + rows
    line = early_total[at : at + lines].reshape(-1).astype(f32)
    out_bias_final, g1, b1, down_bias_final, g2, b2 = [line[i * rows : (i + 1) * rows] for i in range(6)]
    in_bias_final = line[6 * rows : 6 * rows + ff_in_bias.shape[0]]

    part = qkv_total
    column = part[CORES * rows]
    other = swap(jnp.concatenate([lax.dynamic_slice_in_dim(part, (1 - core) * rows, rows, 0), part[CORES * rows : CORES * rows + 16]]))
    own_block = lax.dynamic_slice_in_dim(part, core * rows, rows, 0)
    spread_out = lambda v: jnp.moveaxis(v.reshape(-1, pairs, 3, LANES), 2, 1).reshape(-1, 3, 1, mine)
    qkv_final = either(core, spread_out(own_block), spread_out(other[:rows]), 2).reshape(rows, 3 * width).astype(f32)
    sums = either(core, spread_out(column), spread_out(other[rows]), 2).reshape(3, width)
    shard = lax.axis_index("xy") * CORES + core
    q_final = lax.dynamic_slice_in_dim(sums[0], shard * rows, rows, 0).astype(f32)
    v_final = lax.dynamic_slice_in_dim(sums[2], shard * rows, rows, 0).astype(f32)
    return (
        output, input_grad, qkv_final, q_final, v_final, out_final, out_bias_final, g1, b1, in_final,
        in_bias_final, down_final, down_bias_final, g2, b2,
    )


def solution(mesh):
    fsdp, nseq = mesh.shape["fsdp"], mesh.shape["seq"]
    fine = Mesh(mesh.devices.reshape(fsdp // CORES, CORES, nseq), ("xy", "core", "seq"))
    shard = ("xy", "core")
    stream, matrix, vector = P(shard, None, "seq", None), P(shard, None), P(shard)
    return jax.shard_map(
        per_device,
        mesh=fine,
        in_specs=(
            stream, P(shard, None, None), matrix, vector, vector, matrix, vector, vector, vector,
            matrix, vector, matrix, vector, vector, vector, stream,
        ),
        out_specs=(
            stream, stream, matrix, vector, vector, matrix, vector, vector, vector,
            matrix, vector, matrix, vector, vector, vector,
        ),
        check_vma=False,
    )
```

```python
import functools
import math

import jax
import jax.numpy as jnp
from jax import lax
from jax.experimental import pallas as pl
from jax.experimental.pallas import tpu as pltpu
from jax.sharding import Mesh
from jax.sharding import PartitionSpec as P

HEAD_DIM = 64
LANES = 128
NEG = -1e30
TILE = 256
VALUE_ROWS = HEAD_DIM + 16
KEY_TILES = 2
QUERY_TILES = 2
NT = (((1,), (1,)), ((), ()))
NN = (((1,), (0,)), ((), ()))
TN = (((0,), (0,)), ((), ()))


def mm(left, right, dims):
    return lax.dot_general(left, right, dims, preferred_element_type=jnp.float32)


def key_tiles(ends_ref, first, last, tile, total):
    low = jnp.int32(0)
    high = jnp.int32(total)
    for doc in reversed(range(ends_ref.shape[0])):
        end = ends_ref[doc]
        low = jnp.maximum(low, jnp.where(end <= first, end, 0))
        high = jnp.minimum(high, jnp.where(end > last, end, total))
    return low // tile, (high + tile - 1) // tile


def spans(first, after, count, tiles):
    steps = (after - first + count - 1) // count
    return jnp.minimum(first, tiles - steps * count), steps


def lane_halves(x, fill):
    lane = lax.broadcasted_iota(jnp.int32, x.shape, 1)
    fill = jnp.full_like(x, fill)
    return jnp.where(lane < HEAD_DIM, x, fill), jnp.where(lane < HEAD_DIM, fill, x)


def piece_copies(halves, columns, place, scratch, slot, sems, run, mask, inbound):
    copies = []
    pieces = halves[0].shape[0] // run
    for half, ref in enumerate(halves):
        for part in range(pieces):
            index = half * pieces + part
            natural = pl.multiple_of(jnp.bitwise_xor(mask, index) * run, run)
            outer = ref.at[pl.ds(part * run, run), pl.ds(columns, LANES)]
            inner = scratch.at[place, pl.ds(natural, run), :]
            ends = (outer, inner) if inbound else (inner, outer)
            copies.append(pltpu.make_async_copy(ends[0], ends[1], sems.at[slot, index]))
    return copies


def forward_kernel(run, mask_ref, ends_ref, own, sib, seg_col, seg_row, ctx_own, ctx_sib, lse_ref, qkv, out, turned, acc, top, sems, out_sems):
    total = qkv.shape[1]
    pairs = out.shape[0]
    mask = mask_ref[0]

    def loads(pair):
        copies = []
        for kind in range(3):
            copies += piece_copies(
                (own, sib), (3 * pair + kind) * LANES, kind * pairs + pair, qkv, kind * pairs + pair, sems, run, mask, True
            )
        return copies

    for pair in range(pairs):
        for copy in loads(pair):
            copy.start()

    for head in range(2 * pairs):
        turned[head, HEAD_DIM:, :] = jnp.ones((VALUE_ROWS - HEAD_DIM, total), jnp.bfloat16)
    for pair in range(pairs):
        for copy in loads(pair):
            copy.wait()
    heads = [(pair, head) for pair in range(pairs) for head in range(2)]
    if True:

        @pl.loop(0, total // TILE)
        def _(block):
            rows = pl.multiple_of(block * TILE, TILE)
            for pair in range(pairs):
                values = qkv[2 * pairs + pair, pl.ds(rows, TILE), :].astype(jnp.float32).T.astype(jnp.bfloat16)
                for head in range(2):
                    turned[2 * pair + head, :HEAD_DIM, pl.ds(rows, TILE)] = values[head * HEAD_DIM : (head + 1) * HEAD_DIM]

        @pl.loop(0, total // TILE)
        def _(block):
            rows = pl.multiple_of(block * TILE, TILE)
            q_heads = sum([list(lane_halves(qkv[pair, pl.ds(rows, TILE), :], 0.0)) for pair in range(pairs)], [])
            segq = seg_row[:, pl.ds(rows, TILE)]
            first, after = key_tiles(ends_ref, rows, rows + TILE - 1, TILE, total)
            acc[...] = jnp.zeros_like(acc)
            top[...] = jnp.full_like(top, NEG)

            first, steps = spans(first, after, KEY_TILES, total // TILE)

            @pl.loop(0, steps)
            def _(step):
                at = pl.multiple_of((first + step * KEY_TILES) * TILE, TILE)
                keys = [qkv[pairs + pair, pl.ds(at, KEY_TILES * TILE), :] for pair in range(pairs)]
                segk = seg_col[pl.ds(at, KEY_TILES * TILE), :]
                same = jnp.concatenate([segk] * (TILE // LANES), axis=1) == segq
                for head in range(2 * pairs):
                    scores = jnp.where(same, mm(keys[head // 2], q_heads[head], NT), NEG)
                    old = top[head, 0:1]
                    new = jnp.maximum(old, jnp.max(scores, axis=0, keepdims=True))
                    probs = jnp.exp(scores - new).astype(jnp.bfloat16)
                    acc[head] = acc[head] * jnp.exp(old - new) + mm(turned[head, :, pl.ds(at, KEY_TILES * TILE)], probs, NN)
                    top[head] = jnp.broadcast_to(new, (8, TILE))

            for pair in range(pairs):
                parts = []
                for head in (2 * pair, 2 * pair + 1):
                    weight = acc[head, HEAD_DIM : HEAD_DIM + 1]
                    parts.append(acc[head, :HEAD_DIM] / weight)
                    lse_ref[head, :, pl.ds(rows, TILE)] = top[head] + jnp.log(acc[head, HEAD_DIM : HEAD_DIM + 8])
                out[pair, pl.ds(rows, TILE), :] = jnp.concatenate(parts, axis=0).T.astype(jnp.bfloat16)

    for pair in range(pairs):
        for copy in piece_copies((ctx_own, ctx_sib), pair * LANES, pair, out, pair, out_sems, run, mask, False):
            copy.start()
    for pair in range(pairs):
        for copy in piece_copies((ctx_own, ctx_sib), pair * LANES, pair, out, pair, out_sems, run, mask, False):
            copy.wait()


def attend_forward(mask, ends, own, sib, seg_col, seg_row, run):
    half, columns = own.shape
    total = 2 * half
    pairs = columns // (3 * LANES)
    pieces = total // run
    any_spec = pl.BlockSpec(memory_space=pl.ANY)
    vmem = pl.BlockSpec(memory_space=pltpu.VMEM)
    smem = pl.BlockSpec(memory_space=pltpu.SMEM)
    return pl.pallas_call(
        functools.partial(forward_kernel, run),
        out_shape=(
            jax.ShapeDtypeStruct((half, pairs * LANES), jnp.bfloat16),
            jax.ShapeDtypeStruct((half, pairs * LANES), jnp.bfloat16),
            jax.ShapeDtypeStruct((2 * pairs, 8, total), jnp.float32),
        ),
        in_specs=[smem, smem, any_spec, any_spec, vmem, vmem],
        out_specs=(any_spec, any_spec, vmem),
        scratch_shapes=[
            pltpu.VMEM((3 * pairs, total, LANES), jnp.bfloat16),
            pltpu.VMEM((pairs, total, LANES), jnp.bfloat16),
            pltpu.VMEM((2 * pairs, VALUE_ROWS, total), jnp.bfloat16),
            pltpu.VMEM((2 * pairs, VALUE_ROWS, TILE), jnp.float32),
            pltpu.VMEM((2 * pairs, 8, TILE), jnp.float32),
            pltpu.SemaphoreType.DMA((3 * pairs, pieces)),
            pltpu.SemaphoreType.DMA((pairs, pieces)),
        ],
        compiler_params=pltpu.CompilerParams(vmem_limit_bytes=40 << 20),
        cost_estimate=pl.CostEstimate(flops=1_000_000_000, bytes_accessed=1_000_000, transcendentals=0),
        name="attend_forward",
    )(mask, ends, own, sib, seg_col, seg_row)


def backward_kernel(
    run, pair, mask_ref, ends_ref, own, sib, ctx_own, ctx_sib, dctx_own, dctx_sib, seg_col, seg_row, lse_ref,
    d_own, d_sib, qkv, ctx, out, turned, delta, dq, dkv, sems, out_sems
):
    total = qkv.shape[1]
    mask = mask_ref[0]
    loads, stores = [], []
    for kind in range(3):
        loads += piece_copies((own, sib), (3 * pair + kind) * LANES, kind, qkv, kind, sems, run, mask, True)
        stores += piece_copies((d_own, d_sib), kind * LANES, kind, out, kind, out_sems, run, mask, False)
    loads += piece_copies((ctx_own, ctx_sib), pair * LANES, 0, ctx, 3, sems, run, mask, True)
    loads += piece_copies((dctx_own, dctx_sib), pair * LANES, 1, ctx, 4, sems, run, mask, True)
    for copy in loads:
        copy.start()
    for copy in loads:
        copy.wait()

    @pl.loop(0, total // TILE)
    def _(block):
        rows = pl.multiple_of(block * TILE, TILE)
        product = ctx[0, pl.ds(rows, TILE), :].astype(jnp.float32) * ctx[1, pl.ds(rows, TILE), :].astype(jnp.float32)
        product = product.T
        for head in range(2):
            part = jnp.sum(product[head * HEAD_DIM : (head + 1) * HEAD_DIM], axis=0, keepdims=True)
            delta[head, :, pl.ds(rows, TILE)] = jnp.broadcast_to(part, (8, TILE))
        turned[:, pl.ds(rows, TILE)] = qkv[1, pl.ds(rows, TILE), :].astype(jnp.float32).T.astype(jnp.bfloat16)
        dq[:, pl.ds(rows, TILE)] = jnp.zeros((LANES, TILE), jnp.float32)

    @pl.loop(0, total // TILE)
    def _(block):
        rows = pl.multiple_of(block * TILE, TILE)
        k_heads = lane_halves(qkv[1, pl.ds(rows, TILE), :], 0.0)
        v_heads = lane_halves(qkv[2, pl.ds(rows, TILE), :], 0.0)
        segk = seg_col[pl.ds(rows, TILE), :]
        segk = jnp.concatenate([segk] * (TILE // LANES), axis=1)
        first, after = key_tiles(ends_ref, rows, rows + TILE - 1, TILE, total)
        dkv[...] = jnp.zeros_like(dkv)

        first, steps = spans(first, after, QUERY_TILES, total // TILE)

        @pl.loop(0, steps)
        def _(step):
            at = pl.multiple_of((first + step * QUERY_TILES) * TILE, TILE)
            span = pl.ds(at, QUERY_TILES * TILE)
            queries = qkv[0, span, :]
            grads = ctx[1, span, :]
            q_heads = lane_halves(queries, 0.0)
            g_heads = lane_halves(grads, 0.0)
            same = jnp.concatenate([segk] * QUERY_TILES, axis=1) == seg_row[:, span]
            for head in range(2):
                scores = mm(k_heads[head], queries, NT)
                probs = jnp.exp(jnp.where(same, scores - lse_ref[2 * pair + head, 0:1, span], NEG))
                dprobs = mm(v_heads[head], grads, NT)
                dscores = (probs * (dprobs - delta[head, 0:1, span])).astype(jnp.bfloat16)
                dkv[1] += mm(probs.astype(jnp.bfloat16), g_heads[head], NN)
                dkv[0] += mm(dscores, q_heads[head], NN)
                lanes = slice(head * HEAD_DIM, (head + 1) * HEAD_DIM)
                dq[lanes, span] += mm(turned[lanes, pl.ds(rows, TILE)], dscores, NN)

        out[1, pl.ds(rows, TILE), :] = dkv[0].astype(jnp.bfloat16)
        out[2, pl.ds(rows, TILE), :] = dkv[1].astype(jnp.bfloat16)

    @pl.loop(0, total // TILE)
    def _(block):
        rows = pl.multiple_of(block * TILE, TILE)
        out[0, pl.ds(rows, TILE), :] = (dq[:, pl.ds(rows, TILE)].T * HEAD_DIM**-0.5).astype(jnp.bfloat16)

    for copy in stores:
        copy.start()
    for copy in stores:
        copy.wait()


def attend_backward(pair, mask, ends, own, sib, ctx_own, ctx_sib, dctx_own, dctx_sib, seg_col, seg_row, lse, run):
    half = own.shape[0]
    total = 2 * half
    pieces = total // run
    any_spec = pl.BlockSpec(memory_space=pl.ANY)
    vmem = pl.BlockSpec(memory_space=pltpu.VMEM)
    smem = pl.BlockSpec(memory_space=pltpu.SMEM)
    return pl.pallas_call(
        functools.partial(backward_kernel, run, pair),
        out_shape=(
            jax.ShapeDtypeStruct((half, 3 * LANES), jnp.bfloat16),
            jax.ShapeDtypeStruct((half, 3 * LANES), jnp.bfloat16),
        ),
        in_specs=[smem, smem] + [any_spec] * 6 + [vmem] * 3,
        out_specs=(any_spec, any_spec),
        scratch_shapes=[
            pltpu.VMEM((3, total, LANES), jnp.bfloat16),
            pltpu.VMEM((2, total, LANES), jnp.bfloat16),
            pltpu.VMEM((3, total, LANES), jnp.bfloat16),
            pltpu.VMEM((LANES, total), jnp.bfloat16),
            pltpu.VMEM((2, 8, total), jnp.float32),
            pltpu.VMEM((LANES, total), jnp.float32),
            pltpu.VMEM((2, TILE, LANES), jnp.float32),
            pltpu.SemaphoreType.DMA((5, pieces)),
            pltpu.SemaphoreType.DMA((3, pieces)),
        ],
        compiler_params=pltpu.CompilerParams(vmem_limit_bytes=24 << 20),
        cost_estimate=pl.CostEstimate(flops=1_000_000_000, bytes_accessed=1_000_000, transcendentals=0),
        name=f"attend_backward_{pair}",
    )(mask, ends, own, sib, ctx_own, ctx_sib, dctx_own, dctx_sib, seg_col, seg_row, lse)


EPS = 1e-05


def norm_forward(resid, gain, shift):
    mean = jnp.mean(resid, axis=-1, keepdims=True)
    centered = resid - mean
    inv = lax.rsqrt(jnp.mean(centered * centered, axis=-1, keepdims=True) + EPS)
    normed = centered * inv
    return (normed * gain + shift, normed, inv)


def norm_backward(grad, normed, inv, gain):
    scaled = grad * gain
    return inv * (
        scaled
        - jnp.mean(scaled, axis=-1, keepdims=True)
        - normed * jnp.mean(scaled * normed, axis=-1, keepdims=True)
    )


ROWS = 256
CHUNK = 768


def fold(x):
    return jnp.sum(x.reshape(-1, 8, x.shape[1]), axis=0)


def middle_kernel(
    core_ref, x_ref, near_ref, far_ref, cot_ref, vec_ref, in_bias_ref, w_out, w_in, w_down,
    result_ref, low_ref, act_ref, grad_down_ref, grad_pre_ref, grad_one_ref, grad_attn_ref, dnear_ref, dfar_ref,
    sums_ref, in_sums_ref, wo, wi, wd, slope, acc, sums, in_sums, sems
):
    f32, bf16 = jnp.float32, jnp.bfloat16
    mine = near_ref.shape[1]
    chunks = w_in.shape[1] // CHUNK
    step = pl.program_id(0)
    core = core_ref[0]
    copies = []
    for place in range(2):
        which = core if place == 0 else 1 - core
        rows = pl.multiple_of(which * mine, mine)
        copies.append(pltpu.make_async_copy(w_out.at[pl.ds(rows, mine), :], wo.at[pl.ds(place * mine, mine), :], sems.at[place]))
    for chunk in range(chunks):
        columns = pl.ds(chunk * CHUNK, CHUNK)
        copies.append(pltpu.make_async_copy(w_in.at[:, columns], wi.at[chunk], sems.at[2 + chunk]))
    for chunk in range(chunks):
        columns = pl.ds(chunk * CHUNK, CHUNK)
        copies.append(pltpu.make_async_copy(w_down.at[columns, :], wd.at[chunk], sems.at[2 + chunks + chunk]))

    @pl.when(step == 0)
    def _():
        for copy in copies:
            copy.start()
        sums[...] = jnp.zeros_like(sums)
        in_sums[...] = jnp.zeros_like(in_sums)
        for copy in copies[:2]:
            copy.wait()

    bias_out, gain_one, shift_one, bias_down, gain_two, shift_two = [vec_ref[i : i + 1, :] for i in range(6)]
    near, far = near_ref[...], far_ref[...]
    attn = mm(near, wo[:mine], NN) + mm(far, wo[mine:], NN) + bias_out
    hidden, normed_one, inv_one = norm_forward(x_ref[...].astype(f32) + attn, gain_one, shift_one)
    low_ref[...] = hidden.astype(bf16)
    acc[...] = hidden + bias_down

    @pl.when(step == 0)
    def _():
        for copy in copies[2:]:
            copy.wait()

    @pl.loop(0, chunks)
    def _(chunk):
        columns = pl.ds(pl.multiple_of(chunk * CHUNK, CHUNK), CHUNK)
        pre = mm(low_ref[...], wi[chunk], NN) + in_bias_ref[:, columns]
        cdf = 0.5 * (1.0 + lax.erf(pre * (1.0 / math.sqrt(2.0))))
        density = jnp.exp(-0.5 * pre * pre) * (1.0 / math.sqrt(2.0 * math.pi))
        act = (pre * cdf).astype(bf16)
        act_ref[:, columns] = act
        slope[:, columns] = cdf + pre * density
        acc[...] += mm(act, wd[chunk], NN)

    result, normed_two, inv_two = norm_forward(acc[...], gain_two, shift_two)
    result_ref[...] = result.astype(bf16)
    dy = cot_ref[...].astype(f32)
    grad_two = norm_backward(dy, normed_two, inv_two, gain_two)
    grad_down = grad_two.astype(bf16)
    grad_down_ref[...] = grad_down
    sums[3] += fold(grad_down.astype(f32))
    sums[4] += fold(dy * normed_two)
    sums[5] += fold(dy)
    acc[...] = grad_two

    @pl.loop(0, chunks)
    def _(chunk):
        columns = pl.ds(pl.multiple_of(chunk * CHUNK, CHUNK), CHUNK)
        grad_pre = (mm(grad_down_ref[...], wd[chunk], NT) * slope[:, columns]).astype(bf16)
        grad_pre_ref[:, columns] = grad_pre
        in_sums[:, columns] += fold(grad_pre.astype(f32))
        acc[...] += mm(grad_pre, wi[chunk], NT)

    grad_hidden = acc[...]
    sums[1] += fold(grad_hidden * normed_one)
    sums[2] += fold(grad_hidden)
    grad_one = norm_backward(grad_hidden, normed_one, inv_one, gain_one)
    grad_one_ref[...] = grad_one
    grad_attn = grad_one.astype(bf16)
    grad_attn_ref[...] = grad_attn
    sums[0] += fold(grad_attn.astype(f32))
    dnear_ref[...] = mm(grad_attn, wo[:mine], NT).astype(bf16)
    dfar_ref[...] = mm(grad_attn, wo[mine:], NT).astype(bf16)

    @pl.when(step == pl.num_programs(0) - 1)
    def _():
        sums_ref[...] = jnp.zeros_like(sums_ref)
        for i in range(6):
            sums_ref[i : i + 1, :] = jnp.sum(sums[i], axis=0, keepdims=True)
        in_sums_ref[...] = jnp.sum(in_sums[...], axis=0, keepdims=True)


def middle(core, x, near, far, cot, vec, in_bias, w_out, w_in, w_down):
    count, width = x.shape
    hidden = w_in.shape[1]
    mine = near.shape[1]
    chunks = hidden // CHUNK
    f32, bf16 = jnp.float32, jnp.bfloat16
    any_spec = pl.BlockSpec(memory_space=pl.ANY)
    block = lambda columns: pl.BlockSpec((ROWS, columns), lambda i: (i, 0))
    whole = lambda rows, columns: pl.BlockSpec((rows, columns), lambda i: (0, 0))
    shape = jax.ShapeDtypeStruct
    return pl.pallas_call(
        middle_kernel,
        grid=(count // ROWS,),
        out_shape=(
            shape((count, width), bf16), shape((count, width), bf16), shape((count, hidden), bf16),
            shape((count, width), bf16), shape((count, hidden), bf16), shape((count, width), f32),
            shape((count, width), bf16), shape((count, mine), bf16), shape((count, mine), bf16),
            shape((8, width), f32), shape((1, hidden), f32),
        ),
        in_specs=[
            pl.BlockSpec(memory_space=pltpu.SMEM), block(width), block(mine), block(mine), block(width),
            whole(8, width), whole(1, hidden), any_spec, any_spec, any_spec,
        ],
        out_specs=(
            block(width), block(width), block(hidden), block(width), block(hidden), block(width), block(width),
            block(mine), block(mine), whole(8, width), whole(1, hidden),
        ),
        scratch_shapes=[
            pltpu.VMEM((width, width), bf16),
            pltpu.VMEM((chunks, width, CHUNK), bf16),
            pltpu.VMEM((chunks, CHUNK, width), bf16),
            pltpu.VMEM((ROWS, hidden), f32),
            pltpu.VMEM((ROWS, width), f32),
            pltpu.VMEM((6, 8, width), f32),
            pltpu.VMEM((8, hidden), f32),
            pltpu.SemaphoreType.DMA((2 + 2 * chunks,)),
        ],
        compiler_params=pltpu.CompilerParams(vmem_limit_bytes=48 << 20),
        cost_estimate=pl.CostEstimate(flops=20_000_000_000, bytes_accessed=30_000_000, transcendentals=0),
        name="middle",
    )(core, x, near, far, cot, vec, in_bias, w_out, w_in, w_down)


def doc_ids(ends, count):
    places = jnp.arange(count, dtype=jnp.int32)
    return jnp.sum((places[:, None] >= ends[None, :]).astype(jnp.int32), axis=1)


CORES = 2


def routes(nseq):
    first, second = [], []
    for core in range(CORES):
        for z in range(nseq):
            source = core * nseq + z
            first.append((source, (z // 2) * nseq + 2 * core + z % 2))
            second.append((source, (z // 2) * nseq + 2 * core + 1 - z % 2))
    return first, second


def swap(x):
    return lax.ppermute(x, "core", [(0, 1), (1, 0)])


def after(value, *done):
    return lax.optimization_barrier((value, done))[0]


def pick(value, which, axis=0):
    return lax.dynamic_index_in_dim(value, which, axis, keepdims=False)


def total(keep, received):
    return (keep.astype(jnp.float32) + received.astype(jnp.float32)).astype(jnp.bfloat16)


class Halving:
    def __init__(self, blocks, planes):
        bits = planes.bit_length() - 1
        rows = blocks.shape[1]
        self.planes = planes
        self.orders = (list(range(bits)), list(range(bits))[::-1])
        self.left = [list(range(bits))[::-1] for _ in range(2)]
        parts = (blocks[:, : rows // 2], blocks[:, rows // 2 :])
        self.parts = [p.reshape((2,) * bits + p.shape[1:]) for p in parts]
        self.steps = bits

    def send(self, step):
        place = lax.axis_index("xy")
        self.keep, self.received, self.sent = [], [], []
        for half in range(2):
            bit = self.orders[half][step]
            axis = self.left[half].index(bit)
            mine = (place >> bit) % 2
            self.left[half].remove(bit)
            out = pick(self.parts[half], 1 - mine, axis)
            self.keep.append(pick(self.parts[half], mine, axis))
            self.sent.append(out)
            self.received.append(lax.ppermute(out, "xy", [(i, i ^ (1 << bit)) for i in range(self.planes)]))

    def add(self, *done):
        self.parts = [total(k, after(r, *done)) for k, r in zip(self.keep, self.received)]

    def result(self):
        return jnp.concatenate(self.parts)


class Spread:
    def __init__(self, value, nseq):
        self.nseq, self.rows = nseq, value.shape[0] // nseq
        self.me = lax.axis_index("seq")
        quarter = lambda which: lax.dynamic_slice_in_dim(value, (which % nseq) * self.rows, self.rows, 0)
        self.keep = quarter(self.me)
        self.sent = [quarter(self.me + d) for d in range(1, nseq)]
        self.received = [self.shift(q, d) for d, q in enumerate(self.sent, 1)]

    def shift(self, value, distance):
        return lax.ppermute(value, "seq", [(i, (i + distance) % self.nseq) for i in range(self.nseq)])

    def add(self, *done):
        parts = [self.keep] + [after(r, *done) for r in self.received]
        self.keep = sum(p.astype(jnp.float32) for p in parts).astype(jnp.bfloat16)
        self.received = [self.shift(self.keep, d) for d in range(1, self.nseq)]

    def result(self):
        whole = jnp.zeros((self.nseq * self.rows,) + self.keep.shape[1:], jnp.bfloat16)
        for d, part in enumerate([self.keep] + self.received):
            start = ((self.me - d) % self.nseq) * self.rows
            whole = lax.dynamic_update_slice_in_dim(whole, part, start, 0)
        return whole


def either(core, own, other, axis):
    return jnp.where(core == 0, jnp.concatenate([own, other], axis), jnp.concatenate([other, own], axis))


def per_device(
    tokens, doc_lengths, qkv_weight, q_bias, v_bias, out_weight, out_bias, norm1_gain, norm1_bias,
    ff_in_weight, ff_in_bias, ff_out_weight, ff_out_bias, norm2_gain, norm2_bias, out_cotangent,
):
    bf16, f32 = jnp.bfloat16, jnp.float32
    fsdp = ("xy", "core")
    nseq = lax.axis_size("seq")
    planes = lax.axis_size("xy")
    shards = planes * CORES
    core = lax.axis_index("core")
    odd = lax.axis_index("seq") % 2
    micro, run, width = tokens.shape[1:]
    assert micro == 2 and nseq == 4
    stretch = run * nseq
    mine = width // CORES
    rows = width // shards
    first, second = routes(nseq)
    back = [[(b, a) for a, b in route] for route in (first, second)]

    def spread(x):
        halves = [lax.dynamic_index_in_dim(x[0], which, 0, keepdims=False) for which in (odd, 1 - odd)]
        return [lax.ppermute(h, ("core", "seq"), r) for h, r in zip(halves, (first, second))]

    pieces = spread(tokens)
    lengths = jnp.stack([doc_lengths[0], swap(doc_lengths[0])])
    z = lax.axis_index("seq")
    theirs = jnp.where(z // 2 == core, lengths[0], lengths[1])
    ends = jnp.cumsum(lax.dynamic_index_in_dim(theirs, odd, 0, keepdims=False)).astype(jnp.int32)
    seg = doc_ids(ends, stretch)
    seg_col = jnp.broadcast_to(seg[:, None], (stretch, LANES))
    seg_row = seg[None]
    mask = (odd + 2 * core).astype(jnp.int32)[None]

    pairs = mine // LANES
    own_columns = qkv_weight.reshape(rows, 3, CORES, pairs, LANES)
    own_columns = jnp.moveaxis(own_columns, (2, 3), (0, 2)).reshape(CORES, rows, 3 * mine)
    kept = pick(own_columns, core)
    w_mine = either(core, kept, swap(pick(own_columns, 1 - core)), 0)
    w_mine = lax.all_gather(w_mine, "xy", axis=0, tiled=True)
    small = [q_bias, v_bias, out_bias, norm1_gain, norm1_bias, ff_out_bias, norm2_gain, norm2_bias]
    inner = ff_in_bias.shape[0] // rows
    small = jnp.concatenate([jnp.stack(small), ff_in_bias.reshape(inner, rows)])
    vectors = lax.all_gather(small, fsdp, axis=0, tiled=False).astype(f32)
    bias_in = vectors[:, 8:].reshape(1, -1)
    vectors = jnp.moveaxis(vectors[:, :8], 0, 1).reshape(8, width)
    bias_q, bias_v = vectors[0], vectors[1]
    norms = jnp.concatenate([vectors[2:], jnp.zeros((2, width), f32)])
    w_out = lax.all_gather(out_weight, fsdp, axis=0, tiled=True)
    w_in = lax.all_gather(ff_in_weight, fsdp, axis=0, tiled=True)
    w_down = lax.all_gather(ff_out_weight, fsdp, axis=0, tiled=True)

    own_slice = lambda v: lax.dynamic_slice_in_dim(v, core * mine, mine, 0).reshape(pairs, LANES)
    one = jnp.ones((pairs, LANES), f32)
    bias_mine = jnp.stack([own_slice(bias_q), 0.0 * one, own_slice(bias_v)], axis=1).reshape(-1)
    scale = jnp.stack([HEAD_DIM**-0.5 * one, one, one], axis=1).reshape(-1)
    x_own = after(jnp.concatenate(pieces), norms, bias_in)
    x_sib = jnp.concatenate([swap(p) for p in pieces])
    projected = [((mm(x, w_mine, NN) + bias_mine) * scale).astype(bf16) for x in (x_own, x_sib)]
    ctx_own, ctx_sib, lse = attend_forward(mask, ends, *projected, seg_col, seg_row, run)
    ctx_far = swap(ctx_sib)

    cot = jnp.concatenate(spread(out_cotangent))
    result, hidden_low, act_low, grad_down, grad_pre, grad_one, grad_attn, dctx_own, dctx_far, sums, in_sums = middle(
        core.astype(jnp.int32)[None], x_own, ctx_own, ctx_far, cot, norms, bias_in, w_out, w_in, w_down
    )
    dctx_far = swap(dctx_far)
    output = [lax.ppermute(result[i * run : (i + 1) * run], ("core", "seq"), back[i]) for i in range(2)]

    def cores(blocks):
        return pick(blocks, core, 1), swap(pick(blocks, 1 - core, 1))

    down_grad = cores(mm(act_low, grad_down, TN).astype(bf16).reshape(planes, CORES, -1, width))
    in_grad = cores(mm(hidden_low, grad_pre, TN).astype(bf16).reshape(planes, CORES, rows, -1))
    out_grad = [mm(c, grad_attn, TN).astype(bf16) for c in (ctx_own, ctx_far)]
    out_grad = cores(either(core, *out_grad, 0).reshape(planes, CORES, rows, width))
    vector = [jnp.moveaxis(sums[:6].reshape(6, shards, rows), 1, 0), in_sums.reshape(shards, inner, rows)]
    vector = jnp.concatenate(vector, axis=1).astype(bf16)
    vector = jnp.pad(vector, ((0, 0), (0, 32 - vector.shape[1]), (0, width - rows)))
    vector = cores(vector.reshape(planes, CORES, 32, width))
    inner_blocks = in_grad[0].shape[2] // width
    joined = []
    for which in range(2):
        wide = in_grad[which]
        wide = [wide[:, :, i * width : (i + 1) * width] for i in range(inner_blocks)]
        joined.append(jnp.concatenate([down_grad[which]] + wide + [out_grad[which], vector[which]], axis=1))
    early = Halving(total(*joined), planes)
    early.send(0)
    progress = [early]

    def advance(*done):
        if len(progress) > 1:
            return []
        early.add(*done)
        step = early.steps - len(early.left[0])
        if step < early.steps:
            early.send(step)
            return early.sent
        progress.append(Spread(early.result(), nseq))
        return progress[1].sent

    def attend(pair, *ready):
        held = after(mask, *ready)
        return attend_backward(
            pair, held, ends, *projected, ctx_own, ctx_sib, dctx_own, dctx_far, seg_col, seg_row, lse, run
        )

    def weight_sums(grads):
        near = jnp.concatenate([g[0] for g in grads], axis=1)
        far = jnp.concatenate([g[1] for g in grads], axis=1)
        matrix = (mm(x_own, near, TN) + mm(x_sib, far, TN)).astype(bf16)
        column = (jnp.sum(near.astype(f32), axis=0) + jnp.sum(far.astype(f32), axis=0)).astype(bf16)
        column = jnp.pad(column[None], ((0, 63), (0, 0)))
        column = jnp.broadcast_to(column, (planes,) + column.shape)
        return jnp.concatenate([matrix.reshape(planes, CORES * rows, -1), column], axis=1)

    grads = [attend(0, *early.sent)]
    for pair in range(1, pairs):
        sent = advance(grads[-1][0])
        if pair == pairs - 1:
            first_sums = Halving(weight_sums(grads), planes)
            first_sums.send(0)
            sent = sent + first_sums.sent
        grads.append(attend(pair, *sent, *(output if pair == 1 else ())))
    while len(progress) == 1:
        advance(grads[-1][0])
    early_sum = progress[1]

    near = jnp.concatenate([g[0] for g in grads], axis=1)
    far = jnp.concatenate([g[1] for g in grads], axis=1)
    grad_far = swap(mm(far, w_mine, NT).astype(bf16))
    early_sum.add(grads[-1][0])
    input_grad = (grad_one + mm(near, w_mine, NT) + grad_far.astype(f32)).astype(bf16)
    returned = [lax.ppermute(input_grad[i * run : (i + 1) * run], ("core", "seq"), back[i]) for i in range(2)]
    last_sums = Halving(after(weight_sums(grads[-1:]), input_grad), planes)
    last_sums.send(0)
    for step in range(last_sums.steps):
        for sums in (first_sums, last_sums):
            sums.add()
            if step + 1 < sums.steps:
                sums.send(step + 1)
    qkv_sum = Spread(jnp.concatenate([first_sums.result(), last_sums.result()], axis=1), nseq)
    qkv_sum.add(*returned)
    input_grad = jnp.where(odd == 0, jnp.stack(returned), jnp.stack(returned[::-1]))[None].astype(f32)
    early_total = early_sum.result()
    qkv_total = qkv_sum.result()

    down_rows = down_grad[0].shape[1]
    down_final = early_total[:down_rows].astype(f32)
    wide = [early_total[down_rows + i * rows : down_rows + (i + 1) * rows] for i in range(inner_blocks)]
    in_final = jnp.concatenate(wide, axis=1).astype(f32)
    at = down_rows + inner_blocks * rows
    out_final = early_total[at : at + rows].astype(f32)
    at = at + rows
    line = early_total[at : at + 32, :rows].astype(f32)
    out_bias_final, g1, b1, down_bias_final, g2, b2 = [line[i] for i in range(6)]
    in_bias_final = line[6 : 6 + inner].reshape(-1)

    part = qkv_total
    column = part[CORES * rows]
    other = swap(jnp.concatenate([lax.dynamic_slice_in_dim(part, (1 - core) * rows, rows, 0), part[CORES * rows : CORES * rows + 16]]))
    own_block = lax.dynamic_slice_in_dim(part, core * rows, rows, 0)
    spread_out = lambda v: jnp.moveaxis(v.reshape(-1, pairs, 3, LANES), 2, 1).reshape(-1, 3, 1, mine)
    qkv_final = either(core, spread_out(own_block), spread_out(other[:rows]), 2).reshape(rows, 3 * width).astype(f32)
    sums = either(core, spread_out(column), spread_out(other[rows]), 2).reshape(3, width)
    shard = lax.axis_index("xy") * CORES + core
    q_final = lax.dynamic_slice_in_dim(sums[0], shard * rows, rows, 0).astype(f32)
    v_final = lax.dynamic_slice_in_dim(sums[2], shard * rows, rows, 0).astype(f32)
    output = jnp.where(odd == 0, jnp.stack(output), jnp.stack(output[::-1]))[None]
    return (
        output, input_grad, qkv_final, q_final, v_final, out_final, out_bias_final, g1, b1, in_final,
        in_bias_final, down_final, down_bias_final, g2, b2,
    )


def solution(mesh):
    fsdp, nseq = mesh.shape["fsdp"], mesh.shape["seq"]
    fine = Mesh(mesh.devices.reshape(fsdp // CORES, CORES, nseq), ("xy", "core", "seq"))
    shard = ("xy", "core")
    stream, matrix, vector = P(shard, None, "seq", None), P(shard, None), P(shard)
    return jax.shard_map(
        per_device,
        mesh=fine,
        in_specs=(
            stream, P(shard, None, None), matrix, vector, vector, matrix, vector, vector, vector,
            matrix, vector, matrix, vector, vector, vector, stream,
        ),
        out_specs=(
            stream, stream, matrix, vector, vector, matrix, vector, vector, vector,
            matrix, vector, matrix, vector, vector, vector,
        ),
        check_vma=False,
    )
```

```python
import functools
import math

import jax
import jax.numpy as jnp
from jax import lax
from jax.experimental import pallas as pl
from jax.experimental.pallas import tpu as pltpu
from jax.sharding import Mesh
from jax.sharding import PartitionSpec as P

HEAD_DIM = 64
LANES = 128
NEG = -1e30
TILE = 256
VALUE_ROWS = HEAD_DIM + 16
KEY_TILES = 2
QUERY_TILES = 2
NT = (((1,), (1,)), ((), ()))
NN = (((1,), (0,)), ((), ()))
TN = (((0,), (0,)), ((), ()))


def mm(left, right, dims):
    return lax.dot_general(left, right, dims, preferred_element_type=jnp.float32)


def key_tiles(ends_ref, first, last, tile, total):
    low = jnp.int32(0)
    high = jnp.int32(total)
    for doc in reversed(range(ends_ref.shape[0])):
        end = ends_ref[doc]
        low = jnp.maximum(low, jnp.where(end <= first, end, 0))
        high = jnp.minimum(high, jnp.where(end > last, end, total))
    return low // tile, (high + tile - 1) // tile


def spans(first, after, count, tiles):
    steps = (after - first + count - 1) // count
    return jnp.minimum(first, tiles - steps * count), steps


def lane_halves(x, fill):
    lane = lax.broadcasted_iota(jnp.int32, x.shape, 1)
    fill = jnp.full_like(x, fill)
    return jnp.where(lane < HEAD_DIM, x, fill), jnp.where(lane < HEAD_DIM, fill, x)


def piece_copies(halves, columns, place, scratch, slot, sems, run, mask, inbound):
    copies = []
    pieces = halves[0].shape[0] // run
    for half, ref in enumerate(halves):
        for part in range(pieces):
            index = half * pieces + part
            natural = pl.multiple_of(jnp.bitwise_xor(mask, index) * run, run)
            outer = ref.at[pl.ds(part * run, run), pl.ds(columns, LANES)]
            inner = scratch.at[place, pl.ds(natural, run), :]
            ends = (outer, inner) if inbound else (inner, outer)
            copies.append(pltpu.make_async_copy(ends[0], ends[1], sems.at[slot, index]))
    return copies


def forward_kernel(run, mask_ref, ends_ref, own, sib, seg_col, seg_row, ctx_own, ctx_sib, lse_ref, qkv, out, turned, acc, top, sems, out_sems):
    total = qkv.shape[1]
    pairs = out.shape[0]
    mask = mask_ref[0]

    def loads(pair):
        copies = []
        for kind in range(3):
            copies += piece_copies(
                (own, sib), (3 * pair + kind) * LANES, kind * pairs + pair, qkv, kind * pairs + pair, sems, run, mask, True
            )
        return copies

    for pair in range(pairs):
        for copy in loads(pair):
            copy.start()

    for head in range(2 * pairs):
        turned[head, HEAD_DIM:, :] = jnp.ones((VALUE_ROWS - HEAD_DIM, total), jnp.bfloat16)
    for pair in range(pairs):
        for copy in loads(pair):
            copy.wait()
    heads = [(pair, head) for pair in range(pairs) for head in range(2)]
    if True:

        @pl.loop(0, total // TILE)
        def _(block):
            rows = pl.multiple_of(block * TILE, TILE)
            for pair in range(pairs):
                values = qkv[2 * pairs + pair, pl.ds(rows, TILE), :].astype(jnp.float32).T.astype(jnp.bfloat16)
                for head in range(2):
                    turned[2 * pair + head, :HEAD_DIM, pl.ds(rows, TILE)] = values[head * HEAD_DIM : (head + 1) * HEAD_DIM]

        @pl.loop(0, total // TILE)
        def _(block):
            rows = pl.multiple_of(block * TILE, TILE)
            q_heads = sum([list(lane_halves(qkv[pair, pl.ds(rows, TILE), :], 0.0)) for pair in range(pairs)], [])
            segq = seg_row[:, pl.ds(rows, TILE)]
            first, after = key_tiles(ends_ref, rows, rows + TILE - 1, TILE, total)
            acc[...] = jnp.zeros_like(acc)
            top[...] = jnp.full_like(top, NEG)

            first, steps = spans(first, after, KEY_TILES, total // TILE)

            @pl.loop(0, steps)
            def _(step):
                at = pl.multiple_of((first + step * KEY_TILES) * TILE, TILE)
                keys = [qkv[pairs + pair, pl.ds(at, KEY_TILES * TILE), :] for pair in range(pairs)]
                segk = seg_col[pl.ds(at, KEY_TILES * TILE), :]
                same = jnp.concatenate([segk] * (TILE // LANES), axis=1) == segq
                for head in range(2 * pairs):
                    scores = jnp.where(same, mm(keys[head // 2], q_heads[head], NT), NEG)
                    old = top[head, 0:1]
                    new = jnp.maximum(old, jnp.max(scores, axis=0, keepdims=True))
                    probs = jnp.exp(scores - new).astype(jnp.bfloat16)
                    acc[head] = acc[head] * jnp.exp(old - new) + mm(turned[head, :, pl.ds(at, KEY_TILES * TILE)], probs, NN)
                    top[head] = jnp.broadcast_to(new, (8, TILE))

            for pair in range(pairs):
                parts = []
                for head in (2 * pair, 2 * pair + 1):
                    weight = acc[head, HEAD_DIM : HEAD_DIM + 1]
                    parts.append(acc[head, :HEAD_DIM] / weight)
                    lse_ref[head, :, pl.ds(rows, TILE)] = top[head] + jnp.log(acc[head, HEAD_DIM : HEAD_DIM + 8])
                out[pair, pl.ds(rows, TILE), :] = jnp.concatenate(parts, axis=0).T.astype(jnp.bfloat16)

    for pair in range(pairs):
        for copy in piece_copies((ctx_own, ctx_sib), pair * LANES, pair, out, pair, out_sems, run, mask, False):
            copy.start()
    for pair in range(pairs):
        for copy in piece_copies((ctx_own, ctx_sib), pair * LANES, pair, out, pair, out_sems, run, mask, False):
            copy.wait()


def attend_forward(mask, ends, own, sib, seg_col, seg_row, run):
    half, columns = own.shape
    total = 2 * half
    pairs = columns // (3 * LANES)
    pieces = total // run
    any_spec = pl.BlockSpec(memory_space=pl.ANY)
    vmem = pl.BlockSpec(memory_space=pltpu.VMEM)
    smem = pl.BlockSpec(memory_space=pltpu.SMEM)
    return pl.pallas_call(
        functools.partial(forward_kernel, run),
        out_shape=(
            jax.ShapeDtypeStruct((half, pairs * LANES), jnp.bfloat16),
            jax.ShapeDtypeStruct((half, pairs * LANES), jnp.bfloat16),
            jax.ShapeDtypeStruct((2 * pairs, 8, total), jnp.float32),
        ),
        in_specs=[smem, smem, any_spec, any_spec, vmem, vmem],
        out_specs=(any_spec, any_spec, vmem),
        scratch_shapes=[
            pltpu.VMEM((3 * pairs, total, LANES), jnp.bfloat16),
            pltpu.VMEM((pairs, total, LANES), jnp.bfloat16),
            pltpu.VMEM((2 * pairs, VALUE_ROWS, total), jnp.bfloat16),
            pltpu.VMEM((2 * pairs, VALUE_ROWS, TILE), jnp.float32),
            pltpu.VMEM((2 * pairs, 8, TILE), jnp.float32),
            pltpu.SemaphoreType.DMA((3 * pairs, pieces)),
            pltpu.SemaphoreType.DMA((pairs, pieces)),
        ],
        compiler_params=pltpu.CompilerParams(vmem_limit_bytes=40 << 20),
        cost_estimate=pl.CostEstimate(flops=1_000_000_000, bytes_accessed=1_000_000, transcendentals=0),
        name="attend_forward",
    )(mask, ends, own, sib, seg_col, seg_row)


def backward_kernel(
    run, pair, mask_ref, ends_ref, own, sib, ctx_own, ctx_sib, dctx_own, dctx_sib, seg_col, seg_row, lse_ref,
    d_own, d_sib, qkv, ctx, out, turned, delta, dq, dkv, sems, out_sems
):
    total = qkv.shape[1]
    mask = mask_ref[0]
    loads, stores = [], []
    for kind in range(3):
        loads += piece_copies((own, sib), (3 * pair + kind) * LANES, kind, qkv, kind, sems, run, mask, True)
        stores += piece_copies((d_own, d_sib), kind * LANES, kind, out, kind, out_sems, run, mask, False)
    loads += piece_copies((ctx_own, ctx_sib), pair * LANES, 0, ctx, 3, sems, run, mask, True)
    loads += piece_copies((dctx_own, dctx_sib), pair * LANES, 1, ctx, 4, sems, run, mask, True)
    for copy in loads:
        copy.start()
    for copy in loads:
        copy.wait()

    @pl.loop(0, total // TILE)
    def _(block):
        rows = pl.multiple_of(block * TILE, TILE)
        product = ctx[0, pl.ds(rows, TILE), :].astype(jnp.float32) * ctx[1, pl.ds(rows, TILE), :].astype(jnp.float32)
        product = product.T
        for head in range(2):
            part = jnp.sum(product[head * HEAD_DIM : (head + 1) * HEAD_DIM], axis=0, keepdims=True)
            delta[head, :, pl.ds(rows, TILE)] = jnp.broadcast_to(part, (8, TILE))
        turned[:, pl.ds(rows, TILE)] = qkv[1, pl.ds(rows, TILE), :].astype(jnp.float32).T.astype(jnp.bfloat16)
        dq[:, pl.ds(rows, TILE)] = jnp.zeros((LANES, TILE), jnp.float32)

    @pl.loop(0, total // TILE)
    def _(block):
        rows = pl.multiple_of(block * TILE, TILE)
        k_heads = lane_halves(qkv[1, pl.ds(rows, TILE), :], 0.0)
        v_heads = lane_halves(qkv[2, pl.ds(rows, TILE), :], 0.0)
        segk = seg_col[pl.ds(rows, TILE), :]
        segk = jnp.concatenate([segk] * (TILE // LANES), axis=1)
        first, after = key_tiles(ends_ref, rows, rows + TILE - 1, TILE, total)
        dkv[...] = jnp.zeros_like(dkv)

        first, steps = spans(first, after, QUERY_TILES, total // TILE)

        @pl.loop(0, steps)
        def _(step):
            at = pl.multiple_of((first + step * QUERY_TILES) * TILE, TILE)
            span = pl.ds(at, QUERY_TILES * TILE)
            queries = qkv[0, span, :]
            grads = ctx[1, span, :]
            q_heads = lane_halves(queries, 0.0)
            g_heads = lane_halves(grads, 0.0)
            same = jnp.concatenate([segk] * QUERY_TILES, axis=1) == seg_row[:, span]
            for head in range(2):
                scores = mm(k_heads[head], queries, NT)
                probs = jnp.exp(jnp.where(same, scores - lse_ref[2 * pair + head, 0:1, span], NEG))
                dprobs = mm(v_heads[head], grads, NT)
                dscores = (probs * (dprobs - delta[head, 0:1, span])).astype(jnp.bfloat16)
                dkv[1] += mm(probs.astype(jnp.bfloat16), g_heads[head], NN)
                dkv[0] += mm(dscores, q_heads[head], NN)
                lanes = slice(head * HEAD_DIM, (head + 1) * HEAD_DIM)
                dq[lanes, span] += mm(turned[lanes, pl.ds(rows, TILE)], dscores, NN)

        out[1, pl.ds(rows, TILE), :] = dkv[0].astype(jnp.bfloat16)
        out[2, pl.ds(rows, TILE), :] = dkv[1].astype(jnp.bfloat16)

    @pl.loop(0, total // TILE)
    def _(block):
        rows = pl.multiple_of(block * TILE, TILE)
        out[0, pl.ds(rows, TILE), :] = (dq[:, pl.ds(rows, TILE)].T * HEAD_DIM**-0.5).astype(jnp.bfloat16)

    for copy in stores:
        copy.start()
    for copy in stores:
        copy.wait()


def attend_backward(pair, mask, ends, own, sib, ctx_own, ctx_sib, dctx_own, dctx_sib, seg_col, seg_row, lse, run):
    half = own.shape[0]
    total = 2 * half
    pieces = total // run
    any_spec = pl.BlockSpec(memory_space=pl.ANY)
    vmem = pl.BlockSpec(memory_space=pltpu.VMEM)
    smem = pl.BlockSpec(memory_space=pltpu.SMEM)
    return pl.pallas_call(
        functools.partial(backward_kernel, run, pair),
        out_shape=(
            jax.ShapeDtypeStruct((half, 3 * LANES), jnp.bfloat16),
            jax.ShapeDtypeStruct((half, 3 * LANES), jnp.bfloat16),
        ),
        in_specs=[smem, smem] + [any_spec] * 6 + [vmem] * 3,
        out_specs=(any_spec, any_spec),
        scratch_shapes=[
            pltpu.VMEM((3, total, LANES), jnp.bfloat16),
            pltpu.VMEM((2, total, LANES), jnp.bfloat16),
            pltpu.VMEM((3, total, LANES), jnp.bfloat16),
            pltpu.VMEM((LANES, total), jnp.bfloat16),
            pltpu.VMEM((2, 8, total), jnp.float32),
            pltpu.VMEM((LANES, total), jnp.float32),
            pltpu.VMEM((2, TILE, LANES), jnp.float32),
            pltpu.SemaphoreType.DMA((5, pieces)),
            pltpu.SemaphoreType.DMA((3, pieces)),
        ],
        compiler_params=pltpu.CompilerParams(vmem_limit_bytes=24 << 20),
        cost_estimate=pl.CostEstimate(flops=20_000_000_000, bytes_accessed=8_000_000, transcendentals=0),
        name=f"attend_backward_{pair}",
    )(mask, ends, own, sib, ctx_own, ctx_sib, dctx_own, dctx_sib, seg_col, seg_row, lse)


EPS = 1e-05


def norm_forward(resid, gain, shift):
    mean = jnp.mean(resid, axis=-1, keepdims=True)
    centered = resid - mean
    inv = lax.rsqrt(jnp.mean(centered * centered, axis=-1, keepdims=True) + EPS)
    normed = centered * inv
    return (normed * gain + shift, normed, inv)


def norm_backward(grad, normed, inv, gain):
    scaled = grad * gain
    return inv * (
        scaled
        - jnp.mean(scaled, axis=-1, keepdims=True)
        - normed * jnp.mean(scaled * normed, axis=-1, keepdims=True)
    )


ROWS = 256
CHUNK = 768


def fold(x):
    return jnp.sum(x.reshape(-1, 8, x.shape[1]), axis=0)


def middle_kernel(
    core_ref, x_ref, near_ref, far_ref, cot_ref, vec_ref, in_bias_ref, w_out, w_in, w_down,
    result_ref, low_ref, act_ref, grad_down_ref, grad_pre_ref, grad_one_ref, grad_attn_ref, dnear_ref, dfar_ref,
    sums_ref, in_sums_ref, wo, wi, wd, slope, acc, sums, in_sums, sems
):
    f32, bf16 = jnp.float32, jnp.bfloat16
    mine = near_ref.shape[1]
    chunks = w_in.shape[1] // CHUNK
    step = pl.program_id(0)
    core = core_ref[0]
    copies = []
    for place in range(2):
        which = core if place == 0 else 1 - core
        rows = pl.multiple_of(which * mine, mine)
        copies.append(pltpu.make_async_copy(w_out.at[pl.ds(rows, mine), :], wo.at[pl.ds(place * mine, mine), :], sems.at[place]))
    for chunk in range(chunks):
        columns = pl.ds(chunk * CHUNK, CHUNK)
        copies.append(pltpu.make_async_copy(w_in.at[:, columns], wi.at[chunk], sems.at[2 + chunk]))
    for chunk in range(chunks):
        columns = pl.ds(chunk * CHUNK, CHUNK)
        copies.append(pltpu.make_async_copy(w_down.at[columns, :], wd.at[chunk], sems.at[2 + chunks + chunk]))

    @pl.when(step == 0)
    def _():
        for copy in copies:
            copy.start()
        sums[...] = jnp.zeros_like(sums)
        in_sums[...] = jnp.zeros_like(in_sums)
        for copy in copies[:2]:
            copy.wait()

    bias_out, gain_one, shift_one, bias_down, gain_two, shift_two = [vec_ref[i : i + 1, :] for i in range(6)]
    near, far = near_ref[...], far_ref[...]
    attn = mm(near, wo[:mine], NN) + mm(far, wo[mine:], NN) + bias_out
    hidden, normed_one, inv_one = norm_forward(x_ref[...].astype(f32) + attn, gain_one, shift_one)
    low_ref[...] = hidden.astype(bf16)
    acc[...] = hidden + bias_down

    @pl.when(step == 0)
    def _():
        for copy in copies[2:]:
            copy.wait()

    @pl.loop(0, chunks)
    def _(chunk):
        columns = pl.ds(pl.multiple_of(chunk * CHUNK, CHUNK), CHUNK)
        pre = mm(low_ref[...], wi[chunk], NN) + in_bias_ref[:, columns]
        cdf = 0.5 * (1.0 + lax.erf(pre * (1.0 / math.sqrt(2.0))))
        density = jnp.exp(-0.5 * pre * pre) * (1.0 / math.sqrt(2.0 * math.pi))
        act = (pre * cdf).astype(bf16)
        act_ref[:, columns] = act
        slope[:, columns] = cdf + pre * density
        acc[...] += mm(act, wd[chunk], NN)

    result, normed_two, inv_two = norm_forward(acc[...], gain_two, shift_two)
    result_ref[...] = result.astype(bf16)
    dy = cot_ref[...].astype(f32)
    grad_two = norm_backward(dy, normed_two, inv_two, gain_two)
    grad_down = grad_two.astype(bf16)
    grad_down_ref[...] = grad_down
    sums[3] += fold(grad_down.astype(f32))
    sums[4] += fold(dy * normed_two)
    sums[5] += fold(dy)
    acc[...] = grad_two

    @pl.loop(0, chunks)
    def _(chunk):
        columns = pl.ds(pl.multiple_of(chunk * CHUNK, CHUNK), CHUNK)
        grad_pre = (mm(grad_down_ref[...], wd[chunk], NT) * slope[:, columns]).astype(bf16)
        grad_pre_ref[:, columns] = grad_pre
        in_sums[:, columns] += fold(grad_pre.astype(f32))
        acc[...] += mm(grad_pre, wi[chunk], NT)

    grad_hidden = acc[...]
    sums[1] += fold(grad_hidden * normed_one)
    sums[2] += fold(grad_hidden)
    grad_one = norm_backward(grad_hidden, normed_one, inv_one, gain_one)
    grad_one_ref[...] = grad_one
    grad_attn = grad_one.astype(bf16)
    grad_attn_ref[...] = grad_attn
    sums[0] += fold(grad_attn.astype(f32))
    dnear_ref[...] = mm(grad_attn, wo[:mine], NT).astype(bf16)
    dfar_ref[...] = mm(grad_attn, wo[mine:], NT).astype(bf16)

    @pl.when(step == pl.num_programs(0) - 1)
    def _():
        sums_ref[...] = jnp.zeros_like(sums_ref)
        for i in range(6):
            sums_ref[i : i + 1, :] = jnp.sum(sums[i], axis=0, keepdims=True)
        in_sums_ref[...] = jnp.sum(in_sums[...], axis=0, keepdims=True)


def middle(core, x, near, far, cot, vec, in_bias, w_out, w_in, w_down):
    count, width = x.shape
    hidden = w_in.shape[1]
    mine = near.shape[1]
    chunks = hidden // CHUNK
    f32, bf16 = jnp.float32, jnp.bfloat16
    any_spec = pl.BlockSpec(memory_space=pl.ANY)
    block = lambda columns: pl.BlockSpec((ROWS, columns), lambda i: (i, 0))
    whole = lambda rows, columns: pl.BlockSpec((rows, columns), lambda i: (0, 0))
    shape = jax.ShapeDtypeStruct
    return pl.pallas_call(
        middle_kernel,
        grid=(count // ROWS,),
        out_shape=(
            shape((count, width), bf16), shape((count, width), bf16), shape((count, hidden), bf16),
            shape((count, width), bf16), shape((count, hidden), bf16), shape((count, width), f32),
            shape((count, width), bf16), shape((count, mine), bf16), shape((count, mine), bf16),
            shape((8, width), f32), shape((1, hidden), f32),
        ),
        in_specs=[
            pl.BlockSpec(memory_space=pltpu.SMEM), block(width), block(mine), block(mine), block(width),
            whole(8, width), whole(1, hidden), any_spec, any_spec, any_spec,
        ],
        out_specs=(
            block(width), block(width), block(hidden), block(width), block(hidden), block(width), block(width),
            block(mine), block(mine), whole(8, width), whole(1, hidden),
        ),
        scratch_shapes=[
            pltpu.VMEM((width, width), bf16),
            pltpu.VMEM((chunks, width, CHUNK), bf16),
            pltpu.VMEM((chunks, CHUNK, width), bf16),
            pltpu.VMEM((ROWS, hidden), f32),
            pltpu.VMEM((ROWS, width), f32),
            pltpu.VMEM((6, 8, width), f32),
            pltpu.VMEM((8, hidden), f32),
            pltpu.SemaphoreType.DMA((2 + 2 * chunks,)),
        ],
        compiler_params=pltpu.CompilerParams(vmem_limit_bytes=48 << 20),
        cost_estimate=pl.CostEstimate(flops=20_000_000_000, bytes_accessed=30_000_000, transcendentals=0),
        name="middle",
    )(core, x, near, far, cot, vec, in_bias, w_out, w_in, w_down)


def gradients_kernel(
    rows, core_ref, act_ref, low_ref, down_ref, pre_ref, near_ref, far_ref, attn_ref, vec_ref,
    keep_ref, send_ref, result, sems
):
    step = pl.program_id(0)
    core = core_ref[0]
    shards = low_ref.shape[1] // rows
    chunks = (pl.num_programs(0) - 1) // 2
    blocks = pre_ref.shape[1] * chunks // low_ref.shape[1]
    slot = step % 2

    def wait(which):
        pltpu.make_async_copy(result.at[which], result.at[which], sems.at[which]).wait()

    def put(source, shard_core, plane, at, count, sem):
        target = pl.ds(at, count)

        @pl.when(core == shard_core)
        def _():
            pltpu.make_async_copy(source, keep_ref.at[plane, target, :], sem).start()

        @pl.when(core != shard_core)
        def _():
            pltpu.make_async_copy(source, send_ref.at[plane, target, :], sem).start()

    @pl.when(step >= 2)
    def _():
        wait(slot)

    @pl.when(step < chunks)
    def _():
        result[slot] = mm(act_ref[...], down_ref[...], TN).astype(jnp.bfloat16)
        count = blocks * rows
        here = result.shape[1] // count
        for part in range(here):
            put(result.at[slot, pl.ds(part * count, count), :], part % CORES, step * (here // CORES) + part // CORES, 0, count, sems.at[slot])

    @pl.when(jnp.logical_and(step >= chunks, step < 2 * chunks))
    def _():
        result[slot] = mm(low_ref[...], pre_ref[...], TN).astype(jnp.bfloat16)
        at = pl.multiple_of(blocks * rows + (step - chunks) * rows, 16)
        for shard in range(shards):
            put(result.at[slot, pl.ds(shard * rows, rows), :], shard % CORES, shard // CORES, at, rows, sems.at[slot])

    @pl.when(step == 2 * chunks)
    def _():
        mine = near_ref.shape[1]
        result[slot, :mine] = mm(near_ref[...], attn_ref[...], TN).astype(jnp.bfloat16)
        result[slot, mine:] = mm(far_ref[...], attn_ref[...], TN).astype(jnp.bfloat16)
        half = shards // 2
        for shard in range(shards):
            first = core if shard < half else 1 - core
            plane = first * (half // CORES) + (shard % half) // CORES
            put(result.at[slot, pl.ds(shard * rows, rows), :], shard % CORES, plane, 2 * blocks * rows, rows, sems.at[slot])
        for shard in range(shards):
            put(vec_ref.at[shard], shard % CORES, shard // CORES, (2 * blocks + 1) * rows, vec_ref.shape[1], sems.at[2 + shard])
        wait(0)
        wait(1)
        for shard in range(shards):
            pltpu.make_async_copy(vec_ref.at[shard], vec_ref.at[shard], sems.at[2 + shard]).wait()


def gradients(core, act, low, down, pre, near, far, attn, vec, planes):
    count, width = low.shape
    rows = width // (planes * CORES)
    chunks = pre.shape[1] // width
    total_rows = (2 * chunks + 1) * rows + vec.shape[1]
    whole = lambda x: pl.BlockSpec(x.shape, lambda i: (0,) * x.ndim)
    out = jax.ShapeDtypeStruct((planes, total_rows, width), jnp.bfloat16)
    return pl.pallas_call(
        functools.partial(gradients_kernel, rows),
        grid=(2 * chunks + 1,),
        out_shape=(out, out),
        in_specs=[
            pl.BlockSpec(memory_space=pltpu.SMEM),
            pl.BlockSpec((count, width), lambda i: (0, jnp.minimum(i, chunks - 1))),
            whole(low), whole(down),
            pl.BlockSpec((count, width), lambda i: (0, jnp.clip(i - chunks, 0, chunks - 1))),
            whole(near), whole(far), whole(attn), whole(vec),
        ],
        out_specs=(pl.BlockSpec(memory_space=pl.ANY),) * 2,
        scratch_shapes=[
            pltpu.VMEM((2, width, width), jnp.bfloat16),
            pltpu.SemaphoreType.DMA((2 + planes * CORES,)),
        ],
        compiler_params=pltpu.CompilerParams(vmem_limit_bytes=48 << 20),
        cost_estimate=pl.CostEstimate(flops=11_000_000_000, bytes_accessed=30_000_000, transcendentals=0),
        name="gradients",
    )(core, act, low, down, pre, near, far, attn, vec)


def doc_ids(ends, count):
    places = jnp.arange(count, dtype=jnp.int32)
    return jnp.sum((places[:, None] >= ends[None, :]).astype(jnp.int32), axis=1)


CORES = 2


def routes(nseq):
    first, second = [], []
    for core in range(CORES):
        for z in range(nseq):
            source = core * nseq + z
            first.append((source, (z // 2) * nseq + 2 * core + z % 2))
            second.append((source, (z // 2) * nseq + 2 * core + 1 - z % 2))
    return first, second


def swap(x):
    return lax.ppermute(x, "core", [(0, 1), (1, 0)])


def after(value, *done):
    return lax.optimization_barrier((value, done))[0]


def pick(value, which, axis=0):
    return lax.dynamic_index_in_dim(value, which, axis, keepdims=False)


def total(keep, received):
    return (keep.astype(jnp.float32) + received.astype(jnp.float32)).astype(jnp.bfloat16)


class Halving:
    def __init__(self, blocks, planes):
        bits = planes.bit_length() - 1
        rows = blocks.shape[1]
        self.planes = planes
        self.orders = (list(range(bits)), list(range(bits))[::-1])
        self.left = [list(range(bits))[::-1] for _ in range(2)]
        parts = (blocks[:, : rows // 2], blocks[:, rows // 2 :])
        self.parts = [p.reshape((2,) * bits + p.shape[1:]) for p in parts]
        self.steps = bits

    def send(self, step):
        place = lax.axis_index("xy")
        self.keep, self.received, self.sent = [], [], []
        for half in range(2):
            bit = self.orders[half][step]
            axis = self.left[half].index(bit)
            mine = (place >> bit) % 2
            self.left[half].remove(bit)
            out = pick(self.parts[half], 1 - mine, axis)
            self.keep.append(pick(self.parts[half], mine, axis))
            self.sent.append(out)
            self.received.append(lax.ppermute(out, "xy", [(i, i ^ (1 << bit)) for i in range(self.planes)]))

    def add(self, *done):
        self.parts = [total(k, after(r, *done)) for k, r in zip(self.keep, self.received)]

    def result(self):
        return jnp.concatenate(self.parts)


class Spread:
    def __init__(self, value, nseq):
        self.nseq, self.rows = nseq, value.shape[0] // nseq
        self.me = lax.axis_index("seq")
        quarter = lambda which: lax.dynamic_slice_in_dim(value, (which % nseq) * self.rows, self.rows, 0)
        self.keep = quarter(self.me)
        self.sent = [quarter(self.me + d) for d in range(1, nseq)]
        self.received = [self.shift(q, d) for d, q in enumerate(self.sent, 1)]

    def shift(self, value, distance):
        return lax.ppermute(value, "seq", [(i, (i + distance) % self.nseq) for i in range(self.nseq)])

    def add(self, *done):
        parts = [self.keep] + [after(r, *done) for r in self.received]
        self.keep = sum(p.astype(jnp.float32) for p in parts).astype(jnp.bfloat16)
        self.received = [self.shift(self.keep, d) for d in range(1, self.nseq)]

    def result(self, *done):
        whole = jnp.zeros((self.nseq * self.rows,) + self.keep.shape[1:], jnp.bfloat16)
        for d, part in enumerate([self.keep] + [after(r, *done) for r in self.received]):
            start = ((self.me - d) % self.nseq) * self.rows
            whole = lax.dynamic_update_slice_in_dim(whole, part, start, 0)
        return whole


def either(core, own, other, axis):
    return jnp.where(core == 0, jnp.concatenate([own, other], axis), jnp.concatenate([other, own], axis))


def per_device(
    tokens, doc_lengths, qkv_weight, q_bias, v_bias, out_weight, out_bias, norm1_gain, norm1_bias,
    ff_in_weight, ff_in_bias, ff_out_weight, ff_out_bias, norm2_gain, norm2_bias, out_cotangent,
):
    bf16, f32 = jnp.bfloat16, jnp.float32
    fsdp = ("xy", "core")
    nseq = lax.axis_size("seq")
    planes = lax.axis_size("xy")
    shards = planes * CORES
    core = lax.axis_index("core")
    odd = lax.axis_index("seq") % 2
    micro, run, width = tokens.shape[1:]
    assert micro == 2 and nseq == 4
    stretch = run * nseq
    mine = width // CORES
    rows = width // shards
    first, second = routes(nseq)
    back = [[(b, a) for a, b in route] for route in (first, second)]

    def spread(x):
        halves = [lax.dynamic_index_in_dim(x[0], which, 0, keepdims=False) for which in (odd, 1 - odd)]
        return [lax.ppermute(h, ("core", "seq"), r) for h, r in zip(halves, (first, second))]

    pieces = spread(tokens)
    lengths = jnp.stack([doc_lengths[0], swap(doc_lengths[0])])
    z = lax.axis_index("seq")
    theirs = jnp.where(z // 2 == core, lengths[0], lengths[1])
    ends = jnp.cumsum(lax.dynamic_index_in_dim(theirs, odd, 0, keepdims=False)).astype(jnp.int32)
    seg = doc_ids(ends, stretch)
    seg_col = jnp.broadcast_to(seg[:, None], (stretch, LANES))
    seg_row = seg[None]
    mask = (odd + 2 * core).astype(jnp.int32)[None]

    pairs = mine // LANES
    own_columns = qkv_weight.reshape(rows, 3, CORES, pairs, LANES)
    own_columns = jnp.moveaxis(own_columns, (2, 3), (0, 2)).reshape(CORES, rows, 3 * mine)
    kept = pick(own_columns, core)
    w_mine = either(core, kept, swap(pick(own_columns, 1 - core)), 0)
    w_mine = lax.all_gather(w_mine, "xy", axis=0, tiled=True)
    small = [q_bias, v_bias, out_bias, norm1_gain, norm1_bias, ff_out_bias, norm2_gain, norm2_bias]
    inner = ff_in_bias.shape[0] // rows
    small = jnp.concatenate([jnp.stack(small), ff_in_bias.reshape(inner, rows)])
    vectors = lax.all_gather(small, fsdp, axis=0, tiled=False).astype(f32)
    bias_in = vectors[:, 8:].reshape(1, -1)
    vectors = jnp.moveaxis(vectors[:, :8], 0, 1).reshape(8, width)
    bias_q, bias_v = vectors[0], vectors[1]
    norms = jnp.concatenate([vectors[2:], jnp.zeros((2, width), f32)])
    w_out = lax.all_gather(out_weight, fsdp, axis=0, tiled=True)
    w_in = lax.all_gather(ff_in_weight, fsdp, axis=0, tiled=True)
    w_down = lax.all_gather(ff_out_weight, fsdp, axis=0, tiled=True)

    own_slice = lambda v: lax.dynamic_slice_in_dim(v, core * mine, mine, 0).reshape(pairs, LANES)
    one = jnp.ones((pairs, LANES), f32)
    bias_mine = jnp.stack([own_slice(bias_q), 0.0 * one, own_slice(bias_v)], axis=1).reshape(-1)
    scale = jnp.stack([HEAD_DIM**-0.5 * one, one, one], axis=1).reshape(-1)
    x_own = after(jnp.concatenate(pieces), norms, bias_in)
    x_sib = jnp.concatenate([swap(p) for p in pieces])
    projected = [((mm(x, w_mine, NN) + bias_mine) * scale).astype(bf16) for x in (x_own, x_sib)]
    ctx_own, ctx_sib, lse = attend_forward(mask, ends, *projected, seg_col, seg_row, run)
    ctx_far = swap(ctx_sib)

    cot = jnp.concatenate(spread(after(out_cotangent, x_own)))
    result, hidden_low, act_low, grad_down, grad_pre, grad_one, grad_attn, dctx_own, dctx_far, sums, in_sums = middle(
        core.astype(jnp.int32)[None], x_own, ctx_own, ctx_far, cot, norms, bias_in, w_out, w_in, w_down
    )
    dctx_far = swap(dctx_far)
    output = [lax.ppermute(result[i * run : (i + 1) * run], ("core", "seq"), back[i]) for i in range(2)]

    def cores(blocks):
        return pick(blocks, core, 1), swap(pick(blocks, 1 - core, 1))

    inner_blocks = ff_in_bias.shape[0] * shards // width
    down_rows = ff_out_weight.shape[0]
    vector = [jnp.moveaxis(sums[:6].reshape(6, shards, rows), 1, 0), in_sums.reshape(shards, inner, rows)]
    vector = jnp.concatenate(vector, axis=1).astype(bf16)
    vector = jnp.pad(vector, ((0, 0), (0, 32 - vector.shape[1]), (0, width - rows)))
    if rows % 16 == 0:
        kept, sent = gradients(
            core.astype(jnp.int32)[None], act_low, hidden_low, grad_down, grad_pre, ctx_own, ctx_far, grad_attn, vector, planes
        )
        joined = kept, swap(sent)
    else:
        down_grad = cores(mm(act_low, grad_down, TN).astype(bf16).reshape(planes, CORES, -1, width))
        in_grad = cores(mm(hidden_low, grad_pre, TN).astype(bf16).reshape(planes, CORES, rows, -1))
        out_grad = [mm(c, grad_attn, TN).astype(bf16) for c in (ctx_own, ctx_far)]
        out_grad = cores(either(core, *out_grad, 0).reshape(planes, CORES, rows, width))
        vector = cores(vector.reshape(planes, CORES, 32, width))
        joined = []
        for which in range(2):
            wide = in_grad[which]
            wide = [wide[:, :, i * width : (i + 1) * width] for i in range(inner_blocks)]
            joined.append(jnp.concatenate([down_grad[which]] + wide + [out_grad[which], vector[which]], axis=1))
    early = Halving(total(*joined), planes)
    early.send(0)
    progress = [early]

    def advance(*done):
        if len(progress) > 1:
            return []
        early.add(*done)
        step = early.steps - len(early.left[0])
        if step < early.steps:
            early.send(step)
            return early.sent
        progress.append(Spread(early.result(), nseq))
        return progress[1].sent

    def attend(pair, *ready):
        held = after(mask, *ready)
        return attend_backward(
            pair, held, ends, *projected, ctx_own, ctx_sib, dctx_own, dctx_far, seg_col, seg_row, lse, run
        )

    def weight_sums(grads):
        near = jnp.concatenate([g[0] for g in grads], axis=1)
        far = jnp.concatenate([g[1] for g in grads], axis=1)
        matrix = (mm(x_own, near, TN) + mm(x_sib, far, TN)).astype(bf16)
        column = (jnp.sum(near.astype(f32), axis=0) + jnp.sum(far.astype(f32), axis=0)).astype(bf16)
        column = jnp.pad(column[None], ((0, 63), (0, 0)))
        column = jnp.broadcast_to(column, (planes,) + column.shape)
        return jnp.concatenate([matrix.reshape(planes, CORES * rows, -1), column], axis=1)

    grads = [attend(0, *early.sent)]
    for pair in range(1, pairs):
        sent = advance(grads[-1][0])
        if pair == pairs - 1:
            first_sums = Halving(weight_sums(grads), planes)
            first_sums.send(0)
            sent = list(sent) + first_sums.sent
        grads.append(attend(pair, *sent, *(output if pair == 1 else ())))
    while len(progress) == 1:
        advance(grads[-1][0])
    early_sum = progress[1]

    near = jnp.concatenate([g[0] for g in grads], axis=1)
    far = jnp.concatenate([g[1] for g in grads], axis=1)
    grad_far = swap(mm(far, w_mine, NT).astype(bf16))
    early_sum.add(grads[-1][0])
    input_grad = (grad_one + mm(near, w_mine, NT) + grad_far.astype(f32)).astype(bf16)
    returned = [lax.ppermute(input_grad[i * run : (i + 1) * run], ("core", "seq"), back[i]) for i in range(2)]
    last_sums = Halving(after(weight_sums(grads[-1:]), input_grad), planes)
    last_sums.send(0)
    for step in range(last_sums.steps):
        for sums in (first_sums, last_sums):
            sums.add(input_grad)
            if step + 1 < sums.steps:
                sums.send(step + 1)
    qkv_sum = Spread(jnp.concatenate([first_sums.result(), last_sums.result()], axis=1), nseq)
    qkv_sum.add(*returned)
    input_grad = jnp.where(odd == 0, jnp.stack(returned), jnp.stack(returned[::-1]))[None].astype(f32)
    early_total = early_sum.result(qkv_sum.keep)
    qkv_total = qkv_sum.result()

    down_final = early_total[:down_rows].astype(f32)
    wide = [early_total[down_rows + i * rows : down_rows + (i + 1) * rows] for i in range(inner_blocks)]
    in_final = jnp.concatenate(wide, axis=1).astype(f32)
    at = down_rows + inner_blocks * rows
    out_final = early_total[at : at + rows].astype(f32)
    at = at + rows
    line = early_total[at : at + 32, :rows].astype(f32)
    out_bias_final, g1, b1, down_bias_final, g2, b2 = [line[i] for i in range(6)]
    in_bias_final = line[6 : 6 + inner].reshape(-1)

    part = qkv_total
    column = part[CORES * rows]
    other = swap(jnp.concatenate([lax.dynamic_slice_in_dim(part, (1 - core) * rows, rows, 0), part[CORES * rows : CORES * rows + 16]]))
    own_block = lax.dynamic_slice_in_dim(part, core * rows, rows, 0)
    spread_out = lambda v: jnp.moveaxis(v.reshape(-1, pairs, 3, LANES), 2, 1).reshape(-1, 3, 1, mine)
    qkv_final = either(core, spread_out(own_block), spread_out(other[:rows]), 2).reshape(rows, 3 * width).astype(f32)
    sums = either(core, spread_out(column), spread_out(other[rows]), 2).reshape(3, width)
    shard = lax.axis_index("xy") * CORES + core
    q_final = lax.dynamic_slice_in_dim(sums[0], shard * rows, rows, 0).astype(f32)
    v_final = lax.dynamic_slice_in_dim(sums[2], shard * rows, rows, 0).astype(f32)
    output = jnp.where(odd == 0, jnp.stack(output), jnp.stack(output[::-1]))[None]
    return (
        output, input_grad, qkv_final, q_final, v_final, out_final, out_bias_final, g1, b1, in_final,
        in_bias_final, down_final, down_bias_final, g2, b2,
    )


def solution(mesh):
    fsdp, nseq = mesh.shape["fsdp"], mesh.shape["seq"]
    fine = Mesh(mesh.devices.reshape(fsdp // CORES, CORES, nseq), ("xy", "core", "seq"))
    shard = ("xy", "core")
    stream, matrix, vector = P(shard, None, "seq", None), P(shard, None), P(shard)
    return jax.shard_map(
        per_device,
        mesh=fine,
        in_specs=(
            stream, P(shard, None, None), matrix, vector, vector, matrix, vector, vector, vector,
            matrix, vector, matrix, vector, vector, vector, stream,
        ),
        out_specs=(
            stream, stream, matrix, vector, vector, matrix, vector, vector, vector,
            matrix, vector, matrix, vector, vector, vector,
        ),
        check_vma=False,
    )
```

```python
import functools
import math

import jax
import jax.numpy as jnp
from jax import lax
from jax.experimental import pallas as pl
from jax.experimental.pallas import tpu as pltpu
from jax.sharding import Mesh
from jax.sharding import PartitionSpec as P

HEAD_DIM = 64
LANES = 128
NEG = -1e30
TILE = 256
VALUE_ROWS = HEAD_DIM + 16
KEY_TILES = 2
QUERY_TILES = 2
NT = (((1,), (1,)), ((), ()))
NN = (((1,), (0,)), ((), ()))
TN = (((0,), (0,)), ((), ()))


def mm(left, right, dims):
    return lax.dot_general(left, right, dims, preferred_element_type=jnp.float32)


def key_tiles(ends_ref, first, last, tile, total):
    low = jnp.int32(0)
    high = jnp.int32(total)
    for doc in reversed(range(ends_ref.shape[0])):
        end = ends_ref[doc]
        low = jnp.maximum(low, jnp.where(end <= first, end, 0))
        high = jnp.minimum(high, jnp.where(end > last, end, total))
    return low // tile, (high + tile - 1) // tile


def spans(first, after, count, tiles):
    steps = (after - first + count - 1) // count
    return jnp.minimum(first, tiles - steps * count), steps


def lane_halves(x, fill):
    lane = lax.broadcasted_iota(jnp.int32, x.shape, 1)
    fill = jnp.full_like(x, fill)
    return jnp.where(lane < HEAD_DIM, x, fill), jnp.where(lane < HEAD_DIM, fill, x)


def piece_copies(halves, columns, place, scratch, slot, sems, run, mask, inbound):
    copies = []
    pieces = halves[0].shape[0] // run
    for half, ref in enumerate(halves):
        for part in range(pieces):
            index = half * pieces + part
            natural = pl.multiple_of(jnp.bitwise_xor(mask, index) * run, run)
            outer = ref.at[pl.ds(part * run, run), pl.ds(columns, LANES)]
            inner = scratch.at[place, pl.ds(natural, run), :]
            ends = (outer, inner) if inbound else (inner, outer)
            copies.append(pltpu.make_async_copy(ends[0], ends[1], sems.at[slot, index]))
    return copies


def forward_kernel(run, mask_ref, ends_ref, own, sib, seg_col, seg_row, ctx_own, ctx_sib, lse_ref, qkv, out, turned, acc, top, sems, out_sems):
    total = qkv.shape[1]
    pairs = out.shape[0]
    mask = mask_ref[0]

    def loads(pair):
        copies = []
        for kind in range(3):
            copies += piece_copies(
                (own, sib), (3 * pair + kind) * LANES, kind * pairs + pair, qkv, kind * pairs + pair, sems, run, mask, True
            )
        return copies

    for pair in range(pairs):
        for copy in loads(pair):
            copy.start()

    for head in range(2 * pairs):
        turned[head, HEAD_DIM:, :] = jnp.ones((VALUE_ROWS - HEAD_DIM, total), jnp.bfloat16)
    for pair in range(pairs):
        for copy in loads(pair):
            copy.wait()
    heads = [(pair, head) for pair in range(pairs) for head in range(2)]
    if True:

        @pl.loop(0, total // TILE)
        def _(block):
            rows = pl.multiple_of(block * TILE, TILE)
            for pair in range(pairs):
                values = qkv[2 * pairs + pair, pl.ds(rows, TILE), :].astype(jnp.float32).T.astype(jnp.bfloat16)
                for head in range(2):
                    turned[2 * pair + head, :HEAD_DIM, pl.ds(rows, TILE)] = values[head * HEAD_DIM : (head + 1) * HEAD_DIM]

        @pl.loop(0, total // TILE)
        def _(block):
            rows = pl.multiple_of(block * TILE, TILE)
            q_heads = sum([list(lane_halves(qkv[pair, pl.ds(rows, TILE), :], 0.0)) for pair in range(pairs)], [])
            segq = seg_row[:, pl.ds(rows, TILE)]
            first, after = key_tiles(ends_ref, rows, rows + TILE - 1, TILE, total)
            acc[...] = jnp.zeros_like(acc)
            top[...] = jnp.full_like(top, NEG)

            first, steps = spans(first, after, KEY_TILES, total // TILE)

            @pl.loop(0, steps)
            def _(step):
                at = pl.multiple_of((first + step * KEY_TILES) * TILE, TILE)
                keys = [qkv[pairs + pair, pl.ds(at, KEY_TILES * TILE), :] for pair in range(pairs)]
                segk = seg_col[pl.ds(at, KEY_TILES * TILE), :]
                same = jnp.concatenate([segk] * (TILE // LANES), axis=1) == segq
                for head in range(2 * pairs):
                    scores = jnp.where(same, mm(keys[head // 2], q_heads[head], NT), NEG)
                    old = top[head, 0:1]
                    new = jnp.maximum(old, jnp.max(scores, axis=0, keepdims=True))
                    probs = jnp.exp(scores - new).astype(jnp.bfloat16)
                    acc[head] = acc[head] * jnp.exp(old - new) + mm(turned[head, :, pl.ds(at, KEY_TILES * TILE)], probs, NN)
                    top[head] = jnp.broadcast_to(new, (8, TILE))

            for pair in range(pairs):
                parts = []
                for head in (2 * pair, 2 * pair + 1):
                    weight = acc[head, HEAD_DIM : HEAD_DIM + 1]
                    parts.append(acc[head, :HEAD_DIM] / weight)
                    lse_ref[head, :, pl.ds(rows, TILE)] = top[head] + jnp.log(acc[head, HEAD_DIM : HEAD_DIM + 8])
                out[pair, pl.ds(rows, TILE), :] = jnp.concatenate(parts, axis=0).T.astype(jnp.bfloat16)

    for pair in range(pairs):
        for copy in piece_copies((ctx_own, ctx_sib), pair * LANES, pair, out, pair, out_sems, run, mask, False):
            copy.start()
    for pair in range(pairs):
        for copy in piece_copies((ctx_own, ctx_sib), pair * LANES, pair, out, pair, out_sems, run, mask, False):
            copy.wait()


def attend_forward(mask, ends, own, sib, seg_col, seg_row, run):
    half, columns = own.shape
    total = 2 * half
    pairs = columns // (3 * LANES)
    pieces = total // run
    any_spec = pl.BlockSpec(memory_space=pl.ANY)
    vmem = pl.BlockSpec(memory_space=pltpu.VMEM)
    smem = pl.BlockSpec(memory_space=pltpu.SMEM)
    return pl.pallas_call(
        functools.partial(forward_kernel, run),
        out_shape=(
            jax.ShapeDtypeStruct((half, pairs * LANES), jnp.bfloat16),
            jax.ShapeDtypeStruct((half, pairs * LANES), jnp.bfloat16),
            jax.ShapeDtypeStruct((2 * pairs, 8, total), jnp.float32),
        ),
        in_specs=[smem, smem, any_spec, any_spec, vmem, vmem],
        out_specs=(any_spec, any_spec, vmem),
        scratch_shapes=[
            pltpu.VMEM((3 * pairs, total, LANES), jnp.bfloat16),
            pltpu.VMEM((pairs, total, LANES), jnp.bfloat16),
            pltpu.VMEM((2 * pairs, VALUE_ROWS, total), jnp.bfloat16),
            pltpu.VMEM((2 * pairs, VALUE_ROWS, TILE), jnp.float32),
            pltpu.VMEM((2 * pairs, 8, TILE), jnp.float32),
            pltpu.SemaphoreType.DMA((3 * pairs, pieces)),
            pltpu.SemaphoreType.DMA((pairs, pieces)),
        ],
        compiler_params=pltpu.CompilerParams(vmem_limit_bytes=40 << 20),
        cost_estimate=pl.CostEstimate(flops=1_000_000_000, bytes_accessed=1_000_000, transcendentals=0),
        name="attend_forward",
    )(mask, ends, own, sib, seg_col, seg_row)


def backward_kernel(
    run, pair, mask_ref, ends_ref, own, sib, ctx_own, ctx_sib, dctx_own, dctx_sib, seg_col, seg_row, lse_ref,
    d_own, d_sib, qkv, ctx, out, turned, delta, dq, dkv, sems, out_sems
):
    total = qkv.shape[1]
    mask = mask_ref[0]
    loads, stores = [], []
    for kind in range(3):
        loads += piece_copies((own, sib), (3 * pair + kind) * LANES, kind, qkv, kind, sems, run, mask, True)
        stores += piece_copies((d_own, d_sib), kind * LANES, kind, out, kind, out_sems, run, mask, False)
    loads += piece_copies((ctx_own, ctx_sib), pair * LANES, 0, ctx, 3, sems, run, mask, True)
    loads += piece_copies((dctx_own, dctx_sib), pair * LANES, 1, ctx, 4, sems, run, mask, True)
    for copy in loads:
        copy.start()
    for copy in loads:
        copy.wait()

    @pl.loop(0, total // TILE)
    def _(block):
        rows = pl.multiple_of(block * TILE, TILE)
        product = ctx[0, pl.ds(rows, TILE), :].astype(jnp.float32) * ctx[1, pl.ds(rows, TILE), :].astype(jnp.float32)
        product = product.T
        for head in range(2):
            part = jnp.sum(product[head * HEAD_DIM : (head + 1) * HEAD_DIM], axis=0, keepdims=True)
            delta[head, :, pl.ds(rows, TILE)] = jnp.broadcast_to(part, (8, TILE))
        turned[:, pl.ds(rows, TILE)] = qkv[1, pl.ds(rows, TILE), :].astype(jnp.float32).T.astype(jnp.bfloat16)
        dq[:, pl.ds(rows, TILE)] = jnp.zeros((LANES, TILE), jnp.float32)

    @pl.loop(0, total // TILE)
    def _(block):
        rows = pl.multiple_of(block * TILE, TILE)
        k_heads = lane_halves(qkv[1, pl.ds(rows, TILE), :], 0.0)
        v_heads = lane_halves(qkv[2, pl.ds(rows, TILE), :], 0.0)
        segk = seg_col[pl.ds(rows, TILE), :]
        segk = jnp.concatenate([segk] * (TILE // LANES), axis=1)
        first, after = key_tiles(ends_ref, rows, rows + TILE - 1, TILE, total)
        dkv[...] = jnp.zeros_like(dkv)

        first, steps = spans(first, after, QUERY_TILES, total // TILE)

        @pl.loop(0, steps)
        def _(step):
            at = pl.multiple_of((first + step * QUERY_TILES) * TILE, TILE)
            span = pl.ds(at, QUERY_TILES * TILE)
            queries = qkv[0, span, :]
            grads = ctx[1, span, :]
            q_heads = lane_halves(queries, 0.0)
            g_heads = lane_halves(grads, 0.0)
            same = jnp.concatenate([segk] * QUERY_TILES, axis=1) == seg_row[:, span]
            for head in range(2):
                scores = mm(k_heads[head], queries, NT)
                probs = jnp.exp(jnp.where(same, scores - lse_ref[2 * pair + head, 0:1, span], NEG))
                dprobs = mm(v_heads[head], grads, NT)
                dscores = (probs * (dprobs - delta[head, 0:1, span])).astype(jnp.bfloat16)
                dkv[1] += mm(probs.astype(jnp.bfloat16), g_heads[head], NN)
                dkv[0] += mm(dscores, q_heads[head], NN)
                lanes = slice(head * HEAD_DIM, (head + 1) * HEAD_DIM)
                dq[lanes, span] += mm(turned[lanes, pl.ds(rows, TILE)], dscores, NN)

        out[1, pl.ds(rows, TILE), :] = dkv[0].astype(jnp.bfloat16)
        out[2, pl.ds(rows, TILE), :] = dkv[1].astype(jnp.bfloat16)

    @pl.loop(0, total // TILE)
    def _(block):
        rows = pl.multiple_of(block * TILE, TILE)
        out[0, pl.ds(rows, TILE), :] = (dq[:, pl.ds(rows, TILE)].T * HEAD_DIM**-0.5).astype(jnp.bfloat16)

    for copy in stores:
        copy.start()
    for copy in stores:
        copy.wait()


def attend_backward(pair, mask, ends, own, sib, ctx_own, ctx_sib, dctx_own, dctx_sib, seg_col, seg_row, lse, run):
    half = own.shape[0]
    total = 2 * half
    pieces = total // run
    any_spec = pl.BlockSpec(memory_space=pl.ANY)
    vmem = pl.BlockSpec(memory_space=pltpu.VMEM)
    smem = pl.BlockSpec(memory_space=pltpu.SMEM)
    return pl.pallas_call(
        functools.partial(backward_kernel, run, pair),
        out_shape=(
            jax.ShapeDtypeStruct((half, 3 * LANES), jnp.bfloat16),
            jax.ShapeDtypeStruct((half, 3 * LANES), jnp.bfloat16),
        ),
        in_specs=[smem, smem] + [any_spec] * 6 + [vmem] * 3,
        out_specs=(any_spec, any_spec),
        scratch_shapes=[
            pltpu.VMEM((3, total, LANES), jnp.bfloat16),
            pltpu.VMEM((2, total, LANES), jnp.bfloat16),
            pltpu.VMEM((3, total, LANES), jnp.bfloat16),
            pltpu.VMEM((LANES, total), jnp.bfloat16),
            pltpu.VMEM((2, 8, total), jnp.float32),
            pltpu.VMEM((LANES, total), jnp.float32),
            pltpu.VMEM((2, TILE, LANES), jnp.float32),
            pltpu.SemaphoreType.DMA((5, pieces)),
            pltpu.SemaphoreType.DMA((3, pieces)),
        ],
        compiler_params=pltpu.CompilerParams(vmem_limit_bytes=24 << 20),
        cost_estimate=pl.CostEstimate(flops=20_000_000_000, bytes_accessed=8_000_000, transcendentals=0),
        name=f"attend_backward_{pair}",
    )(mask, ends, own, sib, ctx_own, ctx_sib, dctx_own, dctx_sib, seg_col, seg_row, lse)


EPS = 1e-05


def norm_forward(resid, gain, shift):
    mean = jnp.mean(resid, axis=-1, keepdims=True)
    centered = resid - mean
    inv = lax.rsqrt(jnp.mean(centered * centered, axis=-1, keepdims=True) + EPS)
    normed = centered * inv
    return (normed * gain + shift, normed, inv)


def norm_backward(grad, normed, inv, gain):
    scaled = grad * gain
    return inv * (
        scaled
        - jnp.mean(scaled, axis=-1, keepdims=True)
        - normed * jnp.mean(scaled * normed, axis=-1, keepdims=True)
    )


ROWS = 256
CHUNK = 768


def fold(x):
    return jnp.sum(x.reshape(-1, 8, x.shape[1]), axis=0)


def middle_kernel(
    core_ref, x_ref, near_ref, far_ref, cot_ref, vec_ref, in_bias_ref, packed,
    result_ref, low_ref, act_ref, grad_down_ref, grad_pre_ref, grad_one_ref, grad_attn_ref, dnear_ref, dfar_ref,
    sums_ref, in_sums_ref, wo, wi, wd, slope, acc, sums, in_sums, sems
):
    f32, bf16 = jnp.float32, jnp.bfloat16
    mine = near_ref.shape[1]
    chunks = wi.shape[0]
    step = pl.program_id(0)
    core = core_ref[0]
    shards = packed.shape[0]
    rows = packed.shape[1] // (2 * chunks + 1)
    copies = []

    def load(shard, at, count, target):
        copies.append(pltpu.make_async_copy(packed.at[shard, pl.ds(at, count), :], target, sems.at[len(copies)]))

    if shards == 1:
        for place in range(2):
            which = core if place == 0 else 1 - core
            load(0, pl.multiple_of(2 * chunks * rows + which * mine, 16), mine, wo.at[pl.ds(place * mine, mine), :])
    else:
        for place in range(2):
            which = core if place == 0 else 1 - core
            for part in range(shards // 2):
                target = wo.at[pl.ds(place * mine + part * rows, rows), :]
                load(which * (shards // 2) + part, 2 * chunks * rows, rows, target)
    outs = len(copies)
    for chunk in range(chunks):
        for shard in range(shards):
            load(shard, (chunks + chunk) * rows, rows, wi.at[chunk, pl.ds(shard * rows, rows), :])
    for chunk in range(chunks):
        for shard in range(shards):
            first = shard * chunks * rows
            low, high = max(first, chunk * CHUNK), min(first + chunks * rows, (chunk + 1) * CHUNK)
            if low < high:
                load(shard, low - first, high - low, wd.at[chunk, pl.ds(low - chunk * CHUNK, high - low), :])

    @pl.when(step == 0)
    def _():
        for copy in copies:
            copy.start()
        sums[...] = jnp.zeros_like(sums)
        in_sums[...] = jnp.zeros_like(in_sums)
        for copy in copies[:outs]:
            copy.wait()

    bias_out, gain_one, shift_one, bias_down, gain_two, shift_two = [vec_ref[i : i + 1, :] for i in range(6)]
    near, far = near_ref[...], far_ref[...]
    attn = mm(near, wo[:mine], NN) + mm(far, wo[mine:], NN) + bias_out
    hidden, normed_one, inv_one = norm_forward(x_ref[...].astype(f32) + attn, gain_one, shift_one)
    low_ref[...] = hidden.astype(bf16)
    acc[...] = hidden + bias_down

    @pl.when(step == 0)
    def _():
        for copy in copies[outs:]:
            copy.wait()

    @pl.loop(0, chunks)
    def _(chunk):
        columns = pl.ds(pl.multiple_of(chunk * CHUNK, CHUNK), CHUNK)
        pre = mm(low_ref[...], wi[chunk], NN) + in_bias_ref[:, columns]
        cdf = 0.5 * (1.0 + lax.erf(pre * (1.0 / math.sqrt(2.0))))
        density = jnp.exp(-0.5 * pre * pre) * (1.0 / math.sqrt(2.0 * math.pi))
        act = (pre * cdf).astype(bf16)
        act_ref[:, columns] = act
        slope[:, columns] = cdf + pre * density
        acc[...] += mm(act, wd[chunk], NN)

    result, normed_two, inv_two = norm_forward(acc[...], gain_two, shift_two)
    result_ref[...] = result.astype(bf16)
    dy = cot_ref[...].astype(f32)
    grad_two = norm_backward(dy, normed_two, inv_two, gain_two)
    grad_down = grad_two.astype(bf16)
    grad_down_ref[...] = grad_down
    sums[3] += fold(grad_down.astype(f32))
    sums[4] += fold(dy * normed_two)
    sums[5] += fold(dy)
    acc[...] = grad_two

    @pl.loop(0, chunks)
    def _(chunk):
        columns = pl.ds(pl.multiple_of(chunk * CHUNK, CHUNK), CHUNK)
        grad_pre = (mm(grad_down_ref[...], wd[chunk], NT) * slope[:, columns]).astype(bf16)
        grad_pre_ref[:, columns] = grad_pre
        in_sums[:, columns] += fold(grad_pre.astype(f32))
        acc[...] += mm(grad_pre, wi[chunk], NT)

    grad_hidden = acc[...]
    sums[1] += fold(grad_hidden * normed_one)
    sums[2] += fold(grad_hidden)
    grad_one = norm_backward(grad_hidden, normed_one, inv_one, gain_one)
    grad_one_ref[...] = grad_one
    grad_attn = grad_one.astype(bf16)
    grad_attn_ref[...] = grad_attn
    sums[0] += fold(grad_attn.astype(f32))
    dnear_ref[...] = mm(grad_attn, wo[:mine], NT).astype(bf16)
    dfar_ref[...] = mm(grad_attn, wo[mine:], NT).astype(bf16)

    @pl.when(step == pl.num_programs(0) - 1)
    def _():
        sums_ref[...] = jnp.zeros_like(sums_ref)
        for i in range(6):
            sums_ref[i : i + 1, :] = jnp.sum(sums[i], axis=0, keepdims=True)
        in_sums_ref[...] = jnp.sum(in_sums[...], axis=0, keepdims=True)


def middle(core, x, near, far, cot, vec, in_bias, packed):
    count, width = x.shape
    hidden = in_bias.shape[1]
    mine = near.shape[1]
    chunks = hidden // CHUNK
    f32, bf16 = jnp.float32, jnp.bfloat16
    any_spec = pl.BlockSpec(memory_space=pl.ANY)
    block = lambda columns: pl.BlockSpec((ROWS, columns), lambda i: (i, 0))
    whole = lambda rows, columns: pl.BlockSpec((rows, columns), lambda i: (0, 0))
    shape = jax.ShapeDtypeStruct
    return pl.pallas_call(
        middle_kernel,
        grid=(count // ROWS,),
        out_shape=(
            shape((count, width), bf16), shape((count, width), bf16), shape((count, hidden), bf16),
            shape((count, width), bf16), shape((count, hidden), bf16), shape((count, width), f32),
            shape((count, width), bf16), shape((count, mine), bf16), shape((count, mine), bf16),
            shape((8, width), f32), shape((1, hidden), f32),
        ),
        in_specs=[
            pl.BlockSpec(memory_space=pltpu.SMEM), block(width), block(mine), block(mine), block(width),
            whole(8, width), whole(1, hidden), any_spec,
        ],
        out_specs=(
            block(width), block(width), block(hidden), block(width), block(hidden), block(width), block(width),
            block(mine), block(mine), whole(8, width), whole(1, hidden),
        ),
        scratch_shapes=[
            pltpu.VMEM((width, width), bf16),
            pltpu.VMEM((chunks, width, CHUNK), bf16),
            pltpu.VMEM((chunks, CHUNK, width), bf16),
            pltpu.VMEM((ROWS, hidden), f32),
            pltpu.VMEM((ROWS, width), f32),
            pltpu.VMEM((6, 8, width), f32),
            pltpu.VMEM((8, hidden), f32),
            pltpu.SemaphoreType.DMA(((2 * chunks + 1) * max(packed.shape[0], 2),)),
        ],
        compiler_params=pltpu.CompilerParams(vmem_limit_bytes=48 << 20),
        cost_estimate=pl.CostEstimate(flops=20_000_000_000, bytes_accessed=30_000_000, transcendentals=0),
        name="middle",
    )(core, x, near, far, cot, vec, in_bias, packed)


def gradients_kernel(
    rows, core_ref, act_ref, low_ref, down_ref, pre_ref, near_ref, far_ref, attn_ref, vec_ref,
    keep_ref, send_ref, result, sems
):
    step = pl.program_id(0)
    core = core_ref[0]
    shards = low_ref.shape[1] // rows
    chunks = (pl.num_programs(0) - 1) // 2
    blocks = pre_ref.shape[1] * chunks // low_ref.shape[1]
    slot = step % 2

    def wait(which):
        pltpu.make_async_copy(result.at[which], result.at[which], sems.at[which]).wait()

    def put(source, shard_core, plane, at, count, sem):
        target = pl.ds(at, count)

        @pl.when(core == shard_core)
        def _():
            pltpu.make_async_copy(source, keep_ref.at[plane, target, :], sem).start()

        @pl.when(core != shard_core)
        def _():
            pltpu.make_async_copy(source, send_ref.at[plane, target, :], sem).start()

    @pl.when(step >= 2)
    def _():
        wait(slot)

    @pl.when(step < chunks)
    def _():
        result[slot] = mm(act_ref[...], down_ref[...], TN).astype(jnp.bfloat16)
        count = blocks * rows
        here = result.shape[1] // count
        for part in range(here):
            put(result.at[slot, pl.ds(part * count, count), :], part % CORES, step * (here // CORES) + part // CORES, 0, count, sems.at[slot])

    @pl.when(jnp.logical_and(step >= chunks, step < 2 * chunks))
    def _():
        result[slot] = mm(low_ref[...], pre_ref[...], TN).astype(jnp.bfloat16)
        at = pl.multiple_of(blocks * rows + (step - chunks) * rows, 16)
        for shard in range(shards):
            put(result.at[slot, pl.ds(shard * rows, rows), :], shard % CORES, shard // CORES, at, rows, sems.at[slot])

    @pl.when(step == 2 * chunks)
    def _():
        mine = near_ref.shape[1]
        result[slot, :mine] = mm(near_ref[...], attn_ref[...], TN).astype(jnp.bfloat16)
        result[slot, mine:] = mm(far_ref[...], attn_ref[...], TN).astype(jnp.bfloat16)
        half = shards // 2
        for shard in range(shards):
            first = core if shard < half else 1 - core
            plane = first * (half // CORES) + (shard % half) // CORES
            put(result.at[slot, pl.ds(shard * rows, rows), :], shard % CORES, plane, 2 * blocks * rows, rows, sems.at[slot])
        for shard in range(shards):
            put(vec_ref.at[shard], shard % CORES, shard // CORES, (2 * blocks + 1) * rows, vec_ref.shape[1], sems.at[2 + shard])
        wait(0)
        wait(1)
        for shard in range(shards):
            pltpu.make_async_copy(vec_ref.at[shard], vec_ref.at[shard], sems.at[2 + shard]).wait()


def gradients(core, act, low, down, pre, near, far, attn, vec, planes):
    count, width = low.shape
    rows = width // (planes * CORES)
    chunks = pre.shape[1] // width
    total_rows = (2 * chunks + 1) * rows + vec.shape[1]
    whole = lambda x: pl.BlockSpec(x.shape, lambda i: (0,) * x.ndim)
    out = jax.ShapeDtypeStruct((planes, total_rows, width), jnp.bfloat16)
    return pl.pallas_call(
        functools.partial(gradients_kernel, rows),
        grid=(2 * chunks + 1,),
        out_shape=(out, out),
        in_specs=[
            pl.BlockSpec(memory_space=pltpu.SMEM),
            pl.BlockSpec((count, width), lambda i: (0, jnp.minimum(i, chunks - 1))),
            whole(low), whole(down),
            pl.BlockSpec((count, width), lambda i: (0, jnp.clip(i - chunks, 0, chunks - 1))),
            whole(near), whole(far), whole(attn), whole(vec),
        ],
        out_specs=(pl.BlockSpec(memory_space=pl.ANY),) * 2,
        scratch_shapes=[
            pltpu.VMEM((2, width, width), jnp.bfloat16),
            pltpu.SemaphoreType.DMA((2 + planes * CORES,)),
        ],
        compiler_params=pltpu.CompilerParams(vmem_limit_bytes=48 << 20),
        cost_estimate=pl.CostEstimate(flops=11_000_000_000, bytes_accessed=30_000_000, transcendentals=0),
        name="gradients",
    )(core, act, low, down, pre, near, far, attn, vec)


def doc_ids(ends, count):
    places = jnp.arange(count, dtype=jnp.int32)
    return jnp.sum((places[:, None] >= ends[None, :]).astype(jnp.int32), axis=1)


CORES = 2


def routes(nseq):
    first, second = [], []
    for core in range(CORES):
        for z in range(nseq):
            source = core * nseq + z
            first.append((source, (z // 2) * nseq + 2 * core + z % 2))
            second.append((source, (z // 2) * nseq + 2 * core + 1 - z % 2))
    return first, second


def swap(x):
    return lax.ppermute(x, "core", [(0, 1), (1, 0)])


def after(value, *done):
    return lax.optimization_barrier((value, done))[0]


def pick(value, which, axis=0):
    return lax.dynamic_index_in_dim(value, which, axis, keepdims=False)


def total(keep, received):
    return (keep.astype(jnp.float32) + received.astype(jnp.float32)).astype(jnp.bfloat16)


class Halving:
    def __init__(self, blocks, planes):
        bits = planes.bit_length() - 1
        rows = blocks.shape[1]
        self.planes = planes
        self.orders = (list(range(bits)), list(range(bits))[::-1])
        self.left = [list(range(bits))[::-1] for _ in range(2)]
        parts = (blocks[:, : rows // 2], blocks[:, rows // 2 :])
        self.parts = [p.reshape((2,) * bits + p.shape[1:]) for p in parts]
        self.steps = bits

    def send(self, step):
        place = lax.axis_index("xy")
        self.keep, self.received, self.sent = [], [], []
        for half in range(2):
            bit = self.orders[half][step]
            axis = self.left[half].index(bit)
            mine = (place >> bit) % 2
            self.left[half].remove(bit)
            out = pick(self.parts[half], 1 - mine, axis)
            self.keep.append(pick(self.parts[half], mine, axis))
            self.sent.append(out)
            self.received.append(lax.ppermute(out, "xy", [(i, i ^ (1 << bit)) for i in range(self.planes)]))

    def add(self, *done):
        self.parts = [total(k, after(r, *done)) for k, r in zip(self.keep, self.received)]

    def result(self):
        return jnp.concatenate(self.parts)


class Spread:
    def __init__(self, value, nseq):
        self.nseq, self.rows = nseq, value.shape[0] // nseq
        self.me = lax.axis_index("seq")
        quarter = lambda which: lax.dynamic_slice_in_dim(value, (which % nseq) * self.rows, self.rows, 0)
        self.keep = quarter(self.me)
        self.sent = [quarter(self.me + d) for d in range(1, nseq)]
        self.received = [self.shift(q, d) for d, q in enumerate(self.sent, 1)]

    def shift(self, value, distance):
        return lax.ppermute(value, "seq", [(i, (i + distance) % self.nseq) for i in range(self.nseq)])

    def add(self, *done):
        parts = [self.keep] + [after(r, *done) for r in self.received]
        self.keep = sum(p.astype(jnp.float32) for p in parts).astype(jnp.bfloat16)
        self.received = [self.shift(self.keep, d) for d in range(1, self.nseq)]

    def result(self, *done):
        whole = jnp.zeros((self.nseq * self.rows,) + self.keep.shape[1:], jnp.bfloat16)
        for d, part in enumerate([self.keep] + [after(r, *done) for r in self.received]):
            start = ((self.me - d) % self.nseq) * self.rows
            whole = lax.dynamic_update_slice_in_dim(whole, part, start, 0)
        return whole


def either(core, own, other, axis):
    return jnp.where(core == 0, jnp.concatenate([own, other], axis), jnp.concatenate([other, own], axis))


def per_device(
    tokens, doc_lengths, qkv_weight, q_bias, v_bias, out_weight, out_bias, norm1_gain, norm1_bias,
    ff_in_weight, ff_in_bias, ff_out_weight, ff_out_bias, norm2_gain, norm2_bias, out_cotangent,
):
    bf16, f32 = jnp.bfloat16, jnp.float32
    fsdp = ("xy", "core")
    nseq = lax.axis_size("seq")
    planes = lax.axis_size("xy")
    shards = planes * CORES
    core = lax.axis_index("core")
    odd = lax.axis_index("seq") % 2
    micro, run, width = tokens.shape[1:]
    assert micro == 2 and nseq == 4
    stretch = run * nseq
    mine = width // CORES
    rows = width // shards
    first, second = routes(nseq)
    back = [[(b, a) for a, b in route] for route in (first, second)]

    def spread(x):
        halves = [lax.dynamic_index_in_dim(x[0], which, 0, keepdims=False) for which in (odd, 1 - odd)]
        return [lax.ppermute(h, ("core", "seq"), r) for h, r in zip(halves, (first, second))]

    pieces = spread(tokens)
    lengths = jnp.stack([doc_lengths[0], swap(doc_lengths[0])])
    z = lax.axis_index("seq")
    theirs = jnp.where(z // 2 == core, lengths[0], lengths[1])
    ends = jnp.cumsum(lax.dynamic_index_in_dim(theirs, odd, 0, keepdims=False)).astype(jnp.int32)
    seg = doc_ids(ends, stretch)
    seg_col = jnp.broadcast_to(seg[:, None], (stretch, LANES))
    seg_row = seg[None]
    mask = (odd + 2 * core).astype(jnp.int32)[None]

    pairs = mine // LANES
    own_columns = qkv_weight.reshape(rows, 3, CORES, pairs, LANES)
    own_columns = jnp.moveaxis(own_columns, (2, 3), (0, 2)).reshape(CORES, rows, 3 * mine)
    kept = pick(own_columns, core)
    w_mine = either(core, kept, swap(pick(own_columns, 1 - core)), 0)
    w_mine = lax.all_gather(w_mine, "xy", axis=0, tiled=True)
    small = [q_bias, v_bias, out_bias, norm1_gain, norm1_bias, ff_out_bias, norm2_gain, norm2_bias]
    inner = ff_in_bias.shape[0] // rows
    small = jnp.concatenate([jnp.stack(small), ff_in_bias.reshape(inner, rows)])
    vectors = lax.all_gather(small, fsdp, axis=0, tiled=False).astype(f32)
    bias_in = vectors[:, 8:].reshape(1, -1)
    vectors = jnp.moveaxis(vectors[:, :8], 0, 1).reshape(8, width)
    bias_q, bias_v = vectors[0], vectors[1]
    norms = jnp.concatenate([vectors[2:], jnp.zeros((2, width), f32)])
    wide = [ff_in_weight[:, i * width : (i + 1) * width] for i in range(inner)]
    packed = lax.all_gather(jnp.concatenate([ff_out_weight] + wide + [out_weight]), fsdp, axis=0, tiled=False)
    if rows % 16:
        parts = [packed[:, : inner * rows].reshape(-1, width)]
        parts += [packed[:, (inner + i) * rows : (inner + i + 1) * rows].reshape(width, width) for i in range(inner + 1)]
        packed = jnp.concatenate(parts)[None]

    own_slice = lambda v: lax.dynamic_slice_in_dim(v, core * mine, mine, 0).reshape(pairs, LANES)
    one = jnp.ones((pairs, LANES), f32)
    bias_mine = jnp.stack([own_slice(bias_q), 0.0 * one, own_slice(bias_v)], axis=1).reshape(-1)
    scale = jnp.stack([HEAD_DIM**-0.5 * one, one, one], axis=1).reshape(-1)
    x_own = after(jnp.concatenate(pieces), norms, bias_in)
    x_sib = jnp.concatenate([swap(p) for p in pieces])
    projected = [((mm(x, w_mine, NN) + bias_mine) * scale).astype(bf16) for x in (x_own, x_sib)]
    ctx_own, ctx_sib, lse = attend_forward(mask, ends, *projected, seg_col, seg_row, run)
    ctx_far = swap(ctx_sib)

    cot = jnp.concatenate(spread(after(out_cotangent, *projected)))
    result, hidden_low, act_low, grad_down, grad_pre, grad_one, grad_attn, dctx_own, dctx_far, sums, in_sums = middle(
        core.astype(jnp.int32)[None], x_own, ctx_own, ctx_far, cot, norms, bias_in, packed
    )
    dctx_far = swap(dctx_far)
    output = [lax.ppermute(result[i * run : (i + 1) * run], ("core", "seq"), back[i]) for i in range(2)]

    def cores(blocks):
        return pick(blocks, core, 1), swap(pick(blocks, 1 - core, 1))

    inner_blocks = ff_in_bias.shape[0] * shards // width
    down_rows = ff_out_weight.shape[0]
    vector = [jnp.moveaxis(sums[:6].reshape(6, shards, rows), 1, 0), in_sums.reshape(shards, inner, rows)]
    vector = jnp.concatenate(vector, axis=1).astype(bf16)
    vector = jnp.pad(vector, ((0, 0), (0, 32 - vector.shape[1]), (0, width - rows)))
    if rows % 16 == 0:
        kept, sent = gradients(
            core.astype(jnp.int32)[None], act_low, hidden_low, grad_down, grad_pre, ctx_own, ctx_far, grad_attn, vector, planes
        )
        joined = kept, swap(sent)
    else:
        down_grad = cores(mm(act_low, grad_down, TN).astype(bf16).reshape(planes, CORES, -1, width))
        in_grad = cores(mm(hidden_low, grad_pre, TN).astype(bf16).reshape(planes, CORES, rows, -1))
        out_grad = [mm(c, grad_attn, TN).astype(bf16) for c in (ctx_own, ctx_far)]
        out_grad = cores(either(core, *out_grad, 0).reshape(planes, CORES, rows, width))
        vector = cores(vector.reshape(planes, CORES, 32, width))
        joined = []
        for which in range(2):
            wide = in_grad[which]
            wide = [wide[:, :, i * width : (i + 1) * width] for i in range(inner_blocks)]
            joined.append(jnp.concatenate([down_grad[which]] + wide + [out_grad[which], vector[which]], axis=1))
    early = Halving(total(*joined), planes)
    early.send(0)
    progress = [early]

    def advance(*done):
        if len(progress) > 1:
            return []
        early.add(*done)
        step = early.steps - len(early.left[0])
        if step < early.steps:
            early.send(step)
            return early.sent
        progress.append(Spread(early.result(), nseq))
        return progress[1].sent

    def attend(pair, *ready):
        held = after(mask, *ready)
        return attend_backward(
            pair, held, ends, *projected, ctx_own, ctx_sib, dctx_own, dctx_far, seg_col, seg_row, lse, run
        )

    def weight_sums(near, far):
        matrix = (mm(x_own, near, TN) + mm(x_sib, far, TN)).astype(bf16)
        column = (jnp.sum(near.astype(f32), axis=0) + jnp.sum(far.astype(f32), axis=0)).astype(bf16)
        column = jnp.pad(column[None], ((0, 63), (0, 0)))
        column = jnp.broadcast_to(column, (planes,) + column.shape)
        return jnp.concatenate([matrix.reshape(planes, CORES * rows, -1), column], axis=1)

    grads = [attend(0, *early.sent)]
    for pair in range(1, pairs):
        sent = advance(grads[-1][0])
        grads.append(attend(pair, *sent, *(output if pair == 1 else ())))
    while len(progress) == 1:
        advance(grads[-1][0])
    early_sum = progress[1]

    near = jnp.concatenate([g[0] for g in grads], axis=1)
    far = jnp.concatenate([g[1] for g in grads], axis=1)
    grad_far = swap(mm(far, w_mine, NT).astype(bf16))
    early_sum.add(grads[-1][0])
    input_grad = (grad_one + mm(near, w_mine, NT) + grad_far.astype(f32)).astype(bf16)
    returned = [lax.ppermute(input_grad[i * run : (i + 1) * run], ("core", "seq"), back[i]) for i in range(2)]
    qkv_halves = Halving(after(weight_sums(near, far), input_grad), planes)
    for step in range(qkv_halves.steps):
        qkv_halves.send(step)
        qkv_halves.add(input_grad)
    qkv_sum = Spread(qkv_halves.result(), nseq)
    qkv_sum.add(*returned)
    input_grad = jnp.where(odd == 0, jnp.stack(returned), jnp.stack(returned[::-1]))[None].astype(f32)
    early_total = early_sum.result(qkv_sum.keep)
    qkv_total = qkv_sum.result()

    down_final = early_total[:down_rows].astype(f32)
    wide = [early_total[down_rows + i * rows : down_rows + (i + 1) * rows] for i in range(inner_blocks)]
    in_final = jnp.concatenate(wide, axis=1).astype(f32)
    at = down_rows + inner_blocks * rows
    out_final = early_total[at : at + rows].astype(f32)
    at = at + rows
    line = early_total[at : at + 32, :rows].astype(f32)
    out_bias_final, g1, b1, down_bias_final, g2, b2 = [line[i] for i in range(6)]
    in_bias_final = line[6 : 6 + inner].reshape(-1)

    part = qkv_total
    column = part[CORES * rows]
    other = swap(jnp.concatenate([lax.dynamic_slice_in_dim(part, (1 - core) * rows, rows, 0), part[CORES * rows : CORES * rows + 16]]))
    own_block = lax.dynamic_slice_in_dim(part, core * rows, rows, 0)
    spread_out = lambda v: jnp.moveaxis(v.reshape(-1, pairs, 3, LANES), 2, 1).reshape(-1, 3, 1, mine)
    qkv_final = either(core, spread_out(own_block), spread_out(other[:rows]), 2).reshape(rows, 3 * width).astype(f32)
    sums = either(core, spread_out(column), spread_out(other[rows]), 2).reshape(3, width)
    shard = lax.axis_index("xy") * CORES + core
    q_final = lax.dynamic_slice_in_dim(sums[0], shard * rows, rows, 0).astype(f32)
    v_final = lax.dynamic_slice_in_dim(sums[2], shard * rows, rows, 0).astype(f32)
    output = jnp.where(odd == 0, jnp.stack(output), jnp.stack(output[::-1]))[None]
    return (
        output, input_grad, qkv_final, q_final, v_final, out_final, out_bias_final, g1, b1, in_final,
        in_bias_final, down_final, down_bias_final, g2, b2,
    )


def solution(mesh):
    fsdp, nseq = mesh.shape["fsdp"], mesh.shape["seq"]
    fine = Mesh(mesh.devices.reshape(fsdp // CORES, CORES, nseq), ("xy", "core", "seq"))
    shard = ("xy", "core")
    stream, matrix, vector = P(shard, None, "seq", None), P(shard, None), P(shard)
    return jax.shard_map(
        per_device,
        mesh=fine,
        in_specs=(
            stream, P(shard, None, None), matrix, vector, vector, matrix, vector, vector, vector,
            matrix, vector, matrix, vector, vector, vector, stream,
        ),
        out_specs=(
            stream, stream, matrix, vector, vector, matrix, vector, vector, vector,
            matrix, vector, matrix, vector, vector, vector,
        ),
        check_vma=False,
    )
```

```python
import functools
import math

import jax
import jax.numpy as jnp
from jax import lax
from jax.experimental import pallas as pl
from jax.experimental.pallas import tpu as pltpu
from jax.sharding import Mesh
from jax.sharding import PartitionSpec as P

HEAD_DIM = 64
LANES = 128
NEG = -1e30
TILE = 256
VALUE_ROWS = HEAD_DIM + 16
KEY_TILES = 2
QUERY_TILES = 2
NT = (((1,), (1,)), ((), ()))
NN = (((1,), (0,)), ((), ()))
TN = (((0,), (0,)), ((), ()))


def mm(left, right, dims):
    return lax.dot_general(left, right, dims, preferred_element_type=jnp.float32)


def key_tiles(ends_ref, first, last, tile, total):
    low = jnp.int32(0)
    high = jnp.int32(total)
    for doc in reversed(range(ends_ref.shape[0])):
        end = ends_ref[doc]
        low = jnp.maximum(low, jnp.where(end <= first, end, 0))
        high = jnp.minimum(high, jnp.where(end > last, end, total))
    return low // tile, (high + tile - 1) // tile


def spans(first, after, count, tiles):
    steps = (after - first + count - 1) // count
    return jnp.minimum(first, tiles - steps * count), steps


def lane_halves(x, fill):
    lane = lax.broadcasted_iota(jnp.int32, x.shape, 1)
    fill = jnp.full_like(x, fill)
    return jnp.where(lane < HEAD_DIM, x, fill), jnp.where(lane < HEAD_DIM, fill, x)


def piece_copies(halves, columns, place, scratch, slot, sems, run, mask, inbound):
    copies = []
    pieces = halves[0].shape[0] // run
    for half, ref in enumerate(halves):
        for part in range(pieces):
            index = half * pieces + part
            natural = pl.multiple_of(jnp.bitwise_xor(mask, index) * run, run)
            outer = ref.at[pl.ds(part * run, run), pl.ds(columns, LANES)]
            inner = scratch.at[place, pl.ds(natural, run), :]
            ends = (outer, inner) if inbound else (inner, outer)
            copies.append(pltpu.make_async_copy(ends[0], ends[1], sems.at[slot, index]))
    return copies


def forward_kernel(run, mask_ref, ends_ref, own, sib, seg_col, seg_row, ctx_own, ctx_sib, lse_ref, qkv, out, turned, acc, top, sems, out_sems):
    total = qkv.shape[1]
    pairs = out.shape[0]
    mask = mask_ref[0]

    def loads(pair):
        copies = []
        for kind in range(3):
            copies += piece_copies(
                (own, sib), (3 * pair + kind) * LANES, kind * pairs + pair, qkv, kind * pairs + pair, sems, run, mask, True
            )
        return copies

    for pair in range(pairs):
        for copy in loads(pair):
            copy.start()

    for head in range(2 * pairs):
        turned[head, HEAD_DIM:, :] = jnp.ones((VALUE_ROWS - HEAD_DIM, total), jnp.bfloat16)
    for pair in range(pairs):
        for copy in loads(pair):
            copy.wait()
    heads = [(pair, head) for pair in range(pairs) for head in range(2)]
    if True:

        @pl.loop(0, total // TILE)
        def _(block):
            rows = pl.multiple_of(block * TILE, TILE)
            for pair in range(pairs):
                values = qkv[2 * pairs + pair, pl.ds(rows, TILE), :].astype(jnp.float32).T.astype(jnp.bfloat16)
                for head in range(2):
                    turned[2 * pair + head, :HEAD_DIM, pl.ds(rows, TILE)] = values[head * HEAD_DIM : (head + 1) * HEAD_DIM]

        @pl.loop(0, total // TILE)
        def _(block):
            rows = pl.multiple_of(block * TILE, TILE)
            q_heads = sum([list(lane_halves(qkv[pair, pl.ds(rows, TILE), :], 0.0)) for pair in range(pairs)], [])
            segq = seg_row[:, pl.ds(rows, TILE)]
            first, after = key_tiles(ends_ref, rows, rows + TILE - 1, TILE, total)
            acc[...] = jnp.zeros_like(acc)
            top[...] = jnp.full_like(top, NEG)

            first, steps = spans(first, after, KEY_TILES, total // TILE)

            @pl.loop(0, steps)
            def _(step):
                at = pl.multiple_of((first + step * KEY_TILES) * TILE, TILE)
                keys = [qkv[pairs + pair, pl.ds(at, KEY_TILES * TILE), :] for pair in range(pairs)]
                segk = seg_col[pl.ds(at, KEY_TILES * TILE), :]
                same = jnp.concatenate([segk] * (TILE // LANES), axis=1) == segq
                for head in range(2 * pairs):
                    scores = jnp.where(same, mm(keys[head // 2], q_heads[head], NT), NEG)
                    old = top[head, 0:1]
                    new = jnp.maximum(old, jnp.max(scores, axis=0, keepdims=True))
                    probs = jnp.exp(scores - new).astype(jnp.bfloat16)
                    acc[head] = acc[head] * jnp.exp(old - new) + mm(turned[head, :, pl.ds(at, KEY_TILES * TILE)], probs, NN)
                    top[head] = jnp.broadcast_to(new, (8, TILE))

            for pair in range(pairs):
                parts = []
                for head in (2 * pair, 2 * pair + 1):
                    weight = acc[head, HEAD_DIM : HEAD_DIM + 1]
                    parts.append(acc[head, :HEAD_DIM] / weight)
                    lse_ref[head, :, pl.ds(rows, TILE)] = top[head] + jnp.log(acc[head, HEAD_DIM : HEAD_DIM + 8])
                out[pair, pl.ds(rows, TILE), :] = jnp.concatenate(parts, axis=0).T.astype(jnp.bfloat16)

    for pair in range(pairs):
        for copy in piece_copies((ctx_own, ctx_sib), pair * LANES, pair, out, pair, out_sems, run, mask, False):
            copy.start()
    for pair in range(pairs):
        for copy in piece_copies((ctx_own, ctx_sib), pair * LANES, pair, out, pair, out_sems, run, mask, False):
            copy.wait()


def attend_forward(mask, ends, own, sib, seg_col, seg_row, run):
    half, columns = own.shape
    total = 2 * half
    pairs = columns // (3 * LANES)
    pieces = total // run
    any_spec = pl.BlockSpec(memory_space=pl.ANY)
    vmem = pl.BlockSpec(memory_space=pltpu.VMEM)
    smem = pl.BlockSpec(memory_space=pltpu.SMEM)
    return pl.pallas_call(
        functools.partial(forward_kernel, run),
        out_shape=(
            jax.ShapeDtypeStruct((half, pairs * LANES), jnp.bfloat16),
            jax.ShapeDtypeStruct((half, pairs * LANES), jnp.bfloat16),
            jax.ShapeDtypeStruct((2 * pairs, 8, total), jnp.float32),
        ),
        in_specs=[smem, smem, any_spec, any_spec, vmem, vmem],
        out_specs=(any_spec, any_spec, vmem),
        scratch_shapes=[
            pltpu.VMEM((3 * pairs, total, LANES), jnp.bfloat16),
            pltpu.VMEM((pairs, total, LANES), jnp.bfloat16),
            pltpu.VMEM((2 * pairs, VALUE_ROWS, total), jnp.bfloat16),
            pltpu.VMEM((2 * pairs, VALUE_ROWS, TILE), jnp.float32),
            pltpu.VMEM((2 * pairs, 8, TILE), jnp.float32),
            pltpu.SemaphoreType.DMA((3 * pairs, pieces)),
            pltpu.SemaphoreType.DMA((pairs, pieces)),
        ],
        compiler_params=pltpu.CompilerParams(vmem_limit_bytes=40 << 20),
        cost_estimate=pl.CostEstimate(flops=1_000_000_000, bytes_accessed=1_000_000, transcendentals=0),
        name="attend_forward",
    )(mask, ends, own, sib, seg_col, seg_row)


def backward_kernel(
    run, pair, mask_ref, ends_ref, own, sib, ctx_own, ctx_sib, dctx_own, dctx_sib, seg_col, seg_row, lse_ref,
    d_own, d_sib, qkv, ctx, out, turned, delta, dq, dkv, sems, out_sems
):
    total = qkv.shape[1]
    mask = mask_ref[0]
    loads, stores = [], []
    for kind in range(3):
        loads += piece_copies((own, sib), (3 * pair + kind) * LANES, kind, qkv, kind, sems, run, mask, True)
        stores += piece_copies((d_own, d_sib), kind * LANES, kind, out, kind, out_sems, run, mask, False)
    loads += piece_copies((ctx_own, ctx_sib), pair * LANES, 0, ctx, 3, sems, run, mask, True)
    loads += piece_copies((dctx_own, dctx_sib), pair * LANES, 1, ctx, 4, sems, run, mask, True)
    for copy in loads:
        copy.start()
    for copy in loads:
        copy.wait()

    @pl.loop(0, total // TILE)
    def _(block):
        rows = pl.multiple_of(block * TILE, TILE)
        product = ctx[0, pl.ds(rows, TILE), :].astype(jnp.float32) * ctx[1, pl.ds(rows, TILE), :].astype(jnp.float32)
        product = product.T
        for head in range(2):
            part = jnp.sum(product[head * HEAD_DIM : (head + 1) * HEAD_DIM], axis=0, keepdims=True)
            delta[head, :, pl.ds(rows, TILE)] = jnp.broadcast_to(part, (8, TILE))
        turned[:, pl.ds(rows, TILE)] = qkv[1, pl.ds(rows, TILE), :].astype(jnp.float32).T.astype(jnp.bfloat16)
        dq[:, pl.ds(rows, TILE)] = jnp.zeros((LANES, TILE), jnp.float32)

    @pl.loop(0, total // TILE)
    def _(block):
        rows = pl.multiple_of(block * TILE, TILE)
        k_heads = lane_halves(qkv[1, pl.ds(rows, TILE), :], 0.0)
        v_heads = lane_halves(qkv[2, pl.ds(rows, TILE), :], 0.0)
        segk = seg_col[pl.ds(rows, TILE), :]
        segk = jnp.concatenate([segk] * (TILE // LANES), axis=1)
        first, after = key_tiles(ends_ref, rows, rows + TILE - 1, TILE, total)
        dkv[...] = jnp.zeros_like(dkv)

        first, steps = spans(first, after, QUERY_TILES, total // TILE)

        @pl.loop(0, steps)
        def _(step):
            at = pl.multiple_of((first + step * QUERY_TILES) * TILE, TILE)
            span = pl.ds(at, QUERY_TILES * TILE)
            queries = qkv[0, span, :]
            grads = ctx[1, span, :]
            q_heads = lane_halves(queries, 0.0)
            g_heads = lane_halves(grads, 0.0)
            same = jnp.concatenate([segk] * QUERY_TILES, axis=1) == seg_row[:, span]
            for head in range(2):
                scores = mm(k_heads[head], queries, NT)
                probs = jnp.exp(jnp.where(same, scores - lse_ref[2 * pair + head, 0:1, span], NEG))
                dprobs = mm(v_heads[head], grads, NT)
                dscores = (probs * (dprobs - delta[head, 0:1, span])).astype(jnp.bfloat16)
                dkv[1] += mm(probs.astype(jnp.bfloat16), g_heads[head], NN)
                dkv[0] += mm(dscores, q_heads[head], NN)
                lanes = slice(head * HEAD_DIM, (head + 1) * HEAD_DIM)
                dq[lanes, span] += mm(turned[lanes, pl.ds(rows, TILE)], dscores, NN)

        out[1, pl.ds(rows, TILE), :] = dkv[0].astype(jnp.bfloat16)
        out[2, pl.ds(rows, TILE), :] = dkv[1].astype(jnp.bfloat16)

    @pl.loop(0, total // TILE)
    def _(block):
        rows = pl.multiple_of(block * TILE, TILE)
        out[0, pl.ds(rows, TILE), :] = (dq[:, pl.ds(rows, TILE)].T * HEAD_DIM**-0.5).astype(jnp.bfloat16)

    for copy in stores:
        copy.start()
    for copy in stores:
        copy.wait()


def attend_backward(pair, mask, ends, own, sib, ctx_own, ctx_sib, dctx_own, dctx_sib, seg_col, seg_row, lse, run):
    half = own.shape[0]
    total = 2 * half
    pieces = total // run
    any_spec = pl.BlockSpec(memory_space=pl.ANY)
    vmem = pl.BlockSpec(memory_space=pltpu.VMEM)
    smem = pl.BlockSpec(memory_space=pltpu.SMEM)
    return pl.pallas_call(
        functools.partial(backward_kernel, run, pair),
        out_shape=(
            jax.ShapeDtypeStruct((half, 3 * LANES), jnp.bfloat16),
            jax.ShapeDtypeStruct((half, 3 * LANES), jnp.bfloat16),
        ),
        in_specs=[smem, smem] + [any_spec] * 6 + [vmem] * 3,
        out_specs=(any_spec, any_spec),
        scratch_shapes=[
            pltpu.VMEM((3, total, LANES), jnp.bfloat16),
            pltpu.VMEM((2, total, LANES), jnp.bfloat16),
            pltpu.VMEM((3, total, LANES), jnp.bfloat16),
            pltpu.VMEM((LANES, total), jnp.bfloat16),
            pltpu.VMEM((2, 8, total), jnp.float32),
            pltpu.VMEM((LANES, total), jnp.float32),
            pltpu.VMEM((2, TILE, LANES), jnp.float32),
            pltpu.SemaphoreType.DMA((5, pieces)),
            pltpu.SemaphoreType.DMA((3, pieces)),
        ],
        compiler_params=pltpu.CompilerParams(vmem_limit_bytes=24 << 20),
        cost_estimate=pl.CostEstimate(flops=20_000_000_000, bytes_accessed=8_000_000, transcendentals=0),
        name=f"attend_backward_{pair}",
    )(mask, ends, own, sib, ctx_own, ctx_sib, dctx_own, dctx_sib, seg_col, seg_row, lse)


EPS = 1e-05


def norm_forward(resid, gain, shift):
    mean = jnp.mean(resid, axis=-1, keepdims=True)
    centered = resid - mean
    inv = lax.rsqrt(jnp.mean(centered * centered, axis=-1, keepdims=True) + EPS)
    normed = centered * inv
    return (normed * gain + shift, normed, inv)


def norm_backward(grad, normed, inv, gain):
    scaled = grad * gain
    return inv * (
        scaled
        - jnp.mean(scaled, axis=-1, keepdims=True)
        - normed * jnp.mean(scaled * normed, axis=-1, keepdims=True)
    )


ROWS = 256
CHUNK = 768


def fold(x):
    return jnp.sum(x.reshape(-1, 8, x.shape[1]), axis=0)


def middle_kernel(
    core_ref, x_ref, near_ref, far_ref, cot_ref, vec_ref, in_bias_ref, packed,
    result_ref, low_ref, act_ref, grad_down_ref, grad_pre_ref, grad_one_ref, grad_attn_ref, dnear_ref, dfar_ref,
    sums_ref, in_sums_ref, wo, wi, wd, slope, acc, sums, in_sums, sems
):
    f32, bf16 = jnp.float32, jnp.bfloat16
    mine = near_ref.shape[1]
    chunks = wi.shape[0]
    step = pl.program_id(0)
    core = core_ref[0]
    shards = packed.shape[0]
    rows = packed.shape[1] // (2 * chunks + 1)
    copies = []

    def load(shard, at, count, target):
        copies.append(pltpu.make_async_copy(packed.at[shard, pl.ds(at, count), :], target, sems.at[len(copies)]))

    if shards == 1:
        for place in range(2):
            which = core if place == 0 else 1 - core
            load(0, pl.multiple_of(2 * chunks * rows + which * mine, 16), mine, wo.at[pl.ds(place * mine, mine), :])
    else:
        for place in range(2):
            which = core if place == 0 else 1 - core
            for part in range(shards // 2):
                target = wo.at[pl.ds(place * mine + part * rows, rows), :]
                load(which * (shards // 2) + part, 2 * chunks * rows, rows, target)
    outs = len(copies)
    for chunk in range(chunks):
        for shard in range(shards):
            load(shard, (chunks + chunk) * rows, rows, wi.at[chunk, pl.ds(shard * rows, rows), :])
    for chunk in range(chunks):
        for shard in range(shards):
            first = shard * chunks * rows
            low, high = max(first, chunk * CHUNK), min(first + chunks * rows, (chunk + 1) * CHUNK)
            if low < high:
                load(shard, low - first, high - low, wd.at[chunk, pl.ds(low - chunk * CHUNK, high - low), :])

    @pl.when(step == 0)
    def _():
        for copy in copies:
            copy.start()
        sums[...] = jnp.zeros_like(sums)
        in_sums[...] = jnp.zeros_like(in_sums)
        for copy in copies[:outs]:
            copy.wait()

    bias_out, gain_one, shift_one, bias_down, gain_two, shift_two = [vec_ref[i : i + 1, :] for i in range(6)]
    near, far = near_ref[...], far_ref[...]
    attn = mm(near, wo[:mine], NN) + mm(far, wo[mine:], NN) + bias_out
    hidden, normed_one, inv_one = norm_forward(x_ref[...].astype(f32) + attn, gain_one, shift_one)
    low_ref[...] = hidden.astype(bf16)
    acc[...] = hidden + bias_down

    @pl.when(step == 0)
    def _():
        for copy in copies[outs:]:
            copy.wait()

    @pl.loop(0, chunks)
    def _(chunk):
        columns = pl.ds(pl.multiple_of(chunk * CHUNK, CHUNK), CHUNK)
        pre = mm(low_ref[...], wi[chunk], NN) + in_bias_ref[:, columns]
        cdf = 0.5 * (1.0 + lax.erf(pre * (1.0 / math.sqrt(2.0))))
        density = jnp.exp(-0.5 * pre * pre) * (1.0 / math.sqrt(2.0 * math.pi))
        act = (pre * cdf).astype(bf16)
        act_ref[:, columns] = act
        slope[:, columns] = cdf + pre * density
        acc[...] += mm(act, wd[chunk], NN)

    result, normed_two, inv_two = norm_forward(acc[...], gain_two, shift_two)
    result_ref[...] = result.astype(bf16)
    dy = cot_ref[...].astype(f32)
    grad_two = norm_backward(dy, normed_two, inv_two, gain_two)
    grad_down = grad_two.astype(bf16)
    grad_down_ref[...] = grad_down
    sums[3] += fold(grad_down.astype(f32))
    sums[4] += fold(dy * normed_two)
    sums[5] += fold(dy)
    acc[...] = grad_two

    @pl.loop(0, chunks)
    def _(chunk):
        columns = pl.ds(pl.multiple_of(chunk * CHUNK, CHUNK), CHUNK)
        grad_pre = (mm(grad_down_ref[...], wd[chunk], NT) * slope[:, columns]).astype(bf16)
        grad_pre_ref[:, columns] = grad_pre
        in_sums[:, columns] += fold(grad_pre.astype(f32))
        acc[...] += mm(grad_pre, wi[chunk], NT)

    grad_hidden = acc[...]
    sums[1] += fold(grad_hidden * normed_one)
    sums[2] += fold(grad_hidden)
    grad_one = norm_backward(grad_hidden, normed_one, inv_one, gain_one)
    grad_one_ref[...] = grad_one
    grad_attn = grad_one.astype(bf16)
    grad_attn_ref[...] = grad_attn
    sums[0] += fold(grad_attn.astype(f32))
    dnear_ref[...] = mm(grad_attn, wo[:mine], NT).astype(bf16)
    dfar_ref[...] = mm(grad_attn, wo[mine:], NT).astype(bf16)

    @pl.when(step == pl.num_programs(0) - 1)
    def _():
        sums_ref[...] = jnp.zeros_like(sums_ref)
        for i in range(6):
            sums_ref[i : i + 1, :] = jnp.sum(sums[i], axis=0, keepdims=True)
        in_sums_ref[...] = jnp.sum(in_sums[...], axis=0, keepdims=True)


def middle(core, x, near, far, cot, vec, in_bias, packed):
    count, width = x.shape
    hidden = in_bias.shape[1]
    mine = near.shape[1]
    chunks = hidden // CHUNK
    f32, bf16 = jnp.float32, jnp.bfloat16
    any_spec = pl.BlockSpec(memory_space=pl.ANY)
    block = lambda columns: pl.BlockSpec((ROWS, columns), lambda i: (i, 0))
    whole = lambda rows, columns: pl.BlockSpec((rows, columns), lambda i: (0, 0))
    shape = jax.ShapeDtypeStruct
    return pl.pallas_call(
        middle_kernel,
        grid=(count // ROWS,),
        out_shape=(
            shape((count, width), bf16), shape((count, width), bf16), shape((count, hidden), bf16),
            shape((count, width), bf16), shape((count, hidden), bf16), shape((count, width), f32),
            shape((count, width), bf16), shape((count, mine), bf16), shape((count, mine), bf16),
            shape((8, width), f32), shape((1, hidden), f32),
        ),
        in_specs=[
            pl.BlockSpec(memory_space=pltpu.SMEM), block(width), block(mine), block(mine), block(width),
            whole(8, width), whole(1, hidden), any_spec,
        ],
        out_specs=(
            block(width), block(width), block(hidden), block(width), block(hidden), block(width), block(width),
            block(mine), block(mine), whole(8, width), whole(1, hidden),
        ),
        scratch_shapes=[
            pltpu.VMEM((width, width), bf16),
            pltpu.VMEM((chunks, width, CHUNK), bf16),
            pltpu.VMEM((chunks, CHUNK, width), bf16),
            pltpu.VMEM((ROWS, hidden), f32),
            pltpu.VMEM((ROWS, width), f32),
            pltpu.VMEM((6, 8, width), f32),
            pltpu.VMEM((8, hidden), f32),
            pltpu.SemaphoreType.DMA(((2 * chunks + 1) * max(packed.shape[0], 2),)),
        ],
        compiler_params=pltpu.CompilerParams(vmem_limit_bytes=48 << 20),
        cost_estimate=pl.CostEstimate(flops=20_000_000_000, bytes_accessed=30_000_000, transcendentals=0),
        name="middle",
    )(core, x, near, far, cot, vec, in_bias, packed)


def gradients_kernel(
    rows, core_ref, act_ref, low_ref, down_ref, pre_ref, near_ref, far_ref, attn_ref, vec_ref,
    keep_ref, send_ref, result, sems
):
    step = pl.program_id(0)
    core = core_ref[0]
    shards = low_ref.shape[1] // rows
    chunks = (pl.num_programs(0) - 1) // 2
    blocks = pre_ref.shape[1] * chunks // low_ref.shape[1]
    slot = step % 2

    def wait(which):
        pltpu.make_async_copy(result.at[which], result.at[which], sems.at[which]).wait()

    def put(source, shard_core, plane, at, count, sem):
        target = pl.ds(at, count)

        @pl.when(core == shard_core)
        def _():
            pltpu.make_async_copy(source, keep_ref.at[plane, target, :], sem).start()

        @pl.when(core != shard_core)
        def _():
            pltpu.make_async_copy(source, send_ref.at[plane, target, :], sem).start()

    @pl.when(step >= 2)
    def _():
        wait(slot)

    @pl.when(step < chunks)
    def _():
        result[slot] = mm(act_ref[...], down_ref[...], TN).astype(jnp.bfloat16)
        count = blocks * rows
        here = result.shape[1] // count
        for part in range(here):
            put(result.at[slot, pl.ds(part * count, count), :], part % CORES, step * (here // CORES) + part // CORES, 0, count, sems.at[slot])

    @pl.when(jnp.logical_and(step >= chunks, step < 2 * chunks))
    def _():
        result[slot] = mm(low_ref[...], pre_ref[...], TN).astype(jnp.bfloat16)
        at = pl.multiple_of(blocks * rows + (step - chunks) * rows, 16)
        for shard in range(shards):
            put(result.at[slot, pl.ds(shard * rows, rows), :], shard % CORES, shard // CORES, at, rows, sems.at[slot])

    @pl.when(step == 2 * chunks)
    def _():
        mine = near_ref.shape[1]
        result[slot, :mine] = mm(near_ref[...], attn_ref[...], TN).astype(jnp.bfloat16)
        result[slot, mine:] = mm(far_ref[...], attn_ref[...], TN).astype(jnp.bfloat16)
        half = shards // 2
        for shard in range(shards):
            first = core if shard < half else 1 - core
            plane = first * (half // CORES) + (shard % half) // CORES
            put(result.at[slot, pl.ds(shard * rows, rows), :], shard % CORES, plane, 2 * blocks * rows, rows, sems.at[slot])
        for shard in range(shards):
            put(vec_ref.at[shard], shard % CORES, shard // CORES, (2 * blocks + 1) * rows, vec_ref.shape[1], sems.at[2 + shard])
        wait(0)
        wait(1)
        for shard in range(shards):
            pltpu.make_async_copy(vec_ref.at[shard], vec_ref.at[shard], sems.at[2 + shard]).wait()


def gradients(core, act, low, down, pre, near, far, attn, vec, planes):
    count, width = low.shape
    rows = width // (planes * CORES)
    chunks = pre.shape[1] // width
    total_rows = (2 * chunks + 1) * rows + vec.shape[1]
    whole = lambda x: pl.BlockSpec(x.shape, lambda i: (0,) * x.ndim)
    out = jax.ShapeDtypeStruct((planes, total_rows, width), jnp.bfloat16)
    return pl.pallas_call(
        functools.partial(gradients_kernel, rows),
        grid=(2 * chunks + 1,),
        out_shape=(out, out),
        in_specs=[
            pl.BlockSpec(memory_space=pltpu.SMEM),
            pl.BlockSpec((count, width), lambda i: (0, jnp.minimum(i, chunks - 1))),
            whole(low), whole(down),
            pl.BlockSpec((count, width), lambda i: (0, jnp.clip(i - chunks, 0, chunks - 1))),
            whole(near), whole(far), whole(attn), whole(vec),
        ],
        out_specs=(pl.BlockSpec(memory_space=pl.ANY),) * 2,
        scratch_shapes=[
            pltpu.VMEM((2, width, width), jnp.bfloat16),
            pltpu.SemaphoreType.DMA((2 + planes * CORES,)),
        ],
        compiler_params=pltpu.CompilerParams(vmem_limit_bytes=48 << 20),
        cost_estimate=pl.CostEstimate(flops=11_000_000_000, bytes_accessed=30_000_000, transcendentals=0),
        name="gradients",
    )(core, act, low, down, pre, near, far, attn, vec)


def doc_ids(ends, count):
    places = jnp.arange(count, dtype=jnp.int32)
    return jnp.sum((places[:, None] >= ends[None, :]).astype(jnp.int32), axis=1)


CORES = 2


def routes(nseq):
    first, second = [], []
    for core in range(CORES):
        for z in range(nseq):
            source = core * nseq + z
            first.append((source, (z // 2) * nseq + 2 * core + z % 2))
            second.append((source, (z // 2) * nseq + 2 * core + 1 - z % 2))
    return first, second


def swap(x):
    return lax.ppermute(x, "core", [(0, 1), (1, 0)])


def after(value, *done):
    return lax.optimization_barrier((value, done))[0]


def pick(value, which, axis=0):
    return lax.dynamic_index_in_dim(value, which, axis, keepdims=False)


def total(keep, received):
    return (keep.astype(jnp.float32) + received.astype(jnp.float32)).astype(jnp.bfloat16)


class Halving:
    def __init__(self, blocks, planes):
        bits = planes.bit_length() - 1
        rows = blocks.shape[1]
        self.planes = planes
        self.orders = (list(range(bits)), list(range(bits))[::-1])
        self.left = [list(range(bits))[::-1] for _ in range(2)]
        parts = (blocks[:, : rows // 2], blocks[:, rows // 2 :])
        self.parts = [p.reshape((2,) * bits + p.shape[1:]) for p in parts]
        self.steps = bits

    def send(self, step):
        place = lax.axis_index("xy")
        self.keep, self.received, self.sent = [], [], []
        for half in range(2):
            bit = self.orders[half][step]
            axis = self.left[half].index(bit)
            mine = (place >> bit) % 2
            self.left[half].remove(bit)
            out = pick(self.parts[half], 1 - mine, axis)
            self.keep.append(pick(self.parts[half], mine, axis))
            self.sent.append(out)
            self.received.append(lax.ppermute(out, "xy", [(i, i ^ (1 << bit)) for i in range(self.planes)]))

    def add(self, *done):
        self.parts = [total(k, after(r, *done)) for k, r in zip(self.keep, self.received)]

    def result(self):
        return jnp.concatenate(self.parts)


class Spread:
    def __init__(self, value, nseq):
        self.nseq, self.rows = nseq, value.shape[0] // nseq
        self.me = lax.axis_index("seq")
        quarter = lambda which: lax.dynamic_slice_in_dim(value, (which % nseq) * self.rows, self.rows, 0)
        self.keep = quarter(self.me)
        self.sent = [quarter(self.me + d) for d in range(1, nseq)]
        self.received = [self.shift(q, d) for d, q in enumerate(self.sent, 1)]

    def shift(self, value, distance):
        return lax.ppermute(value, "seq", [(i, (i + distance) % self.nseq) for i in range(self.nseq)])

    def add(self, *done):
        parts = [self.keep] + [after(r, *done) for r in self.received]
        self.keep = sum(p.astype(jnp.float32) for p in parts).astype(jnp.bfloat16)
        self.received = [self.shift(self.keep, d) for d in range(1, self.nseq)]

    def result(self, *done):
        whole = jnp.zeros((self.nseq * self.rows,) + self.keep.shape[1:], jnp.bfloat16)
        for d, part in enumerate([self.keep] + [after(r, *done) for r in self.received]):
            start = ((self.me - d) % self.nseq) * self.rows
            whole = lax.dynamic_update_slice_in_dim(whole, part, start, 0)
        return whole


def either(core, own, other, axis):
    return jnp.where(core == 0, jnp.concatenate([own, other], axis), jnp.concatenate([other, own], axis))


def per_device(
    tokens, doc_lengths, qkv_weight, q_bias, v_bias, out_weight, out_bias, norm1_gain, norm1_bias,
    ff_in_weight, ff_in_bias, ff_out_weight, ff_out_bias, norm2_gain, norm2_bias, out_cotangent,
):
    bf16, f32 = jnp.bfloat16, jnp.float32
    fsdp = ("xy", "core")
    nseq = lax.axis_size("seq")
    planes = lax.axis_size("xy")
    shards = planes * CORES
    core = lax.axis_index("core")
    odd = lax.axis_index("seq") % 2
    micro, run, width = tokens.shape[1:]
    assert micro == 2 and nseq == 4
    stretch = run * nseq
    mine = width // CORES
    rows = width // shards
    first, second = routes(nseq)
    back = [[(b, a) for a, b in route] for route in (first, second)]

    def spread(x):
        halves = [lax.dynamic_index_in_dim(x[0], which, 0, keepdims=False) for which in (odd, 1 - odd)]
        return [lax.ppermute(h, ("core", "seq"), r) for h, r in zip(halves, (first, second))]

    pieces = spread(tokens)
    lengths = jnp.stack([doc_lengths[0], swap(doc_lengths[0])])
    z = lax.axis_index("seq")
    theirs = jnp.where(z // 2 == core, lengths[0], lengths[1])
    ends = jnp.cumsum(lax.dynamic_index_in_dim(theirs, odd, 0, keepdims=False)).astype(jnp.int32)
    seg = doc_ids(ends, stretch)
    seg_col = jnp.broadcast_to(seg[:, None], (stretch, LANES))
    seg_row = seg[None]
    mask = (odd + 2 * core).astype(jnp.int32)[None]

    pairs = mine // LANES
    own_columns = qkv_weight.reshape(rows, 3, CORES, pairs, LANES)
    own_columns = jnp.moveaxis(own_columns, (2, 3), (0, 2)).reshape(CORES, rows, 3 * mine)
    kept = pick(own_columns, core)
    w_mine = either(core, kept, swap(pick(own_columns, 1 - core)), 0)
    w_mine = lax.all_gather(w_mine, "xy", axis=0, tiled=True)
    small = [q_bias, v_bias, out_bias, norm1_gain, norm1_bias, ff_out_bias, norm2_gain, norm2_bias]
    inner = ff_in_bias.shape[0] // rows
    small = jnp.concatenate([jnp.stack(small), ff_in_bias.reshape(inner, rows)])
    vectors = lax.all_gather(small, fsdp, axis=0, tiled=False).astype(f32)
    bias_in = vectors[:, 8:].reshape(1, -1)
    vectors = jnp.moveaxis(vectors[:, :8], 0, 1).reshape(8, width)
    bias_q, bias_v = vectors[0], vectors[1]
    norms = jnp.concatenate([vectors[2:], jnp.zeros((2, width), f32)])
    wide = [ff_in_weight[:, i * width : (i + 1) * width] for i in range(inner)]
    packed = lax.all_gather(jnp.concatenate([ff_out_weight] + wide + [out_weight]), fsdp, axis=0, tiled=False)
    if rows % 16:
        parts = [packed[:, : inner * rows].reshape(-1, width)]
        parts += [packed[:, (inner + i) * rows : (inner + i + 1) * rows].reshape(width, width) for i in range(inner + 1)]
        packed = jnp.concatenate(parts)[None]

    own_slice = lambda v: lax.dynamic_slice_in_dim(v, core * mine, mine, 0).reshape(pairs, LANES)
    one = jnp.ones((pairs, LANES), f32)
    bias_mine = jnp.stack([own_slice(bias_q), 0.0 * one, own_slice(bias_v)], axis=1).reshape(-1)
    scale = jnp.stack([HEAD_DIM**-0.5 * one, one, one], axis=1).reshape(-1)
    x_own = after(jnp.concatenate(pieces), norms, bias_in)
    x_sib = jnp.concatenate([swap(p) for p in pieces])
    projected = [((mm(x, w_mine, NN) + bias_mine) * scale).astype(bf16) for x in (x_own, x_sib)]
    ctx_own, ctx_sib, lse = attend_forward(mask, ends, *projected, seg_col, seg_row, run)
    ctx_far = swap(ctx_sib)

    cot = jnp.concatenate(spread(after(out_cotangent, *projected)))
    result, hidden_low, act_low, grad_down, grad_pre, grad_one, grad_attn, dctx_own, dctx_far, sums, in_sums = middle(
        core.astype(jnp.int32)[None], x_own, ctx_own, ctx_far, cot, norms, bias_in, packed
    )
    dctx_far = swap(dctx_far)
    output = [lax.ppermute(result[i * run : (i + 1) * run], ("core", "seq"), back[i]) for i in range(2)]

    def cores(blocks):
        return pick(blocks, core, 1), swap(pick(blocks, 1 - core, 1))

    inner_blocks = ff_in_bias.shape[0] * shards // width
    down_rows = ff_out_weight.shape[0]
    vector = [jnp.moveaxis(sums[:6].reshape(6, shards, rows), 1, 0), in_sums.reshape(shards, inner, rows)]
    vector = jnp.concatenate(vector, axis=1).astype(bf16)
    vector = jnp.pad(vector, ((0, 0), (0, 32 - vector.shape[1]), (0, width - rows)))
    if rows % 16 == 0:
        kept, sent = gradients(
            core.astype(jnp.int32)[None], act_low, hidden_low, grad_down, grad_pre, ctx_own, ctx_far, grad_attn, vector, planes
        )
        joined = kept, swap(sent)
    else:
        down_grad = cores(mm(act_low, grad_down, TN).astype(bf16).reshape(planes, CORES, -1, width))
        in_grad = cores(mm(hidden_low, grad_pre, TN).astype(bf16).reshape(planes, CORES, rows, -1))
        out_grad = [mm(c, grad_attn, TN).astype(bf16) for c in (ctx_own, ctx_far)]
        out_grad = cores(either(core, *out_grad, 0).reshape(planes, CORES, rows, width))
        vector = cores(vector.reshape(planes, CORES, 32, width))
        joined = []
        for which in range(2):
            wide = in_grad[which]
            wide = [wide[:, :, i * width : (i + 1) * width] for i in range(inner_blocks)]
            joined.append(jnp.concatenate([down_grad[which]] + wide + [out_grad[which], vector[which]], axis=1))
    early = Halving(total(*joined), planes)
    early.send(0)
    progress = [early]

    def advance(*done):
        if len(progress) > 1:
            return []
        early.add(*done)
        step = early.steps - len(early.left[0])
        if step < early.steps:
            early.send(step)
            return early.sent
        progress.append(Spread(early.result(), nseq))
        return progress[1].sent

    def attend(pair, *ready):
        held = after(mask, *ready)
        return attend_backward(
            pair, held, ends, *projected, ctx_own, ctx_sib, dctx_own, dctx_far, seg_col, seg_row, lse, run
        )

    def weight_sums(near, far):
        matrix = (mm(x_own, near, TN) + mm(x_sib, far, TN)).astype(bf16)
        column = (jnp.sum(near.astype(f32), axis=0) + jnp.sum(far.astype(f32), axis=0)).astype(bf16)
        column = jnp.pad(column[None], ((0, 63), (0, 0)))
        column = jnp.broadcast_to(column, (planes,) + column.shape)
        return jnp.concatenate([matrix.reshape(planes, CORES * rows, -1), column], axis=1)

    grads = [attend(0, *early.sent)]
    for pair in range(1, pairs):
        sent = advance(grads[-1][0])
        if pair == pairs - 1:
            output = [after(o, grads[-1][0]) for o in output]
            sent = list(sent) + output
        grads.append(attend(pair, *sent))
    while len(progress) == 1:
        advance(grads[-1][0])
    early_sum = progress[1]

    near = jnp.concatenate([g[0] for g in grads], axis=1)
    far = jnp.concatenate([g[1] for g in grads], axis=1)
    grad_far = swap(mm(far, w_mine, NT).astype(bf16))
    early_sum.add(grads[-1][0])
    input_grad = (grad_one + mm(near, w_mine, NT) + grad_far.astype(f32)).astype(bf16)
    returned = [lax.ppermute(input_grad[i * run : (i + 1) * run], ("core", "seq"), back[i]) for i in range(2)]
    qkv_halves = Halving(after(weight_sums(near, far), input_grad), planes)
    for step in range(qkv_halves.steps):
        qkv_halves.send(step)
        qkv_halves.add(input_grad)
    qkv_sum = Spread(qkv_halves.result(), nseq)
    qkv_sum.add(*returned)
    input_grad = jnp.where(odd == 0, jnp.stack(returned), jnp.stack(returned[::-1]))[None].astype(f32)
    early_total = early_sum.result(qkv_sum.keep)
    qkv_total = qkv_sum.result()

    down_final = early_total[:down_rows].astype(f32)
    wide = [early_total[down_rows + i * rows : down_rows + (i + 1) * rows] for i in range(inner_blocks)]
    in_final = jnp.concatenate(wide, axis=1).astype(f32)
    at = down_rows + inner_blocks * rows
    out_final = early_total[at : at + rows].astype(f32)
    at = at + rows
    line = early_total[at : at + 32, :rows].astype(f32)
    out_bias_final, g1, b1, down_bias_final, g2, b2 = [line[i] for i in range(6)]
    in_bias_final = line[6 : 6 + inner].reshape(-1)

    part = qkv_total
    column = part[CORES * rows]
    other = swap(jnp.concatenate([lax.dynamic_slice_in_dim(part, (1 - core) * rows, rows, 0), part[CORES * rows : CORES * rows + 16]]))
    own_block = lax.dynamic_slice_in_dim(part, core * rows, rows, 0)
    spread_out = lambda v: jnp.moveaxis(v.reshape(-1, pairs, 3, LANES), 2, 1).reshape(-1, 3, 1, mine)
    qkv_final = either(core, spread_out(own_block), spread_out(other[:rows]), 2).reshape(rows, 3 * width).astype(f32)
    sums = either(core, spread_out(column), spread_out(other[rows]), 2).reshape(3, width)
    shard = lax.axis_index("xy") * CORES + core
    q_final = lax.dynamic_slice_in_dim(sums[0], shard * rows, rows, 0).astype(f32)
    v_final = lax.dynamic_slice_in_dim(sums[2], shard * rows, rows, 0).astype(f32)
    output = [after(o, qkv_sum.keep) for o in output]
    output = jnp.where(odd == 0, jnp.stack(output), jnp.stack(output[::-1]))[None]
    return (
        output, input_grad, qkv_final, q_final, v_final, out_final, out_bias_final, g1, b1, in_final,
        in_bias_final, down_final, down_bias_final, g2, b2,
    )


def solution(mesh):
    fsdp, nseq = mesh.shape["fsdp"], mesh.shape["seq"]
    fine = Mesh(mesh.devices.reshape(fsdp // CORES, CORES, nseq), ("xy", "core", "seq"))
    shard = ("xy", "core")
    stream, matrix, vector = P(shard, None, "seq", None), P(shard, None), P(shard)
    return jax.shard_map(
        per_device,
        mesh=fine,
        in_specs=(
            stream, P(shard, None, None), matrix, vector, vector, matrix, vector, vector, vector,
            matrix, vector, matrix, vector, vector, vector, stream,
        ),
        out_specs=(
            stream, stream, matrix, vector, vector, matrix, vector, vector, vector,
            matrix, vector, matrix, vector, vector, vector,
        ),
        check_vma=False,
    )
```

```python
import functools
import math

import jax
import jax.numpy as jnp
from jax import lax
from jax.experimental import pallas as pl
from jax.experimental.pallas import tpu as pltpu
from jax.sharding import Mesh
from jax.sharding import PartitionSpec as P

HEAD_DIM = 64
LANES = 128
NEG = -1e30
TILE = 256
VALUE_ROWS = HEAD_DIM + 16
KEY_TILES = 1
QUERY_TILES = 1
NT = (((1,), (1,)), ((), ()))
NN = (((1,), (0,)), ((), ()))
TN = (((0,), (0,)), ((), ()))


def mm(left, right, dims):
    return lax.dot_general(left, right, dims, preferred_element_type=jnp.float32)


def key_tiles(ends_ref, first, last, tile, total):
    low = jnp.int32(0)
    high = jnp.int32(total)
    for doc in reversed(range(ends_ref.shape[0])):
        end = ends_ref[doc]
        low = jnp.maximum(low, jnp.where(end <= first, end, 0))
        high = jnp.minimum(high, jnp.where(end > last, end, total))
    return low // tile, (high + tile - 1) // tile


def spans(first, after, count, tiles):
    steps = (after - first + count - 1) // count
    return jnp.minimum(first, tiles - steps * count), steps


def lane_halves(x, fill):
    lane = lax.broadcasted_iota(jnp.int32, x.shape, 1)
    fill = jnp.full_like(x, fill)
    return jnp.where(lane < HEAD_DIM, x, fill), jnp.where(lane < HEAD_DIM, fill, x)


def piece_copies(halves, columns, place, scratch, slot, sems, run, mask, inbound):
    copies = []
    pieces = halves[0].shape[0] // run
    for half, ref in enumerate(halves):
        for part in range(pieces):
            index = half * pieces + part
            natural = pl.multiple_of(jnp.bitwise_xor(mask, index) * run, run)
            outer = ref.at[pl.ds(part * run, run), pl.ds(columns, LANES)]
            inner = scratch.at[place, pl.ds(natural, run), :]
            ends = (outer, inner) if inbound else (inner, outer)
            copies.append(pltpu.make_async_copy(ends[0], ends[1], sems.at[slot, index]))
    return copies


def forward_kernel(run, mask_ref, ends_ref, own, sib, seg_col, seg_row, ctx_own, ctx_sib, lse_ref, qkv, out, turned, acc, top, sems, out_sems):
    total = qkv.shape[1]
    pairs = out.shape[0]
    mask = mask_ref[0]

    def loads(pair):
        copies = []
        for kind in range(3):
            copies += piece_copies(
                (own, sib), (3 * pair + kind) * LANES, kind * pairs + pair, qkv, kind * pairs + pair, sems, run, mask, True
            )
        return copies

    for pair in range(pairs):
        for copy in loads(pair):
            copy.start()

    for head in range(2 * pairs):
        turned[head, HEAD_DIM:, :] = jnp.ones((VALUE_ROWS - HEAD_DIM, total), jnp.bfloat16)
    for pair in range(pairs):
        for copy in loads(pair):
            copy.wait()
    heads = [(pair, head) for pair in range(pairs) for head in range(2)]
    if True:

        @pl.loop(0, total // TILE)
        def _(block):
            rows = pl.multiple_of(block * TILE, TILE)
            for pair in range(pairs):
                values = qkv[2 * pairs + pair, pl.ds(rows, TILE), :].astype(jnp.float32).T.astype(jnp.bfloat16)
                for head in range(2):
                    turned[2 * pair + head, :HEAD_DIM, pl.ds(rows, TILE)] = values[head * HEAD_DIM : (head + 1) * HEAD_DIM]

        @pl.loop(0, total // TILE)
        def _(block):
            rows = pl.multiple_of(block * TILE, TILE)
            q_heads = sum([list(lane_halves(qkv[pair, pl.ds(rows, TILE), :], 0.0)) for pair in range(pairs)], [])
            segq = seg_row[:, pl.ds(rows, TILE)]
            first, after = key_tiles(ends_ref, rows, rows + TILE - 1, TILE, total)
            acc[...] = jnp.zeros_like(acc)
            top[...] = jnp.full_like(top, NEG)

            first, steps = spans(first, after, KEY_TILES, total // TILE)

            @pl.loop(0, steps)
            def _(step):
                at = pl.multiple_of((first + step * KEY_TILES) * TILE, TILE)
                keys = [qkv[pairs + pair, pl.ds(at, KEY_TILES * TILE), :] for pair in range(pairs)]
                segk = seg_col[pl.ds(at, KEY_TILES * TILE), :]
                same = jnp.concatenate([segk] * (TILE // LANES), axis=1) == segq
                def scores_of(head):
                    return jnp.where(same, mm(keys[head // 2], q_heads[head], NT), NEG)

                queue = [scores_of(head) for head in range(6)]
                for head in range(2 * pairs):
                    if head + 6 < 2 * pairs:
                        queue.append(scores_of(head + 6))
                    scores = queue.pop(0)
                    old = top[head, 0:1]
                    new = jnp.maximum(old, jnp.max(scores, axis=0, keepdims=True))
                    probs = jnp.exp(scores - new).astype(jnp.bfloat16)
                    acc[head] = acc[head] * jnp.exp(old - new) + mm(turned[head, :, pl.ds(at, KEY_TILES * TILE)], probs, NN)
                    top[head] = jnp.broadcast_to(new, (8, TILE))

            for pair in range(pairs):
                parts = []
                for head in (2 * pair, 2 * pair + 1):
                    weight = acc[head, HEAD_DIM : HEAD_DIM + 1]
                    parts.append(acc[head, :HEAD_DIM] / weight)
                    lse_ref[head, :, pl.ds(rows, TILE)] = top[head] + jnp.log(acc[head, HEAD_DIM : HEAD_DIM + 8])
                out[pair, pl.ds(rows, TILE), :] = jnp.concatenate(parts, axis=0).T.astype(jnp.bfloat16)

    for pair in range(pairs):
        for copy in piece_copies((ctx_own, ctx_sib), pair * LANES, pair, out, pair, out_sems, run, mask, False):
            copy.start()
    for pair in range(pairs):
        for copy in piece_copies((ctx_own, ctx_sib), pair * LANES, pair, out, pair, out_sems, run, mask, False):
            copy.wait()


def attend_forward(mask, ends, own, sib, seg_col, seg_row, run):
    half, columns = own.shape
    total = 2 * half
    pairs = columns // (3 * LANES)
    pieces = total // run
    any_spec = pl.BlockSpec(memory_space=pl.ANY)
    vmem = pl.BlockSpec(memory_space=pltpu.VMEM)
    smem = pl.BlockSpec(memory_space=pltpu.SMEM)
    return pl.pallas_call(
        functools.partial(forward_kernel, run),
        out_shape=(
            jax.ShapeDtypeStruct((half, pairs * LANES), jnp.bfloat16),
            jax.ShapeDtypeStruct((half, pairs * LANES), jnp.bfloat16),
            jax.ShapeDtypeStruct((2 * pairs, 8, total), jnp.float32),
        ),
        in_specs=[smem, smem, any_spec, any_spec, vmem, vmem],
        out_specs=(any_spec, any_spec, vmem),
        scratch_shapes=[
            pltpu.VMEM((3 * pairs, total, LANES), jnp.bfloat16),
            pltpu.VMEM((pairs, total, LANES), jnp.bfloat16),
            pltpu.VMEM((2 * pairs, VALUE_ROWS, total), jnp.bfloat16),
            pltpu.VMEM((2 * pairs, VALUE_ROWS, TILE), jnp.float32),
            pltpu.VMEM((2 * pairs, 8, TILE), jnp.float32),
            pltpu.SemaphoreType.DMA((3 * pairs, pieces)),
            pltpu.SemaphoreType.DMA((pairs, pieces)),
        ],
        compiler_params=pltpu.CompilerParams(vmem_limit_bytes=40 << 20),
        cost_estimate=pl.CostEstimate(flops=1_000_000_000, bytes_accessed=1_000_000, transcendentals=0),
        name="attend_forward",
    )(mask, ends, own, sib, seg_col, seg_row)


def backward_kernel(
    run, pair, mask_ref, ends_ref, own, sib, ctx_own, ctx_sib, dctx_own, dctx_sib, seg_col, seg_row, lse_ref,
    d_own, d_sib, qkv, ctx, out, turned, delta, dq, dkv, sems, out_sems
):
    total = qkv.shape[1]
    mask = mask_ref[0]
    loads, stores = [], []
    for kind in range(3):
        loads += piece_copies((own, sib), (3 * pair + kind) * LANES, kind, qkv, kind, sems, run, mask, True)
        stores += piece_copies((d_own, d_sib), kind * LANES, kind, out, kind, out_sems, run, mask, False)
    loads += piece_copies((ctx_own, ctx_sib), pair * LANES, 0, ctx, 3, sems, run, mask, True)
    loads += piece_copies((dctx_own, dctx_sib), pair * LANES, 1, ctx, 4, sems, run, mask, True)
    for copy in loads:
        copy.start()
    for copy in loads:
        copy.wait()

    @pl.loop(0, total // TILE)
    def _(block):
        rows = pl.multiple_of(block * TILE, TILE)
        product = ctx[0, pl.ds(rows, TILE), :].astype(jnp.float32) * ctx[1, pl.ds(rows, TILE), :].astype(jnp.float32)
        product = product.T
        for head in range(2):
            part = jnp.sum(product[head * HEAD_DIM : (head + 1) * HEAD_DIM], axis=0, keepdims=True)
            delta[head, :, pl.ds(rows, TILE)] = jnp.broadcast_to(part, (8, TILE))
        turned[:, pl.ds(rows, TILE)] = qkv[1, pl.ds(rows, TILE), :].astype(jnp.float32).T.astype(jnp.bfloat16)
        dq[:, pl.ds(rows, TILE)] = jnp.zeros((LANES, TILE), jnp.float32)

    @pl.loop(0, total // TILE)
    def _(block):
        rows = pl.multiple_of(block * TILE, TILE)
        k_heads = lane_halves(qkv[1, pl.ds(rows, TILE), :], 0.0)
        v_heads = lane_halves(qkv[2, pl.ds(rows, TILE), :], 0.0)
        segk = seg_col[pl.ds(rows, TILE), :]
        segk = jnp.concatenate([segk] * (TILE // LANES), axis=1)
        first, after = key_tiles(ends_ref, rows, rows + TILE - 1, TILE, total)
        dkv[...] = jnp.zeros_like(dkv)

        first, steps = spans(first, after, QUERY_TILES, total // TILE)

        @pl.loop(0, steps)
        def _(step):
            at = pl.multiple_of((first + step * QUERY_TILES) * TILE, TILE)
            span = pl.ds(at, QUERY_TILES * TILE)
            queries = qkv[0, span, :]
            grads = ctx[1, span, :]
            q_heads = lane_halves(queries, 0.0)
            g_heads = lane_halves(grads, 0.0)
            same = jnp.concatenate([segk] * QUERY_TILES, axis=1) == seg_row[:, span]
            scores = [mm(k_heads[head], queries, NT) for head in range(2)]
            dprobs = [mm(v_heads[head], grads, NT) for head in range(2)]
            low, dscores = [], []
            for head in range(2):
                probs = jnp.exp(jnp.where(same, scores[head] - lse_ref[2 * pair + head, 0:1, span], NEG))
                low.append(probs.astype(jnp.bfloat16))
                dscores.append((probs * (dprobs[head] - delta[head, 0:1, span])).astype(jnp.bfloat16))
            dkv[1] += mm(low[0], g_heads[0], NN) + mm(low[1], g_heads[1], NN)
            dkv[0] += mm(dscores[0], q_heads[0], NN) + mm(dscores[1], q_heads[1], NN)
            for head in range(2):
                lanes = slice(head * HEAD_DIM, (head + 1) * HEAD_DIM)
                dq[lanes, span] += mm(turned[lanes, pl.ds(rows, TILE)], dscores[head], NN)

        out[1, pl.ds(rows, TILE), :] = dkv[0].astype(jnp.bfloat16)
        out[2, pl.ds(rows, TILE), :] = dkv[1].astype(jnp.bfloat16)

    @pl.loop(0, total // TILE)
    def _(block):
        rows = pl.multiple_of(block * TILE, TILE)
        out[0, pl.ds(rows, TILE), :] = (dq[:, pl.ds(rows, TILE)].T * HEAD_DIM**-0.5).astype(jnp.bfloat16)

    for copy in stores:
        copy.start()
    for copy in stores:
        copy.wait()


def attend_backward(pair, mask, ends, own, sib, ctx_own, ctx_sib, dctx_own, dctx_sib, seg_col, seg_row, lse, run):
    half = own.shape[0]
    total = 2 * half
    pieces = total // run
    any_spec = pl.BlockSpec(memory_space=pl.ANY)
    vmem = pl.BlockSpec(memory_space=pltpu.VMEM)
    smem = pl.BlockSpec(memory_space=pltpu.SMEM)
    return pl.pallas_call(
        functools.partial(backward_kernel, run, pair),
        out_shape=(
            jax.ShapeDtypeStruct((half, 3 * LANES), jnp.bfloat16),
            jax.ShapeDtypeStruct((half, 3 * LANES), jnp.bfloat16),
        ),
        in_specs=[smem, smem] + [any_spec] * 6 + [vmem] * 3,
        out_specs=(any_spec, any_spec),
        scratch_shapes=[
            pltpu.VMEM((3, total, LANES), jnp.bfloat16),
            pltpu.VMEM((2, total, LANES), jnp.bfloat16),
            pltpu.VMEM((3, total, LANES), jnp.bfloat16),
            pltpu.VMEM((LANES, total), jnp.bfloat16),
            pltpu.VMEM((2, 8, total), jnp.float32),
            pltpu.VMEM((LANES, total), jnp.float32),
            pltpu.VMEM((2, TILE, LANES), jnp.float32),
            pltpu.SemaphoreType.DMA((5, pieces)),
            pltpu.SemaphoreType.DMA((3, pieces)),
        ],
        compiler_params=pltpu.CompilerParams(vmem_limit_bytes=24 << 20),
        cost_estimate=pl.CostEstimate(flops=20_000_000_000, bytes_accessed=8_000_000, transcendentals=0),
        name=f"attend_backward_{pair}",
    )(mask, ends, own, sib, ctx_own, ctx_sib, dctx_own, dctx_sib, seg_col, seg_row, lse)


EPS = 1e-05


def norm_forward(resid, gain, shift):
    mean = jnp.mean(resid, axis=-1, keepdims=True)
    centered = resid - mean
    inv = lax.rsqrt(jnp.mean(centered * centered, axis=-1, keepdims=True) + EPS)
    normed = centered * inv
    return (normed * gain + shift, normed, inv)


def norm_backward(grad, normed, inv, gain):
    scaled = grad * gain
    return inv * (
        scaled
        - jnp.mean(scaled, axis=-1, keepdims=True)
        - normed * jnp.mean(scaled * normed, axis=-1, keepdims=True)
    )


ROWS = 256
CHUNK = 768


def fold(x):
    return jnp.sum(x.reshape(-1, 8, x.shape[1]), axis=0)


def middle_kernel(
    core_ref, x_ref, near_ref, far_ref, cot_ref, vec_ref, in_bias_ref, packed,
    result_ref, low_ref, act_ref, grad_down_ref, grad_pre_ref, grad_one_ref, grad_attn_ref, dnear_ref, dfar_ref,
    sums_ref, in_sums_ref, wo, wi, wd, slope, acc, sums, in_sums, sems
):
    f32, bf16 = jnp.float32, jnp.bfloat16
    mine = near_ref.shape[1]
    chunks = wi.shape[0]
    step = pl.program_id(0)
    core = core_ref[0]
    shards = packed.shape[0]
    rows = packed.shape[1] // (2 * chunks + 1)
    copies = []

    def load(shard, at, count, target):
        copies.append(pltpu.make_async_copy(packed.at[shard, pl.ds(at, count), :], target, sems.at[len(copies)]))

    if shards == 1:
        for place in range(2):
            which = core if place == 0 else 1 - core
            load(0, pl.multiple_of(2 * chunks * rows + which * mine, 16), mine, wo.at[pl.ds(place * mine, mine), :])
    else:
        for place in range(2):
            which = core if place == 0 else 1 - core
            for part in range(shards // 2):
                target = wo.at[pl.ds(place * mine + part * rows, rows), :]
                load(which * (shards // 2) + part, 2 * chunks * rows, rows, target)
    outs = len(copies)
    for chunk in range(chunks):
        for shard in range(shards):
            load(shard, (chunks + chunk) * rows, rows, wi.at[chunk, pl.ds(shard * rows, rows), :])
    for chunk in range(chunks):
        for shard in range(shards):
            first = shard * chunks * rows
            low, high = max(first, chunk * CHUNK), min(first + chunks * rows, (chunk + 1) * CHUNK)
            if low < high:
                load(shard, low - first, high - low, wd.at[chunk, pl.ds(low - chunk * CHUNK, high - low), :])

    @pl.when(step == 0)
    def _():
        for copy in copies:
            copy.start()
        sums[...] = jnp.zeros_like(sums)
        in_sums[...] = jnp.zeros_like(in_sums)
        for copy in copies[:outs]:
            copy.wait()

    bias_out, gain_one, shift_one, bias_down, gain_two, shift_two = [vec_ref[i : i + 1, :] for i in range(6)]
    near, far = near_ref[...], far_ref[...]
    attn = mm(near, wo[:mine], NN) + mm(far, wo[mine:], NN) + bias_out
    hidden, normed_one, inv_one = norm_forward(x_ref[...].astype(f32) + attn, gain_one, shift_one)
    low_ref[...] = hidden.astype(bf16)
    acc[...] = hidden + bias_down

    @pl.when(step == 0)
    def _():
        for copy in copies[outs:]:
            copy.wait()

    @pl.loop(0, chunks)
    def _(chunk):
        columns = pl.ds(pl.multiple_of(chunk * CHUNK, CHUNK), CHUNK)
        pre = mm(low_ref[...], wi[chunk], NN) + in_bias_ref[:, columns]
        cdf = 0.5 * (1.0 + lax.erf(pre * (1.0 / math.sqrt(2.0))))
        density = jnp.exp(-0.5 * pre * pre) * (1.0 / math.sqrt(2.0 * math.pi))
        act = (pre * cdf).astype(bf16)
        act_ref[:, columns] = act
        slope[:, columns] = cdf + pre * density
        acc[...] += mm(act, wd[chunk], NN)

    result, normed_two, inv_two = norm_forward(acc[...], gain_two, shift_two)
    result_ref[...] = result.astype(bf16)
    dy = cot_ref[...].astype(f32)
    grad_two = norm_backward(dy, normed_two, inv_two, gain_two)
    grad_down = grad_two.astype(bf16)
    grad_down_ref[...] = grad_down
    sums[3] += fold(grad_down.astype(f32))
    sums[4] += fold(dy * normed_two)
    sums[5] += fold(dy)
    acc[...] = grad_two

    @pl.loop(0, chunks)
    def _(chunk):
        columns = pl.ds(pl.multiple_of(chunk * CHUNK, CHUNK), CHUNK)
        grad_pre = (mm(grad_down_ref[...], wd[chunk], NT) * slope[:, columns]).astype(bf16)
        grad_pre_ref[:, columns] = grad_pre
        in_sums[:, columns] += fold(grad_pre.astype(f32))
        acc[...] += mm(grad_pre, wi[chunk], NT)

    grad_hidden = acc[...]
    sums[1] += fold(grad_hidden * normed_one)
    sums[2] += fold(grad_hidden)
    grad_one = norm_backward(grad_hidden, normed_one, inv_one, gain_one)
    grad_one_ref[...] = grad_one
    grad_attn = grad_one.astype(bf16)
    grad_attn_ref[...] = grad_attn
    sums[0] += fold(grad_attn.astype(f32))
    dnear_ref[...] = mm(grad_attn, wo[:mine], NT).astype(bf16)
    dfar_ref[...] = mm(grad_attn, wo[mine:], NT).astype(bf16)

    @pl.when(step == pl.num_programs(0) - 1)
    def _():
        sums_ref[...] = jnp.zeros_like(sums_ref)
        for i in range(6):
            sums_ref[i : i + 1, :] = jnp.sum(sums[i], axis=0, keepdims=True)
        in_sums_ref[...] = jnp.sum(in_sums[...], axis=0, keepdims=True)


def middle(core, x, near, far, cot, vec, in_bias, packed):
    count, width = x.shape
    hidden = in_bias.shape[1]
    mine = near.shape[1]
    chunks = hidden // CHUNK
    f32, bf16 = jnp.float32, jnp.bfloat16
    any_spec = pl.BlockSpec(memory_space=pl.ANY)
    block = lambda columns: pl.BlockSpec((ROWS, columns), lambda i: (i, 0))
    whole = lambda rows, columns: pl.BlockSpec((rows, columns), lambda i: (0, 0))
    shape = jax.ShapeDtypeStruct
    return pl.pallas_call(
        middle_kernel,
        grid=(count // ROWS,),
        out_shape=(
            shape((count, width), bf16), shape((count, width), bf16), shape((count, hidden), bf16),
            shape((count, width), bf16), shape((count, hidden), bf16), shape((count, width), f32),
            shape((count, width), bf16), shape((count, mine), bf16), shape((count, mine), bf16),
            shape((8, width), f32), shape((1, hidden), f32),
        ),
        in_specs=[
            pl.BlockSpec(memory_space=pltpu.SMEM), block(width), block(mine), block(mine), block(width),
            whole(8, width), whole(1, hidden), any_spec,
        ],
        out_specs=(
            block(width), block(width), block(hidden), block(width), block(hidden), block(width), block(width),
            block(mine), block(mine), whole(8, width), whole(1, hidden),
        ),
        scratch_shapes=[
            pltpu.VMEM((width, width), bf16),
            pltpu.VMEM((chunks, width, CHUNK), bf16),
            pltpu.VMEM((chunks, CHUNK, width), bf16),
            pltpu.VMEM((ROWS, hidden), f32),
            pltpu.VMEM((ROWS, width), f32),
            pltpu.VMEM((6, 8, width), f32),
            pltpu.VMEM((8, hidden), f32),
            pltpu.SemaphoreType.DMA(((2 * chunks + 1) * max(packed.shape[0], 2),)),
        ],
        compiler_params=pltpu.CompilerParams(vmem_limit_bytes=48 << 20),
        cost_estimate=pl.CostEstimate(flops=20_000_000_000, bytes_accessed=30_000_000, transcendentals=0),
        name="middle",
    )(core, x, near, far, cot, vec, in_bias, packed)


def gradients_kernel(
    rows, core_ref, act_ref, low_ref, down_ref, pre_ref, near_ref, far_ref, attn_ref, vec_ref,
    keep_ref, send_ref, result, sems
):
    step = pl.program_id(0)
    core = core_ref[0]
    shards = low_ref.shape[1] // rows
    chunks = (pl.num_programs(0) - 1) // 2
    blocks = pre_ref.shape[1] * chunks // low_ref.shape[1]
    slot = step % 2

    def wait(which):
        pltpu.make_async_copy(result.at[which], result.at[which], sems.at[which]).wait()

    def put(source, shard_core, plane, at, count, sem):
        target = pl.ds(at, count)

        @pl.when(core == shard_core)
        def _():
            pltpu.make_async_copy(source, keep_ref.at[plane, target, :], sem).start()

        @pl.when(core != shard_core)
        def _():
            pltpu.make_async_copy(source, send_ref.at[plane, target, :], sem).start()

    @pl.when(step >= 2)
    def _():
        wait(slot)

    @pl.when(step < chunks)
    def _():
        result[slot] = mm(act_ref[...], down_ref[...], TN).astype(jnp.bfloat16)
        count = blocks * rows
        here = result.shape[1] // count
        for part in range(here):
            put(result.at[slot, pl.ds(part * count, count), :], part % CORES, step * (here // CORES) + part // CORES, 0, count, sems.at[slot])

    @pl.when(jnp.logical_and(step >= chunks, step < 2 * chunks))
    def _():
        result[slot] = mm(low_ref[...], pre_ref[...], TN).astype(jnp.bfloat16)
        at = pl.multiple_of(blocks * rows + (step - chunks) * rows, 16)
        for shard in range(shards):
            put(result.at[slot, pl.ds(shard * rows, rows), :], shard % CORES, shard // CORES, at, rows, sems.at[slot])

    @pl.when(step == 2 * chunks)
    def _():
        mine = near_ref.shape[1]
        result[slot, :mine] = mm(near_ref[...], attn_ref[...], TN).astype(jnp.bfloat16)
        result[slot, mine:] = mm(far_ref[...], attn_ref[...], TN).astype(jnp.bfloat16)
        half = shards // 2
        for shard in range(shards):
            first = core if shard < half else 1 - core
            plane = first * (half // CORES) + (shard % half) // CORES
            put(result.at[slot, pl.ds(shard * rows, rows), :], shard % CORES, plane, 2 * blocks * rows, rows, sems.at[slot])
        for shard in range(shards):
            put(vec_ref.at[shard], shard % CORES, shard // CORES, (2 * blocks + 1) * rows, vec_ref.shape[1], sems.at[2 + shard])
        wait(0)
        wait(1)
        for shard in range(shards):
            pltpu.make_async_copy(vec_ref.at[shard], vec_ref.at[shard], sems.at[2 + shard]).wait()


def gradients(core, act, low, down, pre, near, far, attn, vec, planes):
    count, width = low.shape
    rows = width // (planes * CORES)
    chunks = pre.shape[1] // width
    total_rows = (2 * chunks + 1) * rows + vec.shape[1]
    whole = lambda x: pl.BlockSpec(x.shape, lambda i: (0,) * x.ndim)
    out = jax.ShapeDtypeStruct((planes, total_rows, width), jnp.bfloat16)
    return pl.pallas_call(
        functools.partial(gradients_kernel, rows),
        grid=(2 * chunks + 1,),
        out_shape=(out, out),
        in_specs=[
            pl.BlockSpec(memory_space=pltpu.SMEM),
            pl.BlockSpec((count, width), lambda i: (0, jnp.minimum(i, chunks - 1))),
            whole(low), whole(down),
            pl.BlockSpec((count, width), lambda i: (0, jnp.clip(i - chunks, 0, chunks - 1))),
            whole(near), whole(far), whole(attn), whole(vec),
        ],
        out_specs=(pl.BlockSpec(memory_space=pl.ANY),) * 2,
        scratch_shapes=[
            pltpu.VMEM((2, width, width), jnp.bfloat16),
            pltpu.SemaphoreType.DMA((2 + planes * CORES,)),
        ],
        compiler_params=pltpu.CompilerParams(vmem_limit_bytes=48 << 20),
        cost_estimate=pl.CostEstimate(flops=11_000_000_000, bytes_accessed=30_000_000, transcendentals=0),
        name="gradients",
    )(core, act, low, down, pre, near, far, attn, vec)


def doc_ids(ends, count):
    places = jnp.arange(count, dtype=jnp.int32)
    return jnp.sum((places[:, None] >= ends[None, :]).astype(jnp.int32), axis=1)


CORES = 2


def routes(nseq):
    first, second = [], []
    for core in range(CORES):
        for z in range(nseq):
            source = core * nseq + z
            first.append((source, (z // 2) * nseq + 2 * core + z % 2))
            second.append((source, (z // 2) * nseq + 2 * core + 1 - z % 2))
    return first, second


def swap(x):
    return lax.ppermute(x, "core", [(0, 1), (1, 0)])


def after(value, *done):
    return lax.optimization_barrier((value, done))[0]


def pick(value, which, axis=0):
    return lax.dynamic_index_in_dim(value, which, axis, keepdims=False)


def total(keep, received):
    return (keep.astype(jnp.float32) + received.astype(jnp.float32)).astype(jnp.bfloat16)


class Halving:
    def __init__(self, blocks, planes):
        bits = planes.bit_length() - 1
        rows = blocks.shape[1]
        self.planes = planes
        self.orders = (list(range(bits)), list(range(bits))[::-1])
        self.left = [list(range(bits))[::-1] for _ in range(2)]
        parts = (blocks[:, : rows // 2], blocks[:, rows // 2 :])
        self.parts = [p.reshape((2,) * bits + p.shape[1:]) for p in parts]
        self.steps = bits

    def send(self, step):
        place = lax.axis_index("xy")
        self.keep, self.received, self.sent = [], [], []
        for half in range(2):
            bit = self.orders[half][step]
            axis = self.left[half].index(bit)
            mine = (place >> bit) % 2
            self.left[half].remove(bit)
            out = pick(self.parts[half], 1 - mine, axis)
            self.keep.append(pick(self.parts[half], mine, axis))
            self.sent.append(out)
            self.received.append(lax.ppermute(out, "xy", [(i, i ^ (1 << bit)) for i in range(self.planes)]))

    def add(self, *done):
        self.parts = [total(k, after(r, *done)) for k, r in zip(self.keep, self.received)]

    def result(self):
        return jnp.concatenate(self.parts)


class Spread:
    def __init__(self, value, nseq):
        self.nseq, self.rows = nseq, value.shape[0] // nseq
        self.me = lax.axis_index("seq")
        quarter = lambda which: lax.dynamic_slice_in_dim(value, (which % nseq) * self.rows, self.rows, 0)
        self.keep = quarter(self.me)
        self.sent = [quarter(self.me + d) for d in range(1, nseq)]
        self.received = [self.shift(q, d) for d, q in enumerate(self.sent, 1)]

    def shift(self, value, distance):
        return lax.ppermute(value, "seq", [(i, (i + distance) % self.nseq) for i in range(self.nseq)])

    def add(self, *done):
        parts = [self.keep] + [after(r, *done) for r in self.received]
        self.keep = sum(p.astype(jnp.float32) for p in parts).astype(jnp.bfloat16)
        self.received = [self.shift(self.keep, d) for d in range(1, self.nseq)]

    def result(self, *done):
        whole = jnp.zeros((self.nseq * self.rows,) + self.keep.shape[1:], jnp.bfloat16)
        for d, part in enumerate([self.keep] + [after(r, *done) for r in self.received]):
            start = ((self.me - d) % self.nseq) * self.rows
            whole = lax.dynamic_update_slice_in_dim(whole, part, start, 0)
        return whole


def either(core, own, other, axis):
    return jnp.where(core == 0, jnp.concatenate([own, other], axis), jnp.concatenate([other, own], axis))


def per_device(
    tokens, doc_lengths, qkv_weight, q_bias, v_bias, out_weight, out_bias, norm1_gain, norm1_bias,
    ff_in_weight, ff_in_bias, ff_out_weight, ff_out_bias, norm2_gain, norm2_bias, out_cotangent,
):
    bf16, f32 = jnp.bfloat16, jnp.float32
    fsdp = ("xy", "core")
    nseq = lax.axis_size("seq")
    planes = lax.axis_size("xy")
    shards = planes * CORES
    core = lax.axis_index("core")
    odd = lax.axis_index("seq") % 2
    micro, run, width = tokens.shape[1:]
    assert micro == 2 and nseq == 4
    stretch = run * nseq
    mine = width // CORES
    rows = width // shards
    first, second = routes(nseq)
    back = [[(b, a) for a, b in route] for route in (first, second)]

    def spread(x):
        halves = [lax.dynamic_index_in_dim(x[0], which, 0, keepdims=False) for which in (odd, 1 - odd)]
        return [lax.ppermute(h, ("core", "seq"), r) for h, r in zip(halves, (first, second))]

    pieces = spread(tokens)
    lengths = jnp.stack([doc_lengths[0], swap(doc_lengths[0])])
    z = lax.axis_index("seq")
    theirs = jnp.where(z // 2 == core, lengths[0], lengths[1])
    ends = jnp.cumsum(lax.dynamic_index_in_dim(theirs, odd, 0, keepdims=False)).astype(jnp.int32)
    seg = doc_ids(ends, stretch)
    seg_col = jnp.broadcast_to(seg[:, None], (stretch, LANES))
    seg_row = seg[None]
    mask = (odd + 2 * core).astype(jnp.int32)[None]

    pairs = mine // LANES
    own_columns = qkv_weight.reshape(rows, 3, CORES, pairs, LANES)
    own_columns = jnp.moveaxis(own_columns, (2, 3), (0, 2)).reshape(CORES, rows, 3 * mine)
    kept = pick(own_columns, core)
    w_mine = either(core, kept, swap(pick(own_columns, 1 - core)), 0)
    w_mine = lax.all_gather(w_mine, "xy", axis=0, tiled=True)
    small = [q_bias, v_bias, out_bias, norm1_gain, norm1_bias, ff_out_bias, norm2_gain, norm2_bias]
    inner = ff_in_bias.shape[0] // rows
    small = jnp.concatenate([jnp.stack(small), ff_in_bias.reshape(inner, rows)])
    vectors = lax.all_gather(small, fsdp, axis=0, tiled=False).astype(f32)
    bias_in = vectors[:, 8:].reshape(1, -1)
    vectors = jnp.moveaxis(vectors[:, :8], 0, 1).reshape(8, width)
    bias_q, bias_v = vectors[0], vectors[1]
    norms = jnp.concatenate([vectors[2:], jnp.zeros((2, width), f32)])
    wide = [ff_in_weight[:, i * width : (i + 1) * width] for i in range(inner)]
    packed = lax.all_gather(jnp.concatenate([ff_out_weight] + wide + [out_weight]), fsdp, axis=0, tiled=False)
    if rows % 16:
        parts = [packed[:, : inner * rows].reshape(-1, width)]
        parts += [packed[:, (inner + i) * rows : (inner + i + 1) * rows].reshape(width, width) for i in range(inner + 1)]
        packed = jnp.concatenate(parts)[None]

    own_slice = lambda v: lax.dynamic_slice_in_dim(v, core * mine, mine, 0).reshape(pairs, LANES)
    one = jnp.ones((pairs, LANES), f32)
    bias_mine = jnp.stack([own_slice(bias_q), 0.0 * one, own_slice(bias_v)], axis=1).reshape(-1)
    scale = jnp.stack([HEAD_DIM**-0.5 * one, one, one], axis=1).reshape(-1)
    x_own = after(jnp.concatenate(pieces), norms, bias_in)
    x_sib = jnp.concatenate([swap(p) for p in pieces])
    projected = [((mm(x, w_mine, NN) + bias_mine) * scale).astype(bf16) for x in (x_own, x_sib)]
    ctx_own, ctx_sib, lse = attend_forward(mask, ends, *projected, seg_col, seg_row, run)
    ctx_far = swap(ctx_sib)

    cot = jnp.concatenate(spread(after(out_cotangent, *projected)))
    result, hidden_low, act_low, grad_down, grad_pre, grad_one, grad_attn, dctx_own, dctx_far, sums, in_sums = middle(
        core.astype(jnp.int32)[None], x_own, ctx_own, ctx_far, cot, norms, bias_in, packed
    )
    dctx_far = swap(dctx_far)
    output = [lax.ppermute(result[i * run : (i + 1) * run], ("core", "seq"), back[i]) for i in range(2)]

    def cores(blocks):
        return pick(blocks, core, 1), swap(pick(blocks, 1 - core, 1))

    inner_blocks = ff_in_bias.shape[0] * shards // width
    down_rows = ff_out_weight.shape[0]
    vector = [jnp.moveaxis(sums[:6].reshape(6, shards, rows), 1, 0), in_sums.reshape(shards, inner, rows)]
    vector = jnp.concatenate(vector, axis=1).astype(bf16)
    vector = jnp.pad(vector, ((0, 0), (0, 32 - vector.shape[1]), (0, width - rows)))
    if rows % 16 == 0:
        kept, sent = gradients(
            core.astype(jnp.int32)[None], act_low, hidden_low, grad_down, grad_pre, ctx_own, ctx_far, grad_attn, vector, planes
        )
        joined = kept, swap(sent)
    else:
        down_grad = cores(mm(act_low, grad_down, TN).astype(bf16).reshape(planes, CORES, -1, width))
        in_grad = cores(mm(hidden_low, grad_pre, TN).astype(bf16).reshape(planes, CORES, rows, -1))
        out_grad = [mm(c, grad_attn, TN).astype(bf16) for c in (ctx_own, ctx_far)]
        out_grad = cores(either(core, *out_grad, 0).reshape(planes, CORES, rows, width))
        vector = cores(vector.reshape(planes, CORES, 32, width))
        joined = []
        for which in range(2):
            wide = in_grad[which]
            wide = [wide[:, :, i * width : (i + 1) * width] for i in range(inner_blocks)]
            joined.append(jnp.concatenate([down_grad[which]] + wide + [out_grad[which], vector[which]], axis=1))
    early = Halving(total(*joined), planes)
    early.send(0)
    progress = [early]

    def advance(*done):
        if len(progress) > 1:
            return []
        early.add(*done)
        step = early.steps - len(early.left[0])
        if step < early.steps:
            early.send(step)
            return early.sent
        progress.append(Spread(early.result(), nseq))
        return progress[1].sent

    def attend(pair, *ready):
        held = after(mask, *ready)
        return attend_backward(
            pair, held, ends, *projected, ctx_own, ctx_sib, dctx_own, dctx_far, seg_col, seg_row, lse, run
        )

    def weight_sums(near, far):
        matrix = (mm(x_own, near, TN) + mm(x_sib, far, TN)).astype(bf16)
        column = (jnp.sum(near.astype(f32), axis=0) + jnp.sum(far.astype(f32), axis=0)).astype(bf16)
        column = jnp.pad(column[None], ((0, 63), (0, 0)))
        column = jnp.broadcast_to(column, (planes,) + column.shape)
        return jnp.concatenate([matrix.reshape(planes, CORES * rows, -1), column], axis=1)

    grads = [attend(0, *early.sent)]
    for pair in range(1, pairs):
        sent = advance(grads[-1][0])
        if pair == pairs - 1:
            output = [after(o, grads[-1][0]) for o in output]
            sent = list(sent) + output
        grads.append(attend(pair, *sent))
    while len(progress) == 1:
        advance(grads[-1][0])
    early_sum = progress[1]

    near = jnp.concatenate([g[0] for g in grads], axis=1)
    far = jnp.concatenate([g[1] for g in grads], axis=1)
    grad_far = swap(mm(far, w_mine, NT).astype(bf16))
    early_sum.add(grads[-1][0])
    input_grad = (grad_one + mm(near, w_mine, NT) + grad_far.astype(f32)).astype(bf16)
    returned = [lax.ppermute(input_grad[i * run : (i + 1) * run], ("core", "seq"), back[i]) for i in range(2)]
    qkv_halves = Halving(after(weight_sums(near, far), input_grad), planes)
    for step in range(qkv_halves.steps):
        qkv_halves.send(step)
        qkv_halves.add(input_grad)
    qkv_sum = Spread(qkv_halves.result(), nseq)
    qkv_sum.add(*returned)
    input_grad = jnp.where(odd == 0, jnp.stack(returned), jnp.stack(returned[::-1]))[None].astype(f32)
    early_total = early_sum.result(qkv_sum.keep)
    qkv_total = qkv_sum.result()

    down_final = early_total[:down_rows].astype(f32)
    wide = [early_total[down_rows + i * rows : down_rows + (i + 1) * rows] for i in range(inner_blocks)]
    in_final = jnp.concatenate(wide, axis=1).astype(f32)
    at = down_rows + inner_blocks * rows
    out_final = early_total[at : at + rows].astype(f32)
    at = at + rows
    line = early_total[at : at + 32, :rows].astype(f32)
    out_bias_final, g1, b1, down_bias_final, g2, b2 = [line[i] for i in range(6)]
    in_bias_final = line[6 : 6 + inner].reshape(-1)

    part = qkv_total
    column = part[CORES * rows]
    other = swap(jnp.concatenate([lax.dynamic_slice_in_dim(part, (1 - core) * rows, rows, 0), part[CORES * rows : CORES * rows + 16]]))
    own_block = lax.dynamic_slice_in_dim(part, core * rows, rows, 0)
    spread_out = lambda v: jnp.moveaxis(v.reshape(-1, pairs, 3, LANES), 2, 1).reshape(-1, 3, 1, mine)
    qkv_final = either(core, spread_out(own_block), spread_out(other[:rows]), 2).reshape(rows, 3 * width).astype(f32)
    sums = either(core, spread_out(column), spread_out(other[rows]), 2).reshape(3, width)
    shard = lax.axis_index("xy") * CORES + core
    q_final = lax.dynamic_slice_in_dim(sums[0], shard * rows, rows, 0).astype(f32)
    v_final = lax.dynamic_slice_in_dim(sums[2], shard * rows, rows, 0).astype(f32)
    output = [after(o, qkv_sum.keep) for o in output]
    output = jnp.where(odd == 0, jnp.stack(output), jnp.stack(output[::-1]))[None]
    return (
        output, input_grad, qkv_final, q_final, v_final, out_final, out_bias_final, g1, b1, in_final,
        in_bias_final, down_final, down_bias_final, g2, b2,
    )


def solution(mesh):
    fsdp, nseq = mesh.shape["fsdp"], mesh.shape["seq"]
    fine = Mesh(mesh.devices.reshape(fsdp // CORES, CORES, nseq), ("xy", "core", "seq"))
    shard = ("xy", "core")
    stream, matrix, vector = P(shard, None, "seq", None), P(shard, None), P(shard)
    return jax.shard_map(
        per_device,
        mesh=fine,
        in_specs=(
            stream, P(shard, None, None), matrix, vector, vector, matrix, vector, vector, vector,
            matrix, vector, matrix, vector, vector, vector, stream,
        ),
        out_specs=(
            stream, stream, matrix, vector, vector, matrix, vector, vector, vector,
            matrix, vector, matrix, vector, vector, vector,
        ),
        check_vma=False,
    )
```

```python
import functools
import math

import jax
import jax.numpy as jnp
from jax import lax
from jax.experimental import pallas as pl
from jax.experimental.pallas import tpu as pltpu
from jax.sharding import Mesh
from jax.sharding import PartitionSpec as P

HEAD_DIM = 64
LANES = 128
NEG = -1e30
TILE = 256
VALUE_ROWS = HEAD_DIM + 16
KEY_TILES = 1
QUERY_TILES = 1
NT = (((1,), (1,)), ((), ()))
NN = (((1,), (0,)), ((), ()))
TN = (((0,), (0,)), ((), ()))


def mm(left, right, dims):
    return lax.dot_general(left, right, dims, preferred_element_type=jnp.float32)


def key_tiles(ends_ref, first, last, tile, total):
    low = jnp.int32(0)
    high = jnp.int32(total)
    for doc in reversed(range(ends_ref.shape[0])):
        end = ends_ref[doc]
        low = jnp.maximum(low, jnp.where(end <= first, end, 0))
        high = jnp.minimum(high, jnp.where(end > last, end, total))
    return low // tile, (high + tile - 1) // tile


def spans(first, after, count, tiles):
    steps = (after - first + count - 1) // count
    return jnp.minimum(first, tiles - steps * count), steps


def lane_halves(x, fill):
    lane = lax.broadcasted_iota(jnp.int32, x.shape, 1)
    fill = jnp.full_like(x, fill)
    return jnp.where(lane < HEAD_DIM, x, fill), jnp.where(lane < HEAD_DIM, fill, x)


def piece_copies(halves, columns, place, scratch, slot, sems, run, mask, inbound):
    copies = []
    pieces = halves[0].shape[0] // run
    for half, ref in enumerate(halves):
        for part in range(pieces):
            index = half * pieces + part
            natural = pl.multiple_of(jnp.bitwise_xor(mask, index) * run, run)
            outer = ref.at[pl.ds(part * run, run), pl.ds(columns, LANES)]
            inner = scratch.at[place, pl.ds(natural, run), :]
            ends = (outer, inner) if inbound else (inner, outer)
            copies.append(pltpu.make_async_copy(ends[0], ends[1], sems.at[slot, index]))
    return copies


def forward_kernel(run, mask_ref, ends_ref, own, sib, seg_col, seg_row, ctx_own, ctx_sib, lse_ref, qkv, out, turned, acc, top, sems, out_sems):
    total = qkv.shape[1]
    pairs = out.shape[0]
    mask = mask_ref[0]

    def loads(pair):
        copies = []
        for kind in range(3):
            copies += piece_copies(
                (own, sib), (3 * pair + kind) * LANES, kind * pairs + pair, qkv, kind * pairs + pair, sems, run, mask, True
            )
        return copies

    for pair in range(pairs):
        for copy in loads(pair):
            copy.start()

    for head in range(2 * pairs):
        turned[head, HEAD_DIM:, :] = jnp.ones((VALUE_ROWS - HEAD_DIM, total), jnp.bfloat16)
    for pair in range(pairs):
        for copy in loads(pair):
            copy.wait()
    heads = [(pair, head) for pair in range(pairs) for head in range(2)]
    if True:

        @pl.loop(0, total // TILE)
        def _(block):
            rows = pl.multiple_of(block * TILE, TILE)
            for pair in range(pairs):
                values = qkv[2 * pairs + pair, pl.ds(rows, TILE), :].astype(jnp.float32).T.astype(jnp.bfloat16)
                for head in range(2):
                    turned[2 * pair + head, :HEAD_DIM, pl.ds(rows, TILE)] = values[head * HEAD_DIM : (head + 1) * HEAD_DIM]

        @pl.loop(0, total // TILE)
        def _(block):
            rows = pl.multiple_of(block * TILE, TILE)
            q_heads = sum([list(lane_halves(qkv[pair, pl.ds(rows, TILE), :], 0.0)) for pair in range(pairs)], [])
            segq = seg_row[:, pl.ds(rows, TILE)]
            first, after = key_tiles(ends_ref, rows, rows + TILE - 1, TILE, total)
            acc[...] = jnp.zeros_like(acc)
            top[...] = jnp.full_like(top, NEG)

            first, steps = spans(first, after, KEY_TILES, total // TILE)

            @pl.loop(0, steps)
            def _(step):
                at = pl.multiple_of((first + step * KEY_TILES) * TILE, TILE)
                keys = [qkv[pairs + pair, pl.ds(at, KEY_TILES * TILE), :] for pair in range(pairs)]
                segk = seg_col[pl.ds(at, KEY_TILES * TILE), :]
                same = jnp.concatenate([segk] * (TILE // LANES), axis=1) == segq
                def scores_of(head):
                    return jnp.where(same, mm(keys[head // 2], q_heads[head], NT), NEG)

                queue = [scores_of(head) for head in range(6)]
                for head in range(2 * pairs):
                    if head + 6 < 2 * pairs:
                        queue.append(scores_of(head + 6))
                    scores = queue.pop(0)
                    old = top[head, 0:1]
                    new = jnp.maximum(old, jnp.max(scores, axis=0, keepdims=True))
                    probs = jnp.exp(scores - new).astype(jnp.bfloat16)
                    acc[head] = acc[head] * jnp.exp(old - new) + mm(turned[head, :, pl.ds(at, KEY_TILES * TILE)], probs, NN)
                    top[head] = jnp.broadcast_to(new, (8, TILE))

            for pair in range(pairs):
                parts = []
                for head in (2 * pair, 2 * pair + 1):
                    weight = acc[head, HEAD_DIM : HEAD_DIM + 1]
                    parts.append(acc[head, :HEAD_DIM] / weight)
                    lse_ref[head, :, pl.ds(rows, TILE)] = top[head] + jnp.log(acc[head, HEAD_DIM : HEAD_DIM + 8])
                out[pair, pl.ds(rows, TILE), :] = jnp.concatenate(parts, axis=0).T.astype(jnp.bfloat16)

    for pair in range(pairs):
        for copy in piece_copies((ctx_own, ctx_sib), pair * LANES, pair, out, pair, out_sems, run, mask, False):
            copy.start()
    for pair in range(pairs):
        for copy in piece_copies((ctx_own, ctx_sib), pair * LANES, pair, out, pair, out_sems, run, mask, False):
            copy.wait()


def attend_forward(mask, ends, own, sib, seg_col, seg_row, run):
    half, columns = own.shape
    total = 2 * half
    pairs = columns // (3 * LANES)
    pieces = total // run
    any_spec = pl.BlockSpec(memory_space=pl.ANY)
    vmem = pl.BlockSpec(memory_space=pltpu.VMEM)
    smem = pl.BlockSpec(memory_space=pltpu.SMEM)
    return pl.pallas_call(
        functools.partial(forward_kernel, run),
        out_shape=(
            jax.ShapeDtypeStruct((half, pairs * LANES), jnp.bfloat16),
            jax.ShapeDtypeStruct((half, pairs * LANES), jnp.bfloat16),
            jax.ShapeDtypeStruct((2 * pairs, 8, total), jnp.float32),
        ),
        in_specs=[smem, smem, any_spec, any_spec, vmem, vmem],
        out_specs=(any_spec, any_spec, vmem),
        scratch_shapes=[
            pltpu.VMEM((3 * pairs, total, LANES), jnp.bfloat16),
            pltpu.VMEM((pairs, total, LANES), jnp.bfloat16),
            pltpu.VMEM((2 * pairs, VALUE_ROWS, total), jnp.bfloat16),
            pltpu.VMEM((2 * pairs, VALUE_ROWS, TILE), jnp.float32),
            pltpu.VMEM((2 * pairs, 8, TILE), jnp.float32),
            pltpu.SemaphoreType.DMA((3 * pairs, pieces)),
            pltpu.SemaphoreType.DMA((pairs, pieces)),
        ],
        compiler_params=pltpu.CompilerParams(vmem_limit_bytes=40 << 20),
        cost_estimate=pl.CostEstimate(flops=1_000_000_000, bytes_accessed=1_000_000, transcendentals=0),
        name="attend_forward",
    )(mask, ends, own, sib, seg_col, seg_row)


def backward_kernel(
    run, pair, mask_ref, ends_ref, own, sib, ctx_own, ctx_sib, dctx_own, dctx_sib, seg_col, seg_row, lse_ref,
    d_own, d_sib, qkv, ctx, out, turned, delta, dq, dkv, sems, out_sems
):
    total = qkv.shape[1]
    mask = mask_ref[0]
    loads, stores = [], []
    for kind in range(3):
        loads += piece_copies((own, sib), (3 * pair + kind) * LANES, kind, qkv, kind, sems, run, mask, True)
        stores += piece_copies((d_own, d_sib), kind * LANES, kind, out, kind, out_sems, run, mask, False)
    loads += piece_copies((ctx_own, ctx_sib), pair * LANES, 0, ctx, 3, sems, run, mask, True)
    loads += piece_copies((dctx_own, dctx_sib), pair * LANES, 1, ctx, 4, sems, run, mask, True)
    for copy in loads:
        copy.start()
    for copy in loads:
        copy.wait()

    @pl.loop(0, total // TILE)
    def _(block):
        rows = pl.multiple_of(block * TILE, TILE)
        product = ctx[0, pl.ds(rows, TILE), :].astype(jnp.float32) * ctx[1, pl.ds(rows, TILE), :].astype(jnp.float32)
        product = product.T
        for head in range(2):
            part = jnp.sum(product[head * HEAD_DIM : (head + 1) * HEAD_DIM], axis=0, keepdims=True)
            delta[head, :, pl.ds(rows, TILE)] = jnp.broadcast_to(part, (8, TILE))
        turned[:, pl.ds(rows, TILE)] = qkv[1, pl.ds(rows, TILE), :].astype(jnp.float32).T.astype(jnp.bfloat16)
        dq[:, pl.ds(rows, TILE)] = jnp.zeros((LANES, TILE), jnp.float32)

    @pl.loop(0, total // TILE)
    def _(block):
        rows = pl.multiple_of(block * TILE, TILE)
        k_heads = lane_halves(qkv[1, pl.ds(rows, TILE), :], 0.0)
        v_heads = lane_halves(qkv[2, pl.ds(rows, TILE), :], 0.0)
        segk = seg_col[pl.ds(rows, TILE), :]
        segk = jnp.concatenate([segk] * (TILE // LANES), axis=1)
        first, after = key_tiles(ends_ref, rows, rows + TILE - 1, TILE, total)
        dkv[...] = jnp.zeros_like(dkv)

        first, steps = spans(first, after, QUERY_TILES, total // TILE)

        @pl.loop(0, steps)
        def _(step):
            at = pl.multiple_of((first + step * QUERY_TILES) * TILE, TILE)
            span = pl.ds(at, QUERY_TILES * TILE)
            queries = qkv[0, span, :]
            grads = ctx[1, span, :]
            q_heads = lane_halves(queries, 0.0)
            g_heads = lane_halves(grads, 0.0)
            same = jnp.concatenate([segk] * QUERY_TILES, axis=1) == seg_row[:, span]
            scores = [mm(k_heads[head], queries, NT) for head in range(2)]
            dprobs = [mm(v_heads[head], grads, NT) for head in range(2)]
            low, dscores = [], []
            for head in range(2):
                probs = jnp.exp(jnp.where(same, scores[head] - lse_ref[2 * pair + head, 0:1, span], NEG))
                low.append(probs.astype(jnp.bfloat16))
                dscores.append((probs * (dprobs[head] - delta[head, 0:1, span])).astype(jnp.bfloat16))
            dkv[1] += mm(low[0], g_heads[0], NN) + mm(low[1], g_heads[1], NN)
            dkv[0] += mm(dscores[0], q_heads[0], NN) + mm(dscores[1], q_heads[1], NN)
            for head in range(2):
                lanes = slice(head * HEAD_DIM, (head + 1) * HEAD_DIM)
                dq[lanes, span] += mm(turned[lanes, pl.ds(rows, TILE)], dscores[head], NN)

        out[1, pl.ds(rows, TILE), :] = dkv[0].astype(jnp.bfloat16)
        out[2, pl.ds(rows, TILE), :] = dkv[1].astype(jnp.bfloat16)

    @pl.loop(0, total // TILE)
    def _(block):
        rows = pl.multiple_of(block * TILE, TILE)
        out[0, pl.ds(rows, TILE), :] = (dq[:, pl.ds(rows, TILE)].T * HEAD_DIM**-0.5).astype(jnp.bfloat16)

    for copy in stores:
        copy.start()
    for copy in stores:
        copy.wait()


def attend_backward(pair, mask, ends, own, sib, ctx_own, ctx_sib, dctx_own, dctx_sib, seg_col, seg_row, lse, run):
    half = own.shape[0]
    total = 2 * half
    pieces = total // run
    any_spec = pl.BlockSpec(memory_space=pl.ANY)
    vmem = pl.BlockSpec(memory_space=pltpu.VMEM)
    smem = pl.BlockSpec(memory_space=pltpu.SMEM)
    return pl.pallas_call(
        functools.partial(backward_kernel, run, pair),
        out_shape=(
            jax.ShapeDtypeStruct((half, 3 * LANES), jnp.bfloat16),
            jax.ShapeDtypeStruct((half, 3 * LANES), jnp.bfloat16),
        ),
        in_specs=[smem, smem] + [any_spec] * 6 + [vmem] * 3,
        out_specs=(any_spec, any_spec),
        scratch_shapes=[
            pltpu.VMEM((3, total, LANES), jnp.bfloat16),
            pltpu.VMEM((2, total, LANES), jnp.bfloat16),
            pltpu.VMEM((3, total, LANES), jnp.bfloat16),
            pltpu.VMEM((LANES, total), jnp.bfloat16),
            pltpu.VMEM((2, 8, total), jnp.float32),
            pltpu.VMEM((LANES, total), jnp.float32),
            pltpu.VMEM((2, TILE, LANES), jnp.float32),
            pltpu.SemaphoreType.DMA((5, pieces)),
            pltpu.SemaphoreType.DMA((3, pieces)),
        ],
        compiler_params=pltpu.CompilerParams(vmem_limit_bytes=24 << 20),
        cost_estimate=pl.CostEstimate(flops=20_000_000_000, bytes_accessed=8_000_000, transcendentals=0),
        name=f"attend_backward_{pair}",
    )(mask, ends, own, sib, ctx_own, ctx_sib, dctx_own, dctx_sib, seg_col, seg_row, lse)


EPS = 1e-05


def norm_forward(resid, gain, shift):
    mean = jnp.mean(resid, axis=-1, keepdims=True)
    centered = resid - mean
    inv = lax.rsqrt(jnp.mean(centered * centered, axis=-1, keepdims=True) + EPS)
    normed = centered * inv
    return (normed * gain + shift, normed, inv)


def norm_backward(grad, normed, inv, gain):
    scaled = grad * gain
    return inv * (
        scaled
        - jnp.mean(scaled, axis=-1, keepdims=True)
        - normed * jnp.mean(scaled * normed, axis=-1, keepdims=True)
    )


ROWS = 256
CHUNK = 768


def fold(x):
    return jnp.sum(x.reshape(-1, 8, x.shape[1]), axis=0)


def middle_kernel(
    core_ref, x_ref, near_ref, far_ref, cot_ref, vec_ref, in_bias_ref, packed,
    result_ref, low_ref, act_ref, grad_down_ref, grad_pre_ref, grad_one_ref, grad_attn_ref, dnear_ref, dfar_ref,
    sums_ref, in_sums_ref, wo, wi, wd, slope, acc, sums, in_sums, sems
):
    f32, bf16 = jnp.float32, jnp.bfloat16
    mine = near_ref.shape[1]
    chunks = wi.shape[0]
    step = pl.program_id(0)
    core = core_ref[0]
    shards = packed.shape[0]
    rows = packed.shape[1] // (2 * chunks + 1)
    copies = []

    def load(shard, at, count, target):
        copies.append(pltpu.make_async_copy(packed.at[shard, pl.ds(at, count), :], target, sems.at[len(copies)]))

    if shards == 1:
        for place in range(2):
            which = core if place == 0 else 1 - core
            load(0, pl.multiple_of(2 * chunks * rows + which * mine, 16), mine, wo.at[pl.ds(place * mine, mine), :])
    else:
        for place in range(2):
            which = core if place == 0 else 1 - core
            for part in range(shards // 2):
                target = wo.at[pl.ds(place * mine + part * rows, rows), :]
                load(which * (shards // 2) + part, 2 * chunks * rows, rows, target)
    outs = len(copies)
    for chunk in range(chunks):
        for shard in range(shards):
            load(shard, (chunks + chunk) * rows, rows, wi.at[chunk, pl.ds(shard * rows, rows), :])
    for chunk in range(chunks):
        for shard in range(shards):
            first = shard * chunks * rows
            low, high = max(first, chunk * CHUNK), min(first + chunks * rows, (chunk + 1) * CHUNK)
            if low < high:
                load(shard, low - first, high - low, wd.at[chunk, pl.ds(low - chunk * CHUNK, high - low), :])

    @pl.when(step == 0)
    def _():
        for copy in copies:
            copy.start()
        sums[...] = jnp.zeros_like(sums)
        in_sums[...] = jnp.zeros_like(in_sums)
        for copy in copies[:outs]:
            copy.wait()

    bias_out, gain_one, shift_one, bias_down, gain_two, shift_two = [vec_ref[i : i + 1, :] for i in range(6)]
    near, far = near_ref[...], far_ref[...]
    attn = mm(near, wo[:mine], NN) + mm(far, wo[mine:], NN) + bias_out
    hidden, normed_one, inv_one = norm_forward(x_ref[...].astype(f32) + attn, gain_one, shift_one)
    low_ref[...] = hidden.astype(bf16)
    acc[...] = hidden + bias_down

    @pl.when(step == 0)
    def _():
        for copy in copies[outs:]:
            copy.wait()

    @pl.loop(0, chunks)
    def _(chunk):
        columns = pl.ds(pl.multiple_of(chunk * CHUNK, CHUNK), CHUNK)
        pre = mm(low_ref[...], wi[chunk], NN) + in_bias_ref[:, columns]
        cdf = 0.5 * (1.0 + lax.erf(pre * (1.0 / math.sqrt(2.0))))
        density = jnp.exp(-0.5 * pre * pre) * (1.0 / math.sqrt(2.0 * math.pi))
        act = (pre * cdf).astype(bf16)
        act_ref[:, columns] = act
        slope[:, columns] = cdf + pre * density
        acc[...] += mm(act, wd[chunk], NN)

    result, normed_two, inv_two = norm_forward(acc[...], gain_two, shift_two)
    result_ref[...] = result.astype(bf16)
    dy = cot_ref[...].astype(f32)
    grad_two = norm_backward(dy, normed_two, inv_two, gain_two)
    grad_down = grad_two.astype(bf16)
    grad_down_ref[...] = grad_down
    sums[3] += fold(grad_down.astype(f32))
    sums[4] += fold(dy * normed_two)
    sums[5] += fold(dy)
    acc[...] = grad_two

    @pl.loop(0, chunks)
    def _(chunk):
        columns = pl.ds(pl.multiple_of(chunk * CHUNK, CHUNK), CHUNK)
        grad_pre = (mm(grad_down_ref[...], wd[chunk], NT) * slope[:, columns]).astype(bf16)
        grad_pre_ref[:, columns] = grad_pre
        in_sums[:, columns] += fold(grad_pre.astype(f32))
        acc[...] += mm(grad_pre, wi[chunk], NT)

    grad_hidden = acc[...]
    sums[1] += fold(grad_hidden * normed_one)
    sums[2] += fold(grad_hidden)
    grad_one = norm_backward(grad_hidden, normed_one, inv_one, gain_one)
    grad_one_ref[...] = grad_one
    grad_attn = grad_one.astype(bf16)
    grad_attn_ref[...] = grad_attn
    sums[0] += fold(grad_attn.astype(f32))
    dnear_ref[...] = mm(grad_attn, wo[:mine], NT).astype(bf16)
    dfar_ref[...] = mm(grad_attn, wo[mine:], NT).astype(bf16)

    @pl.when(step == pl.num_programs(0) - 1)
    def _():
        sums_ref[...] = jnp.zeros_like(sums_ref)
        for i in range(6):
            sums_ref[i : i + 1, :] = jnp.sum(sums[i], axis=0, keepdims=True)
        in_sums_ref[...] = jnp.sum(in_sums[...], axis=0, keepdims=True)


def middle(core, x, near, far, cot, vec, in_bias, packed):
    count, width = x.shape
    hidden = in_bias.shape[1]
    mine = near.shape[1]
    chunks = hidden // CHUNK
    f32, bf16 = jnp.float32, jnp.bfloat16
    any_spec = pl.BlockSpec(memory_space=pl.ANY)
    block = lambda columns: pl.BlockSpec((ROWS, columns), lambda i: (i, 0))
    whole = lambda rows, columns: pl.BlockSpec((rows, columns), lambda i: (0, 0))
    shape = jax.ShapeDtypeStruct
    return pl.pallas_call(
        middle_kernel,
        grid=(count // ROWS,),
        out_shape=(
            shape((count, width), bf16), shape((count, width), bf16), shape((count, hidden), bf16),
            shape((count, width), bf16), shape((count, hidden), bf16), shape((count, width), f32),
            shape((count, width), bf16), shape((count, mine), bf16), shape((count, mine), bf16),
            shape((8, width), f32), shape((1, hidden), f32),
        ),
        in_specs=[
            pl.BlockSpec(memory_space=pltpu.SMEM), block(width), block(mine), block(mine), block(width),
            whole(8, width), whole(1, hidden), any_spec,
        ],
        out_specs=(
            block(width), block(width), block(hidden), block(width), block(hidden), block(width), block(width),
            block(mine), block(mine), whole(8, width), whole(1, hidden),
        ),
        scratch_shapes=[
            pltpu.VMEM((width, width), bf16),
            pltpu.VMEM((chunks, width, CHUNK), bf16),
            pltpu.VMEM((chunks, CHUNK, width), bf16),
            pltpu.VMEM((ROWS, hidden), f32),
            pltpu.VMEM((ROWS, width), f32),
            pltpu.VMEM((6, 8, width), f32),
            pltpu.VMEM((8, hidden), f32),
            pltpu.SemaphoreType.DMA(((2 * chunks + 1) * max(packed.shape[0], 2),)),
        ],
        compiler_params=pltpu.CompilerParams(vmem_limit_bytes=48 << 20),
        cost_estimate=pl.CostEstimate(flops=20_000_000_000, bytes_accessed=30_000_000, transcendentals=0),
        name="middle",
    )(core, x, near, far, cot, vec, in_bias, packed)


def gradients_kernel(
    rows, core_ref, act_ref, low_ref, down_ref, pre_ref, near_ref, far_ref, attn_ref, vec_ref,
    keep_ref, send_ref, result, sems
):
    step = pl.program_id(0)
    core = core_ref[0]
    shards = low_ref.shape[1] // rows
    chunks = (pl.num_programs(0) - 1) // 2
    blocks = pre_ref.shape[1] * chunks // low_ref.shape[1]
    slot = step % 2

    def wait(which):
        pltpu.make_async_copy(result.at[which], result.at[which], sems.at[which]).wait()

    def put(source, shard_core, plane, at, count, sem):
        target = pl.ds(at, count)

        @pl.when(core == shard_core)
        def _():
            pltpu.make_async_copy(source, keep_ref.at[plane, target, :], sem).start()

        @pl.when(core != shard_core)
        def _():
            pltpu.make_async_copy(source, send_ref.at[plane, target, :], sem).start()

    @pl.when(step >= 2)
    def _():
        wait(slot)

    @pl.when(step < chunks)
    def _():
        result[slot] = mm(act_ref[...], down_ref[...], TN).astype(jnp.bfloat16)
        count = blocks * rows
        here = result.shape[1] // count
        for part in range(here):
            put(result.at[slot, pl.ds(part * count, count), :], part % CORES, step * (here // CORES) + part // CORES, 0, count, sems.at[slot])

    @pl.when(jnp.logical_and(step >= chunks, step < 2 * chunks))
    def _():
        result[slot] = mm(low_ref[...], pre_ref[...], TN).astype(jnp.bfloat16)
        at = pl.multiple_of(blocks * rows + (step - chunks) * rows, 16)
        for shard in range(shards):
            put(result.at[slot, pl.ds(shard * rows, rows), :], shard % CORES, shard // CORES, at, rows, sems.at[slot])

    @pl.when(step == 2 * chunks)
    def _():
        mine = near_ref.shape[1]
        result[slot, :mine] = mm(near_ref[...], attn_ref[...], TN).astype(jnp.bfloat16)
        result[slot, mine:] = mm(far_ref[...], attn_ref[...], TN).astype(jnp.bfloat16)
        half = shards // 2
        for shard in range(shards):
            first = core if shard < half else 1 - core
            plane = first * (half // CORES) + (shard % half) // CORES
            put(result.at[slot, pl.ds(shard * rows, rows), :], shard % CORES, plane, 2 * blocks * rows, rows, sems.at[slot])
        for shard in range(shards):
            put(vec_ref.at[shard], shard % CORES, shard // CORES, (2 * blocks + 1) * rows, vec_ref.shape[1], sems.at[2 + shard])
        wait(0)
        wait(1)
        for shard in range(shards):
            pltpu.make_async_copy(vec_ref.at[shard], vec_ref.at[shard], sems.at[2 + shard]).wait()


def gradients(core, act, low, down, pre, near, far, attn, vec, planes):
    count, width = low.shape
    rows = width // (planes * CORES)
    chunks = pre.shape[1] // width
    total_rows = (2 * chunks + 1) * rows + vec.shape[1]
    whole = lambda x: pl.BlockSpec(x.shape, lambda i: (0,) * x.ndim)
    out = jax.ShapeDtypeStruct((planes, total_rows, width), jnp.bfloat16)
    return pl.pallas_call(
        functools.partial(gradients_kernel, rows),
        grid=(2 * chunks + 1,),
        out_shape=(out, out),
        in_specs=[
            pl.BlockSpec(memory_space=pltpu.SMEM),
            pl.BlockSpec((count, width), lambda i: (0, jnp.minimum(i, chunks - 1))),
            whole(low), whole(down),
            pl.BlockSpec((count, width), lambda i: (0, jnp.clip(i - chunks, 0, chunks - 1))),
            whole(near), whole(far), whole(attn), whole(vec),
        ],
        out_specs=(pl.BlockSpec(memory_space=pl.ANY),) * 2,
        scratch_shapes=[
            pltpu.VMEM((2, width, width), jnp.bfloat16),
            pltpu.SemaphoreType.DMA((2 + planes * CORES,)),
        ],
        compiler_params=pltpu.CompilerParams(vmem_limit_bytes=48 << 20),
        cost_estimate=pl.CostEstimate(flops=11_000_000_000, bytes_accessed=30_000_000, transcendentals=0),
        name="gradients",
    )(core, act, low, down, pre, near, far, attn, vec)


def doc_ids(ends, count):
    places = jnp.arange(count, dtype=jnp.int32)
    return jnp.sum((places[:, None] >= ends[None, :]).astype(jnp.int32), axis=1)


CORES = 2


def routes(nseq):
    first, second = [], []
    for core in range(CORES):
        for z in range(nseq):
            source = core * nseq + z
            first.append((source, (z // 2) * nseq + 2 * core + z % 2))
            second.append((source, (z // 2) * nseq + 2 * core + 1 - z % 2))
    return first, second


def swap(x):
    return lax.ppermute(x, "core", [(0, 1), (1, 0)])


def after(value, *done):
    return lax.optimization_barrier((value, done))[0]


def pick(value, which, axis=0):
    return lax.dynamic_index_in_dim(value, which, axis, keepdims=False)


def total(keep, received):
    return (keep.astype(jnp.float32) + received.astype(jnp.float32)).astype(jnp.bfloat16)


class Halving:
    def __init__(self, blocks, planes):
        bits = planes.bit_length() - 1
        rows = blocks.shape[1]
        self.planes = planes
        self.orders = (list(range(bits)), list(range(bits))[::-1])
        self.left = [list(range(bits))[::-1] for _ in range(2)]
        parts = (blocks[:, : rows // 2], blocks[:, rows // 2 :])
        self.parts = [p.reshape((2,) * bits + p.shape[1:]) for p in parts]
        self.steps = bits

    def send(self, step):
        place = lax.axis_index("xy")
        self.keep, self.received, self.sent = [], [], []
        for half in range(2):
            bit = self.orders[half][step]
            axis = self.left[half].index(bit)
            mine = (place >> bit) % 2
            self.left[half].remove(bit)
            out = pick(self.parts[half], 1 - mine, axis)
            self.keep.append(pick(self.parts[half], mine, axis))
            self.sent.append(out)
            self.received.append(lax.ppermute(out, "xy", [(i, i ^ (1 << bit)) for i in range(self.planes)]))

    def add(self, *done):
        self.parts = [total(k, after(r, *done)) for k, r in zip(self.keep, self.received)]

    def result(self):
        return jnp.concatenate(self.parts)


class Spread:
    def __init__(self, value, nseq):
        self.nseq, self.rows = nseq, value.shape[0] // nseq
        self.me = lax.axis_index("seq")
        quarter = lambda which: lax.dynamic_slice_in_dim(value, (which % nseq) * self.rows, self.rows, 0)
        self.keep = quarter(self.me)
        self.sent = [quarter(self.me + d) for d in range(1, nseq)]
        self.received = [self.shift(q, d) for d, q in enumerate(self.sent, 1)]

    def shift(self, value, distance):
        return lax.ppermute(value, "seq", [(i, (i + distance) % self.nseq) for i in range(self.nseq)])

    def add(self, *done):
        parts = [self.keep] + [after(r, *done) for r in self.received]
        self.keep = sum(p.astype(jnp.float32) for p in parts).astype(jnp.bfloat16)
        self.received = [self.shift(self.keep, d) for d in range(1, self.nseq)]

    def result(self, *done):
        whole = jnp.zeros((self.nseq * self.rows,) + self.keep.shape[1:], jnp.bfloat16)
        for d, part in enumerate([self.keep] + [after(r, *done) for r in self.received]):
            start = ((self.me - d) % self.nseq) * self.rows
            whole = lax.dynamic_update_slice_in_dim(whole, part, start, 0)
        return whole


def either(core, own, other, axis):
    return jnp.where(core == 0, jnp.concatenate([own, other], axis), jnp.concatenate([other, own], axis))


def per_device(
    tokens, doc_lengths, qkv_weight, q_bias, v_bias, out_weight, out_bias, norm1_gain, norm1_bias,
    ff_in_weight, ff_in_bias, ff_out_weight, ff_out_bias, norm2_gain, norm2_bias, out_cotangent,
):
    bf16, f32 = jnp.bfloat16, jnp.float32
    fsdp = ("xy", "core")
    nseq = lax.axis_size("seq")
    planes = lax.axis_size("xy")
    shards = planes * CORES
    core = lax.axis_index("core")
    odd = lax.axis_index("seq") % 2
    micro, run, width = tokens.shape[1:]
    assert micro == 2 and nseq == 4
    stretch = run * nseq
    mine = width // CORES
    rows = width // shards
    first, second = routes(nseq)
    back = [[(b, a) for a, b in route] for route in (first, second)]

    def spread(x):
        halves = [lax.dynamic_index_in_dim(x[0], which, 0, keepdims=False) for which in (odd, 1 - odd)]
        return [lax.ppermute(h, ("core", "seq"), r) for h, r in zip(halves, (first, second))]

    pieces = spread(tokens)
    lengths = jnp.stack([doc_lengths[0], swap(doc_lengths[0])])
    z = lax.axis_index("seq")
    theirs = jnp.where(z // 2 == core, lengths[0], lengths[1])
    ends = jnp.cumsum(lax.dynamic_index_in_dim(theirs, odd, 0, keepdims=False)).astype(jnp.int32)
    seg = doc_ids(ends, stretch)
    seg_col = jnp.broadcast_to(seg[:, None], (stretch, LANES))
    seg_row = seg[None]
    mask = (odd + 2 * core).astype(jnp.int32)[None]

    pairs = mine // LANES
    own_columns = qkv_weight.reshape(rows, 3, CORES, pairs, LANES)
    own_columns = jnp.moveaxis(own_columns, (2, 3), (0, 2)).reshape(CORES, rows, 3 * mine)
    kept = pick(own_columns, core)
    w_mine = either(core, kept, swap(pick(own_columns, 1 - core)), 0)
    w_mine = lax.all_gather(w_mine, "xy", axis=0, tiled=True)
    small = [q_bias, v_bias, out_bias, norm1_gain, norm1_bias, ff_out_bias, norm2_gain, norm2_bias]
    inner = ff_in_bias.shape[0] // rows
    small = jnp.concatenate([jnp.stack(small), ff_in_bias.reshape(inner, rows)])
    vectors = lax.all_gather(small, fsdp, axis=0, tiled=False).astype(f32)
    bias_in = vectors[:, 8:].reshape(1, -1)
    vectors = jnp.moveaxis(vectors[:, :8], 0, 1).reshape(8, width)
    bias_q, bias_v = vectors[0], vectors[1]
    norms = jnp.concatenate([vectors[2:], jnp.zeros((2, width), f32)])
    wide = [ff_in_weight[:, i * width : (i + 1) * width] for i in range(inner)]
    packed = lax.all_gather(jnp.concatenate([ff_out_weight] + wide + [out_weight]), fsdp, axis=0, tiled=False)
    if rows % 16:
        parts = [packed[:, : inner * rows].reshape(-1, width)]
        parts += [packed[:, (inner + i) * rows : (inner + i + 1) * rows].reshape(width, width) for i in range(inner + 1)]
        packed = jnp.concatenate(parts)[None]

    own_slice = lambda v: lax.dynamic_slice_in_dim(v, core * mine, mine, 0).reshape(pairs, LANES)
    one = jnp.ones((pairs, LANES), f32)
    bias_mine = jnp.stack([own_slice(bias_q), 0.0 * one, own_slice(bias_v)], axis=1).reshape(-1)
    scale = jnp.stack([HEAD_DIM**-0.5 * one, one, one], axis=1).reshape(-1)
    x_own = after(jnp.concatenate(pieces), norms, bias_in)
    x_sib = jnp.concatenate([swap(p) for p in pieces])
    projected = [((mm(x, w_mine, NN) + bias_mine) * scale).astype(bf16) for x in (x_own, x_sib)]
    ctx_own, ctx_sib, lse = attend_forward(mask, ends, *projected, seg_col, seg_row, run)
    ctx_far = swap(ctx_sib)

    cot = jnp.concatenate(spread(after(out_cotangent, *projected)))
    result, hidden_low, act_low, grad_down, grad_pre, grad_one, grad_attn, dctx_own, dctx_far, sums, in_sums = middle(
        core.astype(jnp.int32)[None], x_own, ctx_own, ctx_far, cot, norms, bias_in, packed
    )
    dctx_far = swap(dctx_far)
    output = [lax.ppermute(result[i * run : (i + 1) * run], ("core", "seq"), back[i]) for i in range(2)]

    def cores(blocks):
        return pick(blocks, core, 1), swap(pick(blocks, 1 - core, 1))

    inner_blocks = ff_in_bias.shape[0] * shards // width
    down_rows = ff_out_weight.shape[0]
    vector = [jnp.moveaxis(sums[:6].reshape(6, shards, rows), 1, 0), in_sums.reshape(shards, inner, rows)]
    vector = jnp.concatenate(vector, axis=1).astype(bf16)
    vector = jnp.pad(vector, ((0, 0), (0, 32 - vector.shape[1]), (0, width - rows)))
    if rows % 16 == 0:
        kept, sent = gradients(
            core.astype(jnp.int32)[None], act_low, hidden_low, grad_down, grad_pre, ctx_own, ctx_far, grad_attn, vector, planes
        )
        joined = kept, swap(sent)
    else:
        down_grad = cores(mm(act_low, grad_down, TN).astype(bf16).reshape(planes, CORES, -1, width))
        in_grad = cores(mm(hidden_low, grad_pre, TN).astype(bf16).reshape(planes, CORES, rows, -1))
        out_grad = [mm(c, grad_attn, TN).astype(bf16) for c in (ctx_own, ctx_far)]
        out_grad = cores(either(core, *out_grad, 0).reshape(planes, CORES, rows, width))
        vector = cores(vector.reshape(planes, CORES, 32, width))
        joined = []
        for which in range(2):
            wide = in_grad[which]
            wide = [wide[:, :, i * width : (i + 1) * width] for i in range(inner_blocks)]
            joined.append(jnp.concatenate([down_grad[which]] + wide + [out_grad[which], vector[which]], axis=1))
    early = Halving(total(*joined), planes)
    early.send(0)
    progress = [early]

    def advance(*done):
        if len(progress) > 1:
            return []
        early.add(*done)
        step = early.steps - len(early.left[0])
        if step < early.steps:
            early.send(step)
            return early.sent
        progress.append(Spread(early.result(), nseq))
        return progress[1].sent

    def attend(pair, *ready):
        held = after(mask, *ready)
        return attend_backward(
            pair, held, ends, *projected, ctx_own, ctx_sib, dctx_own, dctx_far, seg_col, seg_row, lse, run
        )

    def weight_sums(near, far):
        matrix = (mm(x_own, near, TN) + mm(x_sib, far, TN)).astype(bf16)
        column = (jnp.sum(near.astype(f32), axis=0) + jnp.sum(far.astype(f32), axis=0)).astype(bf16)
        column = jnp.pad(column[None], ((0, 15), (0, 0)))
        column = jnp.broadcast_to(column, (planes,) + column.shape)
        return jnp.concatenate([matrix.reshape(planes, CORES * rows, -1), column], axis=1)

    grads = [attend(0, *early.sent)]
    for pair in range(1, pairs):
        sent = advance(grads[-1][0])
        if pair == pairs - 1:
            output = [after(o, grads[-1][0]) for o in output]
            sent = list(sent) + output
        grads.append(attend(pair, *sent))
    while len(progress) == 1:
        advance(grads[-1][0])
    early_sum = progress[1]

    early_sum.add(grads[-1][0])
    near = jnp.concatenate([g[0] for g in grads], axis=1)
    far = after(jnp.concatenate([g[1] for g in grads], axis=1), early_sum.keep)
    grad_far = swap(mm(far, w_mine, NT).astype(bf16))
    input_grad = (grad_one + mm(near, w_mine, NT) + grad_far.astype(f32)).astype(bf16)
    returned = [lax.ppermute(input_grad[i * run : (i + 1) * run], ("core", "seq"), back[i]) for i in range(2)]
    near, far = after((near, far), input_grad)
    qkv_halves = Halving(weight_sums(near, far), planes)
    for step in range(qkv_halves.steps):
        qkv_halves.send(step)
        qkv_halves.add(input_grad)
    qkv_sum = Spread(qkv_halves.result(), nseq)
    qkv_sum.add(*returned)
    input_grad = jnp.where(odd == 0, jnp.stack(returned), jnp.stack(returned[::-1]))[None].astype(f32)
    early_total = early_sum.result(qkv_sum.keep)
    qkv_total = qkv_sum.result()

    down_final = early_total[:down_rows].astype(f32)
    wide = [early_total[down_rows + i * rows : down_rows + (i + 1) * rows] for i in range(inner_blocks)]
    in_final = jnp.concatenate(wide, axis=1).astype(f32)
    at = down_rows + inner_blocks * rows
    out_final = early_total[at : at + rows].astype(f32)
    at = at + rows
    line = early_total[at : at + 32, :rows].astype(f32)
    out_bias_final, g1, b1, down_bias_final, g2, b2 = [line[i] for i in range(6)]
    in_bias_final = line[6 : 6 + inner].reshape(-1)

    part = qkv_total
    column = part[CORES * rows]
    other = swap(jnp.concatenate([lax.dynamic_slice_in_dim(part, (1 - core) * rows, rows, 0), part[CORES * rows : CORES * rows + 16]]))
    own_block = lax.dynamic_slice_in_dim(part, core * rows, rows, 0)
    spread_out = lambda v: jnp.moveaxis(v.reshape(-1, pairs, 3, LANES), 2, 1).reshape(-1, 3, 1, mine)
    qkv_final = either(core, spread_out(own_block), spread_out(other[:rows]), 2).reshape(rows, 3 * width).astype(f32)
    sums = either(core, spread_out(column), spread_out(other[rows]), 2).reshape(3, width)
    shard = lax.axis_index("xy") * CORES + core
    q_final = lax.dynamic_slice_in_dim(sums[0], shard * rows, rows, 0).astype(f32)
    v_final = lax.dynamic_slice_in_dim(sums[2], shard * rows, rows, 0).astype(f32)
    output = [after(o, qkv_sum.keep) for o in output]
    output = jnp.where(odd == 0, jnp.stack(output), jnp.stack(output[::-1]))[None]
    return (
        output, input_grad, qkv_final, q_final, v_final, out_final, out_bias_final, g1, b1, in_final,
        in_bias_final, down_final, down_bias_final, g2, b2,
    )


def solution(mesh):
    fsdp, nseq = mesh.shape["fsdp"], mesh.shape["seq"]
    fine = Mesh(mesh.devices.reshape(fsdp // CORES, CORES, nseq), ("xy", "core", "seq"))
    shard = ("xy", "core")
    stream, matrix, vector = P(shard, None, "seq", None), P(shard, None), P(shard)
    return jax.shard_map(
        per_device,
        mesh=fine,
        in_specs=(
            stream, P(shard, None, None), matrix, vector, vector, matrix, vector, vector, vector,
            matrix, vector, matrix, vector, vector, vector, stream,
        ),
        out_specs=(
            stream, stream, matrix, vector, vector, matrix, vector, vector, vector,
            matrix, vector, matrix, vector, vector, vector,
        ),
        check_vma=False,
    )
```

```python
import functools
import math

import jax
import jax.numpy as jnp
from jax import lax
from jax.experimental import pallas as pl
from jax.experimental.pallas import tpu as pltpu
from jax.sharding import Mesh
from jax.sharding import PartitionSpec as P

HEAD_DIM = 64
LANES = 128
NEG = -1e30
TILE = 256
VALUE_ROWS = HEAD_DIM + 16
KEY_TILES = 1
QUERY_TILES = 1
NT = (((1,), (1,)), ((), ()))
NN = (((1,), (0,)), ((), ()))
TN = (((0,), (0,)), ((), ()))


def mm(left, right, dims):
    return lax.dot_general(left, right, dims, preferred_element_type=jnp.float32)


def key_tiles(ends_ref, first, last, tile, total):
    low = jnp.int32(0)
    high = jnp.int32(total)
    for doc in reversed(range(ends_ref.shape[0])):
        end = ends_ref[doc]
        low = jnp.maximum(low, jnp.where(end <= first, end, 0))
        high = jnp.minimum(high, jnp.where(end > last, end, total))
    return low // tile, (high + tile - 1) // tile


def spans(first, after, count, tiles):
    steps = (after - first + count - 1) // count
    return jnp.minimum(first, tiles - steps * count), steps


def lane_halves(x, fill):
    lane = lax.broadcasted_iota(jnp.int32, x.shape, 1)
    fill = jnp.full_like(x, fill)
    return jnp.where(lane < HEAD_DIM, x, fill), jnp.where(lane < HEAD_DIM, fill, x)


def piece_copies(halves, columns, place, scratch, slot, sems, run, mask, inbound):
    copies = []
    pieces = halves[0].shape[0] // run
    for half, ref in enumerate(halves):
        for part in range(pieces):
            index = half * pieces + part
            natural = pl.multiple_of(jnp.bitwise_xor(mask, index) * run, run)
            outer = ref.at[pl.ds(part * run, run), pl.ds(columns, LANES)]
            inner = scratch.at[place, pl.ds(natural, run), :]
            ends = (outer, inner) if inbound else (inner, outer)
            copies.append(pltpu.make_async_copy(ends[0], ends[1], sems.at[slot, index]))
    return copies


def forward_kernel(run, mask_ref, ends_ref, own, sib, seg_col, seg_row, ctx_own, ctx_sib, lse_ref, qkv, out, turned, acc, top, sems, out_sems):
    total = qkv.shape[1]
    pairs = out.shape[0]
    mask = mask_ref[0]

    def loads(pair):
        copies = []
        for kind in range(3):
            copies += piece_copies(
                (own, sib), (3 * pair + kind) * LANES, kind * pairs + pair, qkv, kind * pairs + pair, sems, run, mask, True
            )
        return copies

    for pair in range(pairs):
        for copy in loads(pair):
            copy.start()

    for head in range(2 * pairs):
        turned[head, HEAD_DIM:, :] = jnp.ones((VALUE_ROWS - HEAD_DIM, total), jnp.bfloat16)
    for pair in range(pairs):
        for copy in loads(pair):
            copy.wait()

    @pl.loop(0, total // TILE)
    def _(block):
        rows = pl.multiple_of(block * TILE, TILE)
        for pair in range(pairs):
            values = qkv[2 * pairs + pair, pl.ds(rows, TILE), :].astype(jnp.float32).T.astype(jnp.bfloat16)
            for head in range(2):
                turned[2 * pair + head, :HEAD_DIM, pl.ds(rows, TILE)] = values[head * HEAD_DIM : (head + 1) * HEAD_DIM]

    @pl.loop(0, total // TILE)
    def _(block):
        rows = pl.multiple_of(block * TILE, TILE)
        q_heads = sum([list(lane_halves(qkv[pair, pl.ds(rows, TILE), :], 0.0)) for pair in range(pairs)], [])
        segq = seg_row[:, pl.ds(rows, TILE)]
        first, after = key_tiles(ends_ref, rows, rows + TILE - 1, TILE, total)
        acc[...] = jnp.zeros_like(acc)
        top[...] = jnp.full_like(top, NEG)

        first, steps = spans(first, after, KEY_TILES, total // TILE)

        @pl.loop(0, steps)
        def _(step):
            at = pl.multiple_of((first + step * KEY_TILES) * TILE, TILE)
            keys = [qkv[pairs + pair, pl.ds(at, KEY_TILES * TILE), :] for pair in range(pairs)]
            segk = seg_col[pl.ds(at, KEY_TILES * TILE), :]
            same = jnp.concatenate([segk] * (TILE // LANES), axis=1) == segq

            def scores_of(head):
                return jnp.where(same, mm(keys[head // 2], q_heads[head], NT), NEG)

            queue = [scores_of(head) for head in range(6)]
            for head in range(2 * pairs):
                if head + 6 < 2 * pairs:
                    queue.append(scores_of(head + 6))
                scores = queue.pop(0)
                old = top[head, 0:1]
                new = jnp.maximum(old, jnp.max(scores, axis=0, keepdims=True))
                probs = jnp.exp(scores - new).astype(jnp.bfloat16)
                acc[head] = acc[head] * jnp.exp(old - new) + mm(turned[head, :, pl.ds(at, KEY_TILES * TILE)], probs, NN)
                top[head] = jnp.broadcast_to(new, (8, TILE))

        for pair in range(pairs):
            parts = []
            for head in (2 * pair, 2 * pair + 1):
                weight = acc[head, HEAD_DIM : HEAD_DIM + 1]
                parts.append(acc[head, :HEAD_DIM] / weight)
                lse_ref[head, :, pl.ds(rows, TILE)] = top[head] + jnp.log(acc[head, HEAD_DIM : HEAD_DIM + 8])
            out[pair, pl.ds(rows, TILE), :] = jnp.concatenate(parts, axis=0).T.astype(jnp.bfloat16)

    for pair in range(pairs):
        for copy in piece_copies((ctx_own, ctx_sib), pair * LANES, pair, out, pair, out_sems, run, mask, False):
            copy.start()
    for pair in range(pairs):
        for copy in piece_copies((ctx_own, ctx_sib), pair * LANES, pair, out, pair, out_sems, run, mask, False):
            copy.wait()


def attend_forward(mask, ends, own, sib, seg_col, seg_row, run):
    half, columns = own.shape
    total = 2 * half
    pairs = columns // (3 * LANES)
    pieces = total // run
    any_spec = pl.BlockSpec(memory_space=pl.ANY)
    vmem = pl.BlockSpec(memory_space=pltpu.VMEM)
    smem = pl.BlockSpec(memory_space=pltpu.SMEM)
    return pl.pallas_call(
        functools.partial(forward_kernel, run),
        out_shape=(
            jax.ShapeDtypeStruct((half, pairs * LANES), jnp.bfloat16),
            jax.ShapeDtypeStruct((half, pairs * LANES), jnp.bfloat16),
            jax.ShapeDtypeStruct((2 * pairs, 8, total), jnp.float32),
        ),
        in_specs=[smem, smem, any_spec, any_spec, vmem, vmem],
        out_specs=(any_spec, any_spec, vmem),
        scratch_shapes=[
            pltpu.VMEM((3 * pairs, total, LANES), jnp.bfloat16),
            pltpu.VMEM((pairs, total, LANES), jnp.bfloat16),
            pltpu.VMEM((2 * pairs, VALUE_ROWS, total), jnp.bfloat16),
            pltpu.VMEM((2 * pairs, VALUE_ROWS, TILE), jnp.float32),
            pltpu.VMEM((2 * pairs, 8, TILE), jnp.float32),
            pltpu.SemaphoreType.DMA((3 * pairs, pieces)),
            pltpu.SemaphoreType.DMA((pairs, pieces)),
        ],
        compiler_params=pltpu.CompilerParams(vmem_limit_bytes=40 << 20),
        cost_estimate=pl.CostEstimate(flops=1_000_000_000, bytes_accessed=1_000_000, transcendentals=0),
        name="attend_forward",
    )(mask, ends, own, sib, seg_col, seg_row)


def backward_kernel(
    run, pair, mask_ref, ends_ref, own, sib, ctx_own, ctx_sib, dctx_own, dctx_sib, seg_col, seg_row, lse_ref,
    d_own, d_sib, qkv, ctx, out, turned, delta, dq, dkv, sems, out_sems
):
    total = qkv.shape[1]
    mask = mask_ref[0]
    loads, stores = [], []
    for kind in range(3):
        loads += piece_copies((own, sib), (3 * pair + kind) * LANES, kind, qkv, kind, sems, run, mask, True)
        stores += piece_copies((d_own, d_sib), kind * LANES, kind, out, kind, out_sems, run, mask, False)
    loads += piece_copies((ctx_own, ctx_sib), pair * LANES, 0, ctx, 3, sems, run, mask, True)
    loads += piece_copies((dctx_own, dctx_sib), pair * LANES, 1, ctx, 4, sems, run, mask, True)
    for copy in loads:
        copy.start()
    for copy in loads:
        copy.wait()

    @pl.loop(0, total // TILE)
    def _(block):
        rows = pl.multiple_of(block * TILE, TILE)
        product = ctx[0, pl.ds(rows, TILE), :].astype(jnp.float32) * ctx[1, pl.ds(rows, TILE), :].astype(jnp.float32)
        product = product.T
        for head in range(2):
            part = jnp.sum(product[head * HEAD_DIM : (head + 1) * HEAD_DIM], axis=0, keepdims=True)
            delta[head, :, pl.ds(rows, TILE)] = jnp.broadcast_to(part, (8, TILE))
        turned[:, pl.ds(rows, TILE)] = qkv[1, pl.ds(rows, TILE), :].astype(jnp.float32).T.astype(jnp.bfloat16)
        dq[:, pl.ds(rows, TILE)] = jnp.zeros((LANES, TILE), jnp.float32)

    @pl.loop(0, total // TILE)
    def _(block):
        rows = pl.multiple_of(block * TILE, TILE)
        k_heads = lane_halves(qkv[1, pl.ds(rows, TILE), :], 0.0)
        v_heads = lane_halves(qkv[2, pl.ds(rows, TILE), :], 0.0)
        segk = seg_col[pl.ds(rows, TILE), :]
        segk = jnp.concatenate([segk] * (TILE // LANES), axis=1)
        first, after = key_tiles(ends_ref, rows, rows + TILE - 1, TILE, total)
        dkv[...] = jnp.zeros_like(dkv)

        first, steps = spans(first, after, QUERY_TILES, total // TILE)

        @pl.loop(0, steps)
        def _(step):
            at = pl.multiple_of((first + step * QUERY_TILES) * TILE, TILE)
            span = pl.ds(at, QUERY_TILES * TILE)
            queries = qkv[0, span, :]
            grads = ctx[1, span, :]
            q_heads = lane_halves(queries, 0.0)
            g_heads = lane_halves(grads, 0.0)
            same = jnp.concatenate([segk] * QUERY_TILES, axis=1) == seg_row[:, span]
            scores = [mm(k_heads[head], queries, NT) for head in range(2)]
            dprobs = [mm(v_heads[head], grads, NT) for head in range(2)]
            low, dscores = [], []
            for head in range(2):
                probs = jnp.exp(jnp.where(same, scores[head] - lse_ref[2 * pair + head, 0:1, span], NEG))
                low.append(probs.astype(jnp.bfloat16))
                dscores.append((probs * (dprobs[head] - delta[head, 0:1, span])).astype(jnp.bfloat16))
            dkv[1] += mm(low[0], g_heads[0], NN) + mm(low[1], g_heads[1], NN)
            dkv[0] += mm(dscores[0], q_heads[0], NN) + mm(dscores[1], q_heads[1], NN)
            for head in range(2):
                lanes = slice(head * HEAD_DIM, (head + 1) * HEAD_DIM)
                dq[lanes, span] += mm(turned[lanes, pl.ds(rows, TILE)], dscores[head], NN)

        out[1, pl.ds(rows, TILE), :] = dkv[0].astype(jnp.bfloat16)
        out[2, pl.ds(rows, TILE), :] = dkv[1].astype(jnp.bfloat16)

    @pl.loop(0, total // TILE)
    def _(block):
        rows = pl.multiple_of(block * TILE, TILE)
        out[0, pl.ds(rows, TILE), :] = (dq[:, pl.ds(rows, TILE)].T * HEAD_DIM**-0.5).astype(jnp.bfloat16)

    for copy in stores:
        copy.start()
    for copy in stores:
        copy.wait()


def attend_backward(pair, mask, ends, own, sib, ctx_own, ctx_sib, dctx_own, dctx_sib, seg_col, seg_row, lse, run):
    half = own.shape[0]
    total = 2 * half
    pieces = total // run
    any_spec = pl.BlockSpec(memory_space=pl.ANY)
    vmem = pl.BlockSpec(memory_space=pltpu.VMEM)
    smem = pl.BlockSpec(memory_space=pltpu.SMEM)
    return pl.pallas_call(
        functools.partial(backward_kernel, run, pair),
        out_shape=(
            jax.ShapeDtypeStruct((half, 3 * LANES), jnp.bfloat16),
            jax.ShapeDtypeStruct((half, 3 * LANES), jnp.bfloat16),
        ),
        in_specs=[smem, smem] + [any_spec] * 6 + [vmem] * 3,
        out_specs=(any_spec, any_spec),
        scratch_shapes=[
            pltpu.VMEM((3, total, LANES), jnp.bfloat16),
            pltpu.VMEM((2, total, LANES), jnp.bfloat16),
            pltpu.VMEM((3, total, LANES), jnp.bfloat16),
            pltpu.VMEM((LANES, total), jnp.bfloat16),
            pltpu.VMEM((2, 8, total), jnp.float32),
            pltpu.VMEM((LANES, total), jnp.float32),
            pltpu.VMEM((2, TILE, LANES), jnp.float32),
            pltpu.SemaphoreType.DMA((5, pieces)),
            pltpu.SemaphoreType.DMA((3, pieces)),
        ],
        compiler_params=pltpu.CompilerParams(vmem_limit_bytes=24 << 20),
        cost_estimate=pl.CostEstimate(flops=20_000_000_000, bytes_accessed=8_000_000, transcendentals=0),
    )(mask, ends, own, sib, ctx_own, ctx_sib, dctx_own, dctx_sib, seg_col, seg_row, lse)


EPS = 1e-05


def norm_forward(resid, gain, shift):
    mean = jnp.mean(resid, axis=-1, keepdims=True)
    centered = resid - mean
    inv = lax.rsqrt(jnp.mean(centered * centered, axis=-1, keepdims=True) + EPS)
    normed = centered * inv
    return (normed * gain + shift, normed, inv)


def norm_backward(grad, normed, inv, gain):
    scaled = grad * gain
    return inv * (
        scaled
        - jnp.mean(scaled, axis=-1, keepdims=True)
        - normed * jnp.mean(scaled * normed, axis=-1, keepdims=True)
    )


ROWS = 256
CHUNK = 768


def fold(x):
    return jnp.sum(x.reshape(-1, 8, x.shape[1]), axis=0)


def middle_kernel(
    core_ref, x_ref, near_ref, far_ref, cot_ref, vec_ref, in_bias_ref, packed,
    result_ref, low_ref, act_ref, grad_down_ref, grad_pre_ref, grad_one_ref, grad_attn_ref, dnear_ref, dfar_ref,
    sums_ref, in_sums_ref, wo, wi, wd, slope, acc, sums, in_sums, sems
):
    f32, bf16 = jnp.float32, jnp.bfloat16
    mine = near_ref.shape[1]
    chunks = wi.shape[0]
    step = pl.program_id(0)
    core = core_ref[0]
    shards = packed.shape[0]
    rows = packed.shape[1] // (2 * chunks + 1)
    copies = []

    def load(shard, at, count, target):
        copies.append(pltpu.make_async_copy(packed.at[shard, pl.ds(at, count), :], target, sems.at[len(copies)]))

    if shards == 1:
        for place in range(2):
            which = core if place == 0 else 1 - core
            load(0, pl.multiple_of(2 * chunks * rows + which * mine, 16), mine, wo.at[pl.ds(place * mine, mine), :])
    else:
        for place in range(2):
            which = core if place == 0 else 1 - core
            for part in range(shards // 2):
                target = wo.at[pl.ds(place * mine + part * rows, rows), :]
                load(which * (shards // 2) + part, 2 * chunks * rows, rows, target)
    outs = len(copies)
    for chunk in range(chunks):
        for shard in range(shards):
            load(shard, (chunks + chunk) * rows, rows, wi.at[chunk, pl.ds(shard * rows, rows), :])
    for chunk in range(chunks):
        for shard in range(shards):
            first = shard * chunks * rows
            low, high = max(first, chunk * CHUNK), min(first + chunks * rows, (chunk + 1) * CHUNK)
            if low < high:
                load(shard, low - first, high - low, wd.at[chunk, pl.ds(low - chunk * CHUNK, high - low), :])

    @pl.when(step == 0)
    def _():
        for copy in copies:
            copy.start()
        sums[...] = jnp.zeros_like(sums)
        in_sums[...] = jnp.zeros_like(in_sums)
        for copy in copies[:outs]:
            copy.wait()

    bias_out, gain_one, shift_one, bias_down, gain_two, shift_two = [vec_ref[i : i + 1, :] for i in range(6)]
    near, far = near_ref[...], far_ref[...]
    attn = mm(near, wo[:mine], NN) + mm(far, wo[mine:], NN) + bias_out
    hidden, normed_one, inv_one = norm_forward(x_ref[...].astype(f32) + attn, gain_one, shift_one)
    low_ref[...] = hidden.astype(bf16)
    acc[...] = hidden + bias_down

    @pl.when(step == 0)
    def _():
        for copy in copies[outs:]:
            copy.wait()

    @pl.loop(0, chunks)
    def _(chunk):
        columns = pl.ds(pl.multiple_of(chunk * CHUNK, CHUNK), CHUNK)
        pre = mm(low_ref[...], wi[chunk], NN) + in_bias_ref[:, columns]
        cdf = 0.5 * (1.0 + lax.erf(pre * (1.0 / math.sqrt(2.0))))
        density = jnp.exp(-0.5 * pre * pre) * (1.0 / math.sqrt(2.0 * math.pi))
        act = (pre * cdf).astype(bf16)
        act_ref[:, columns] = act
        slope[:, columns] = cdf + pre * density
        acc[...] += mm(act, wd[chunk], NN)

    result, normed_two, inv_two = norm_forward(acc[...], gain_two, shift_two)
    result_ref[...] = result.astype(bf16)
    dy = cot_ref[...].astype(f32)
    grad_two = norm_backward(dy, normed_two, inv_two, gain_two)
    grad_down = grad_two.astype(bf16)
    grad_down_ref[...] = grad_down
    sums[3] += fold(grad_down.astype(f32))
    sums[4] += fold(dy * normed_two)
    sums[5] += fold(dy)
    acc[...] = grad_two

    @pl.loop(0, chunks)
    def _(chunk):
        columns = pl.ds(pl.multiple_of(chunk * CHUNK, CHUNK), CHUNK)
        grad_pre = (mm(grad_down_ref[...], wd[chunk], NT) * slope[:, columns]).astype(bf16)
        grad_pre_ref[:, columns] = grad_pre
        in_sums[:, columns] += fold(grad_pre.astype(f32))
        acc[...] += mm(grad_pre, wi[chunk], NT)

    grad_hidden = acc[...]
    sums[1] += fold(grad_hidden * normed_one)
    sums[2] += fold(grad_hidden)
    grad_one = norm_backward(grad_hidden, normed_one, inv_one, gain_one)
    grad_one_ref[...] = grad_one
    grad_attn = grad_one.astype(bf16)
    grad_attn_ref[...] = grad_attn
    sums[0] += fold(grad_attn.astype(f32))
    dnear_ref[...] = mm(grad_attn, wo[:mine], NT).astype(bf16)
    dfar_ref[...] = mm(grad_attn, wo[mine:], NT).astype(bf16)

    @pl.when(step == pl.num_programs(0) - 1)
    def _():
        sums_ref[...] = jnp.zeros_like(sums_ref)
        for i in range(6):
            sums_ref[i : i + 1, :] = jnp.sum(sums[i], axis=0, keepdims=True)
        in_sums_ref[...] = jnp.sum(in_sums[...], axis=0, keepdims=True)


def middle(core, x, near, far, cot, vec, in_bias, packed):
    count, width = x.shape
    hidden = in_bias.shape[1]
    mine = near.shape[1]
    chunks = hidden // CHUNK
    f32, bf16 = jnp.float32, jnp.bfloat16
    any_spec = pl.BlockSpec(memory_space=pl.ANY)
    block = lambda columns: pl.BlockSpec((ROWS, columns), lambda i: (i, 0))
    whole = lambda rows, columns: pl.BlockSpec((rows, columns), lambda i: (0, 0))
    shape = jax.ShapeDtypeStruct
    return pl.pallas_call(
        middle_kernel,
        grid=(count // ROWS,),
        out_shape=(
            shape((count, width), bf16), shape((count, width), bf16), shape((count, hidden), bf16),
            shape((count, width), bf16), shape((count, hidden), bf16), shape((count, width), f32),
            shape((count, width), bf16), shape((count, mine), bf16), shape((count, mine), bf16),
            shape((8, width), f32), shape((1, hidden), f32),
        ),
        in_specs=[
            pl.BlockSpec(memory_space=pltpu.SMEM), block(width), block(mine), block(mine), block(width),
            whole(8, width), whole(1, hidden), any_spec,
        ],
        out_specs=(
            block(width), block(width), block(hidden), block(width), block(hidden), block(width), block(width),
            block(mine), block(mine), whole(8, width), whole(1, hidden),
        ),
        scratch_shapes=[
            pltpu.VMEM((width, width), bf16),
            pltpu.VMEM((chunks, width, CHUNK), bf16),
            pltpu.VMEM((chunks, CHUNK, width), bf16),
            pltpu.VMEM((ROWS, hidden), f32),
            pltpu.VMEM((ROWS, width), f32),
            pltpu.VMEM((6, 8, width), f32),
            pltpu.VMEM((8, hidden), f32),
            pltpu.SemaphoreType.DMA(((2 * chunks + 1) * max(packed.shape[0], 2),)),
        ],
        compiler_params=pltpu.CompilerParams(vmem_limit_bytes=48 << 20),
        cost_estimate=pl.CostEstimate(flops=20_000_000_000, bytes_accessed=30_000_000, transcendentals=0),
        name="middle",
    )(core, x, near, far, cot, vec, in_bias, packed)


def gradients_kernel(
    rows, core_ref, act_ref, low_ref, down_ref, pre_ref, near_ref, far_ref, attn_ref, vec_ref,
    keep_ref, send_ref, result, sems
):
    step = pl.program_id(0)
    core = core_ref[0]
    shards = low_ref.shape[1] // rows
    chunks = (pl.num_programs(0) - 1) // 2
    blocks = pre_ref.shape[1] * chunks // low_ref.shape[1]
    slot = step % 2

    def wait(which):
        pltpu.make_async_copy(result.at[which], result.at[which], sems.at[which]).wait()

    def put(source, shard_core, plane, at, count, sem):
        target = pl.ds(at, count)

        @pl.when(core == shard_core)
        def _():
            pltpu.make_async_copy(source, keep_ref.at[plane, target, :], sem).start()

        @pl.when(core != shard_core)
        def _():
            pltpu.make_async_copy(source, send_ref.at[plane, target, :], sem).start()

    @pl.when(step >= 2)
    def _():
        wait(slot)

    @pl.when(step < chunks)
    def _():
        result[slot] = mm(act_ref[...], down_ref[...], TN).astype(jnp.bfloat16)
        count = blocks * rows
        here = result.shape[1] // count
        for part in range(here):
            put(result.at[slot, pl.ds(part * count, count), :], part % CORES, step * (here // CORES) + part // CORES, 0, count, sems.at[slot])

    @pl.when(jnp.logical_and(step >= chunks, step < 2 * chunks))
    def _():
        result[slot] = mm(low_ref[...], pre_ref[...], TN).astype(jnp.bfloat16)
        at = pl.multiple_of(blocks * rows + (step - chunks) * rows, 16)
        for shard in range(shards):
            put(result.at[slot, pl.ds(shard * rows, rows), :], shard % CORES, shard // CORES, at, rows, sems.at[slot])

    @pl.when(step == 2 * chunks)
    def _():
        mine = near_ref.shape[1]
        result[slot, :mine] = mm(near_ref[...], attn_ref[...], TN).astype(jnp.bfloat16)
        result[slot, mine:] = mm(far_ref[...], attn_ref[...], TN).astype(jnp.bfloat16)
        half = shards // 2
        for shard in range(shards):
            first = core if shard < half else 1 - core
            plane = first * (half // CORES) + (shard % half) // CORES
            put(result.at[slot, pl.ds(shard * rows, rows), :], shard % CORES, plane, 2 * blocks * rows, rows, sems.at[slot])
        for shard in range(shards):
            put(vec_ref.at[shard], shard % CORES, shard // CORES, (2 * blocks + 1) * rows, vec_ref.shape[1], sems.at[2 + shard])
        wait(0)
        wait(1)
        for shard in range(shards):
            pltpu.make_async_copy(vec_ref.at[shard], vec_ref.at[shard], sems.at[2 + shard]).wait()


def gradients(core, act, low, down, pre, near, far, attn, vec, planes):
    count, width = low.shape
    rows = width // (planes * CORES)
    chunks = pre.shape[1] // width
    total_rows = (2 * chunks + 1) * rows + vec.shape[1]
    whole = lambda x: pl.BlockSpec(x.shape, lambda i: (0,) * x.ndim)
    out = jax.ShapeDtypeStruct((planes, total_rows, width), jnp.bfloat16)
    return pl.pallas_call(
        functools.partial(gradients_kernel, rows),
        grid=(2 * chunks + 1,),
        out_shape=(out, out),
        in_specs=[
            pl.BlockSpec(memory_space=pltpu.SMEM),
            pl.BlockSpec((count, width), lambda i: (0, jnp.minimum(i, chunks - 1))),
            whole(low), whole(down),
            pl.BlockSpec((count, width), lambda i: (0, jnp.clip(i - chunks, 0, chunks - 1))),
            whole(near), whole(far), whole(attn), whole(vec),
        ],
        out_specs=(pl.BlockSpec(memory_space=pl.ANY),) * 2,
        scratch_shapes=[
            pltpu.VMEM((2, width, width), jnp.bfloat16),
            pltpu.SemaphoreType.DMA((2 + planes * CORES,)),
        ],
        compiler_params=pltpu.CompilerParams(vmem_limit_bytes=48 << 20),
        cost_estimate=pl.CostEstimate(flops=11_000_000_000, bytes_accessed=30_000_000, transcendentals=0),
        name="gradients",
    )(core, act, low, down, pre, near, far, attn, vec)


def doc_ids(ends, count):
    places = jnp.arange(count, dtype=jnp.int32)
    return jnp.sum((places[:, None] >= ends[None, :]).astype(jnp.int32), axis=1)


CORES = 2


def routes(nseq):
    first, second = [], []
    for core in range(CORES):
        for z in range(nseq):
            source = core * nseq + z
            first.append((source, (z // 2) * nseq + 2 * core + z % 2))
            second.append((source, (z // 2) * nseq + 2 * core + 1 - z % 2))
    return first, second


def swap(x):
    return lax.ppermute(x, "core", [(0, 1), (1, 0)])


def after(value, *done):
    return lax.optimization_barrier((value, done))[0]


def pick(value, which, axis=0):
    return lax.dynamic_index_in_dim(value, which, axis, keepdims=False)


def total(keep, received):
    return (keep.astype(jnp.float32) + received.astype(jnp.float32)).astype(jnp.bfloat16)


class Halving:
    def __init__(self, blocks, planes):
        bits = planes.bit_length() - 1
        rows = blocks.shape[1]
        self.planes = planes
        self.orders = (list(range(bits)), list(range(bits))[::-1])
        self.left = [list(range(bits))[::-1] for _ in range(2)]
        parts = (blocks[:, : rows // 2], blocks[:, rows // 2 :])
        self.parts = [p.reshape((2,) * bits + p.shape[1:]) for p in parts]
        self.steps = bits

    def send(self, step):
        place = lax.axis_index("xy")
        self.keep, self.received, self.sent = [], [], []
        for half in range(2):
            bit = self.orders[half][step]
            axis = self.left[half].index(bit)
            mine = (place >> bit) % 2
            self.left[half].remove(bit)
            out = pick(self.parts[half], 1 - mine, axis)
            self.keep.append(pick(self.parts[half], mine, axis))
            self.sent.append(out)
            self.received.append(lax.ppermute(out, "xy", [(i, i ^ (1 << bit)) for i in range(self.planes)]))

    def add(self, *done):
        self.parts = [total(k, after(r, *done)) for k, r in zip(self.keep, self.received)]

    def result(self):
        return jnp.concatenate(self.parts)


class Spread:
    def __init__(self, value, nseq):
        self.nseq, self.rows = nseq, value.shape[0] // nseq
        self.me = lax.axis_index("seq")
        quarter = lambda which: lax.dynamic_slice_in_dim(value, (which % nseq) * self.rows, self.rows, 0)
        self.keep = quarter(self.me)
        self.sent = [quarter(self.me + d) for d in range(1, nseq)]
        self.received = [self.shift(q, d) for d, q in enumerate(self.sent, 1)]

    def shift(self, value, distance):
        return lax.ppermute(value, "seq", [(i, (i + distance) % self.nseq) for i in range(self.nseq)])

    def add(self, *done):
        parts = [self.keep] + [after(r, *done) for r in self.received]
        self.keep = sum(p.astype(jnp.float32) for p in parts).astype(jnp.bfloat16)
        self.received = [self.shift(self.keep, d) for d in range(1, self.nseq)]

    def result(self, *done):
        whole = jnp.zeros((self.nseq * self.rows,) + self.keep.shape[1:], jnp.bfloat16)
        for d, part in enumerate([self.keep] + [after(r, *done) for r in self.received]):
            start = ((self.me - d) % self.nseq) * self.rows
            whole = lax.dynamic_update_slice_in_dim(whole, part, start, 0)
        return whole


def either(core, own, other, axis):
    return jnp.where(core == 0, jnp.concatenate([own, other], axis), jnp.concatenate([other, own], axis))


def per_device(
    tokens, doc_lengths, qkv_weight, q_bias, v_bias, out_weight, out_bias, norm1_gain, norm1_bias,
    ff_in_weight, ff_in_bias, ff_out_weight, ff_out_bias, norm2_gain, norm2_bias, out_cotangent,
):
    bf16, f32 = jnp.bfloat16, jnp.float32
    fsdp = ("xy", "core")
    nseq = lax.axis_size("seq")
    planes = lax.axis_size("xy")
    shards = planes * CORES
    core = lax.axis_index("core")
    odd = lax.axis_index("seq") % 2
    micro, run, width = tokens.shape[1:]
    assert micro == 2 and nseq == 4
    stretch = run * nseq
    mine = width // CORES
    rows = width // shards
    first, second = routes(nseq)
    back = [[(b, a) for a, b in route] for route in (first, second)]

    def spread(x):
        halves = [lax.dynamic_index_in_dim(x[0], which, 0, keepdims=False) for which in (odd, 1 - odd)]
        return [lax.ppermute(h, ("core", "seq"), r) for h, r in zip(halves, (first, second))]

    pieces = spread(tokens)
    lengths = jnp.stack([doc_lengths[0], swap(doc_lengths[0])])
    z = lax.axis_index("seq")
    theirs = jnp.where(z // 2 == core, lengths[0], lengths[1])
    ends = jnp.cumsum(lax.dynamic_index_in_dim(theirs, odd, 0, keepdims=False)).astype(jnp.int32)
    seg = doc_ids(ends, stretch)
    seg_col = jnp.broadcast_to(seg[:, None], (stretch, LANES))
    seg_row = seg[None]
    mask = (odd + 2 * core).astype(jnp.int32)[None]

    pairs = mine // LANES
    own_columns = qkv_weight.reshape(rows, 3, CORES, pairs, LANES)
    own_columns = jnp.moveaxis(own_columns, (2, 3), (0, 2)).reshape(CORES, rows, 3 * mine)
    kept = pick(own_columns, core)
    w_mine = either(core, kept, swap(pick(own_columns, 1 - core)), 0)
    w_mine = lax.all_gather(w_mine, "xy", axis=0, tiled=True)
    small = [q_bias, v_bias, out_bias, norm1_gain, norm1_bias, ff_out_bias, norm2_gain, norm2_bias]
    inner = ff_in_bias.shape[0] // rows
    small = jnp.concatenate([jnp.stack(small), ff_in_bias.reshape(inner, rows)])
    vectors = lax.all_gather(small, fsdp, axis=0, tiled=False).astype(f32)
    bias_in = vectors[:, 8:].reshape(1, -1)
    vectors = jnp.moveaxis(vectors[:, :8], 0, 1).reshape(8, width)
    bias_q, bias_v = vectors[0], vectors[1]
    norms = jnp.concatenate([vectors[2:], jnp.zeros((2, width), f32)])
    wide = [ff_in_weight[:, i * width : (i + 1) * width] for i in range(inner)]
    packed = lax.all_gather(jnp.concatenate([ff_out_weight] + wide + [out_weight]), fsdp, axis=0, tiled=False)
    if rows % 16:
        parts = [packed[:, : inner * rows].reshape(-1, width)]
        parts += [packed[:, (inner + i) * rows : (inner + i + 1) * rows].reshape(width, width) for i in range(inner + 1)]
        packed = jnp.concatenate(parts)[None]

    own_slice = lambda v: lax.dynamic_slice_in_dim(v, core * mine, mine, 0).reshape(pairs, LANES)
    one = jnp.ones((pairs, LANES), f32)
    bias_mine = jnp.stack([own_slice(bias_q), 0.0 * one, own_slice(bias_v)], axis=1).reshape(-1)
    scale = jnp.stack([HEAD_DIM**-0.5 * one, one, one], axis=1).reshape(-1)
    x_own = after(jnp.concatenate(pieces), norms, bias_in)
    x_sib = jnp.concatenate([swap(p) for p in pieces])
    projected = [((mm(x, w_mine, NN) + bias_mine) * scale).astype(bf16) for x in (x_own, x_sib)]
    ctx_own, ctx_sib, lse = attend_forward(mask, ends, *projected, seg_col, seg_row, run)
    ctx_far = swap(ctx_sib)

    cot = jnp.concatenate(spread(after(out_cotangent, *projected)))
    result, hidden_low, act_low, grad_down, grad_pre, grad_one, grad_attn, dctx_own, dctx_far, sums, in_sums = middle(
        core.astype(jnp.int32)[None], x_own, ctx_own, ctx_far, cot, norms, bias_in, packed
    )
    dctx_far = swap(dctx_far)
    output = [lax.ppermute(result[i * run : (i + 1) * run], ("core", "seq"), back[i]) for i in range(2)]

    def cores(blocks):
        return pick(blocks, core, 1), swap(pick(blocks, 1 - core, 1))

    inner_blocks = ff_in_bias.shape[0] * shards // width
    down_rows = ff_out_weight.shape[0]
    vector = [jnp.moveaxis(sums[:6].reshape(6, shards, rows), 1, 0), in_sums.reshape(shards, inner, rows)]
    vector = jnp.concatenate(vector, axis=1).astype(bf16)
    vector = jnp.pad(vector, ((0, 0), (0, 32 - vector.shape[1]), (0, width - rows)))
    if rows % 16 == 0:
        kept, sent = gradients(
            core.astype(jnp.int32)[None], act_low, hidden_low, grad_down, grad_pre, ctx_own, ctx_far, grad_attn, vector, planes
        )
        joined = kept, swap(sent)
    else:
        down_grad = cores(mm(act_low, grad_down, TN).astype(bf16).reshape(planes, CORES, -1, width))
        in_grad = cores(mm(hidden_low, grad_pre, TN).astype(bf16).reshape(planes, CORES, rows, -1))
        out_grad = [mm(c, grad_attn, TN).astype(bf16) for c in (ctx_own, ctx_far)]
        out_grad = cores(either(core, *out_grad, 0).reshape(planes, CORES, rows, width))
        vector = cores(vector.reshape(planes, CORES, 32, width))
        joined = []
        for which in range(2):
            wide = in_grad[which]
            wide = [wide[:, :, i * width : (i + 1) * width] for i in range(inner_blocks)]
            joined.append(jnp.concatenate([down_grad[which]] + wide + [out_grad[which], vector[which]], axis=1))
    early = Halving(total(*joined), planes)
    early.send(0)
    progress = [early]

    def advance(*done):
        if len(progress) > 1:
            return []
        early.add(*done)
        step = early.steps - len(early.left[0])
        if step < early.steps:
            early.send(step)
            return early.sent
        progress.append(Spread(early.result(), nseq))
        return progress[1].sent

    def attend(pair, *ready):
        held = after(mask, *ready)
        return attend_backward(
            pair, held, ends, *projected, ctx_own, ctx_sib, dctx_own, dctx_far, seg_col, seg_row, lse, run
        )

    def weight_sums(near, far):
        matrix = (mm(x_own, near, TN) + mm(x_sib, far, TN)).astype(bf16)
        column = (jnp.sum(near.astype(f32), axis=0) + jnp.sum(far.astype(f32), axis=0)).astype(bf16)
        column = jnp.pad(column[None], ((0, 15), (0, 0)))
        column = jnp.broadcast_to(column, (planes,) + column.shape)
        return jnp.concatenate([matrix.reshape(planes, CORES * rows, -1), column], axis=1)

    grads = [attend(0, *early.sent)]
    for pair in range(1, pairs):
        sent = advance(grads[-1][0])
        if pair == pairs - 1:
            output = [after(o, grads[-1][0]) for o in output]
            sent = list(sent) + output
        grads.append(attend(pair, *sent))
    while len(progress) == 1:
        advance(grads[-1][0])
    early_sum = progress[1]

    early_sum.add(grads[-1][0])
    near = jnp.concatenate([g[0] for g in grads], axis=1)
    far = after(jnp.concatenate([g[1] for g in grads], axis=1), early_sum.keep)
    grad_far = mm(far, w_mine, NT).astype(bf16)
    grad_far = swap(grad_far)
    input_grad = (grad_one + mm(near, w_mine, NT) + grad_far.astype(f32)).astype(bf16)
    returned = [lax.ppermute(input_grad[i * run : (i + 1) * run], ("core", "seq"), back[i]) for i in range(2)]
    near, far = after((near, far), input_grad)
    blocks = weight_sums(near, far)
    qkv_halves = Halving(blocks, planes)
    for step in range(qkv_halves.steps):
        qkv_halves.send(step)
        qkv_halves.add(input_grad)
    qkv_sum = Spread(qkv_halves.result(), nseq)
    qkv_sum.add(*returned)
    input_grad = jnp.where(odd == 0, jnp.stack(returned), jnp.stack(returned[::-1]))[None].astype(f32)
    early_total = early_sum.result(qkv_sum.keep)
    qkv_total = qkv_sum.result()

    down_final = early_total[:down_rows].astype(f32)
    wide = [early_total[down_rows + i * rows : down_rows + (i + 1) * rows] for i in range(inner_blocks)]
    in_final = jnp.concatenate(wide, axis=1).astype(f32)
    at = down_rows + inner_blocks * rows
    out_final = early_total[at : at + rows].astype(f32)
    at = at + rows
    line = early_total[at : at + 32, :rows].astype(f32)
    out_bias_final, g1, b1, down_bias_final, g2, b2 = [line[i] for i in range(6)]
    in_bias_final = line[6 : 6 + inner].reshape(-1)

    part = qkv_total
    column = part[CORES * rows]
    other = swap(jnp.concatenate([lax.dynamic_slice_in_dim(part, (1 - core) * rows, rows, 0), part[CORES * rows : CORES * rows + 16]]))
    own_block = lax.dynamic_slice_in_dim(part, core * rows, rows, 0)
    spread_out = lambda v: jnp.moveaxis(v.reshape(-1, pairs, 3, LANES), 2, 1).reshape(-1, 3, 1, mine)
    qkv_final = either(core, spread_out(own_block), spread_out(other[:rows]), 2).reshape(rows, 3 * width).astype(f32)
    sums = either(core, spread_out(column), spread_out(other[rows]), 2).reshape(3, width)
    shard = lax.axis_index("xy") * CORES + core
    q_final = lax.dynamic_slice_in_dim(sums[0], shard * rows, rows, 0).astype(f32)
    v_final = lax.dynamic_slice_in_dim(sums[2], shard * rows, rows, 0).astype(f32)
    output = [after(o, qkv_sum.keep) for o in output]
    output = jnp.where(odd == 0, jnp.stack(output), jnp.stack(output[::-1]))[None]
    return (
        output, input_grad, qkv_final, q_final, v_final, out_final, out_bias_final, g1, b1, in_final,
        in_bias_final, down_final, down_bias_final, g2, b2,
    )


def solution(mesh):
    fsdp, nseq = mesh.shape["fsdp"], mesh.shape["seq"]
    fine = Mesh(mesh.devices.reshape(fsdp // CORES, CORES, nseq), ("xy", "core", "seq"))
    shard = ("xy", "core")
    stream, matrix, vector = P(shard, None, "seq", None), P(shard, None), P(shard)
    return jax.shard_map(
        per_device,
        mesh=fine,
        in_specs=(
            stream, P(shard, None, None), matrix, vector, vector, matrix, vector, vector, vector,
            matrix, vector, matrix, vector, vector, vector, stream,
        ),
        out_specs=(
            stream, stream, matrix, vector, vector, matrix, vector, vector, vector,
            matrix, vector, matrix, vector, vector, vector,
        ),
        check_vma=False,
    )
```
